32 devices in a mesh: dp: 8 (over z, y), mp: 4 (over x, core).
Axes of the slice: x: 2, y: 2, z: 4, core: 2. Of those that a mesh axis runs over, the one named last changes fastest.
Arguments:
- tokens: bfloat16 [16384, 768], P('dp'), may hold values from -6 to 6
- qkv_weight: bfloat16 [768, 3, 768], P(None, None, 'mp'), may hold values from -0.21875 to 0.21875
- qkv_bias: float32 [3, 768], P(None, 'mp'), may hold values from -3 to 3
- output_weight: bfloat16 [768, 768], P('mp'), may hold values from -4 to 4
- output_bias: float32 [768], replicated, may hold values from -2 to 2
- first_gain: float32 [768], replicated, may hold values from 0.5 to 1.5
- first_shift: float32 [768], replicated, may hold values from -2 to 2
- inner_weight: bfloat16 [768, 3072], P(None, 'mp'), may hold values from -0.21875 to 0.21875
- inner_bias: float32 [3072], P('mp'), may hold values from -3 to 3
- outer_weight: bfloat16 [3072, 768], P('mp'), may hold values from -0.109375 to 0.109375
- outer_bias: float32 [768], replicated, may hold values from -2 to 2
- second_gain: float32 [768], replicated, may hold values from 0.5 to 1.5
- second_shift: float32 [768], replicated, may hold values from -2 to 2
- cotangent: bfloat16 [16384, 768], P(('dp', 'mp')), may hold values from -6 to 6
- seq_lengths: int32 [16], P('dp'), may hold values from 512 to 1024, as said below
Outputs:
- layer_out: bfloat16 [16384, 768], P(('dp', 'mp'))
- tokens_grad: float32 [16384, 768], P(('dp', 'mp'))
- qkv_weight_grad: float32 [768, 3, 768], P(None, None, 'mp')
- qkv_bias_grad: float32 [3, 768], P(None, 'mp')
- output_weight_grad: float32 [768, 768], P('mp')
- output_bias_grad: float32 [768], replicated
- first_gain_grad: float32 [768], replicated
- first_shift_grad: float32 [768], replicated
- inner_weight_grad: float32 [768, 3072], P(None, 'mp')
- inner_bias_grad: float32 [3072], P('mp')
- outer_weight_grad: float32 [3072, 768], P('mp')
- outer_bias_grad: float32 [768], replicated
- second_gain_grad: float32 [768], replicated
- second_shift_grad: float32 [768], replicated
The draws below stay inside these ranges and needn't reach their ends.
Inputs may be any that keep to these rules, and one draw needn't show every extreme that they name: `seq_lengths`: one sequence slot has exactly 1024 live tokens.
All inputs are finite; a program needn't handle non-finite values.
Results may differ from the reference program's by a relative error of at most 0.017.
Values may be sent and summed in bfloat16 or wider, within the bound.
No kernel may reach another device: no remote copies, remote signals or barrier semaphores. Data moves between devices by JAX's collectives and lax.ppermute only.
A program may use at most 192 MiB of HBM per device.

```python
import jax
import jax.numpy as jnp
from jax import lax

D = 768
H = 12
HD = 64
FF = 3072
LENGTH = 1024
SEQUENCES = 16
TOKENS = 16384


def draw_seq_lengths(key, part):
    first_key, second_key = jax.random.split(jax.random.fold_in(key, 17))
    drawn = jax.random.randint(first_key, (SEQUENCES,), LENGTH // 2, LENGTH + 1)
    chosen = jax.random.randint(second_key, (), 0, SEQUENCES)
    return jnp.where(jnp.arange(SEQUENCES) == chosen, LENGTH, drawn).astype(jnp.int32)


def level_of(key, dims, cuts, smallest, largest):
    def one(axis_at, blocks):
        draws = jax.random.uniform(jax.random.fold_in(jax.random.fold_in(key, 6), axis_at), (blocks,), jnp.float32, smallest / len(cuts), largest / len(cuts))
        return jnp.repeat(jnp.exp(draws), dims[axis_at] // blocks).reshape((-1,) + (1,) * (len(dims) - axis_at - 1))

    level = one(*cuts[0])
    for cut in cuts[1:]:
        level = level * one(*cut)
    return level


def gaussian(own_key, dims, scale, most, shards=(), held_as=jnp.bfloat16):
    entries = jax.random.normal(own_key, dims, jnp.float32) * scale
    if len(shards) > 0:
        entries = level_of(own_key, dims, shards, -0.22, 0.18) * entries
    return jnp.clip(entries, min=-most, max=most).astype(held_as)


def setup_inputs(seed: int = 0) -> dict:
    key_list = jax.random.split(jax.random.key(seed), 16)
    return {
        "tokens": gaussian(key_list[0], (TOKENS, D), 1.0, 6.0, ((0, 8),)),
        "qkv_weight": gaussian(key_list[1], (D, 3, D), D ** -0.5, 0.21875, ((2, 4),)),
        "qkv_bias": gaussian(key_list[2], (3, D), 0.5, 3.0, ((1, 4),), jnp.float32),
        "output_weight": gaussian(key_list[3], (D, D), 2 ** -0.5, 4.0, ((0, 4),)),
        "output_bias": gaussian(key_list[4], (D,), 0.3, 2.0, (), jnp.float32),
        "first_gain": jnp.clip(1.0 + 0.1 * jax.random.normal(key_list[5], (D,), jnp.float32), 0.5, 1.5),
        "first_shift": gaussian(key_list[6], (D,), 0.3, 2.0, (), jnp.float32),
        "inner_weight": gaussian(key_list[7], (D, FF), D ** -0.5, 0.21875, ((1, 4),)),
        "inner_bias": gaussian(key_list[8], (FF,), 0.5, 3.0, ((0, 4),), jnp.float32),
        "outer_weight": gaussian(key_list[9], (FF, D), FF ** -0.5, 0.109375, ((0, 4),)),
        "outer_bias": gaussian(key_list[10], (D,), 0.3, 2.0, (), jnp.float32),
        "second_gain": jnp.clip(1.0 + 0.1 * jax.random.normal(key_list[11], (D,), jnp.float32), 0.5, 1.5),
        "second_shift": gaussian(key_list[12], (D,), 0.3, 2.0, (), jnp.float32),
        "cotangent": gaussian(key_list[13], (TOKENS, D), 1.0, 6.0, ((0, 32),)),
        "seq_lengths": draw_seq_lengths(jax.random.fold_in(key_list[15], 71), 0),
    }


EPSILON = 1e-12
NEGATIVE = -1e+30
HIGHEST = lax.Precision.HIGHEST

@jax.custom_vjp
def low(v):
    return lax.optimization_barrier(v.astype(jnp.bfloat16)).astype(jnp.float32)

@jax.custom_vjp
def low_back(v):
    return v

def low_keep(v):
    return (low(v), None)

def low_pass(kept, grad):
    return (grad,)

def back_keep(v):
    return (v, None)

def back_low(kept, grad):
    return (low(grad),)
low.defvjp(low_keep, low_pass)
low_back.defvjp(back_keep, back_low)

def rotary_tables(row_total):
    half_depth = HD // 2
    frequency = 10000.0 ** (-jnp.arange(half_depth, dtype=jnp.float32) / half_depth)
    places = (jnp.arange(row_total, dtype=jnp.int32) % LENGTH).astype(jnp.float32)
    angle_table = places[:, None] * frequency[None, :]
    return (jnp.cos(angle_table)[:, None, :], jnp.sin(angle_table)[:, None, :])

def rotate(values, cosine, sine):
    half_depth = values.shape[-1] // 2
    front, behind = (values[..., :half_depth], values[..., half_depth:])
    return jnp.concatenate([front * cosine - behind * sine, behind * cosine + front * sine], axis=-1)

def normalize(values, gain, shift):
    mean_value = lax.optimization_barrier(jnp.mean(values, axis=-1, keepdims=True))
    centered = values - mean_value
    variance = lax.optimization_barrier(jnp.mean(centered * centered, axis=-1, keepdims=True))
    return centered * lax.rsqrt(variance + EPSILON) * gain + shift

def attend(operands):
    queries, keys, values_seq, live_length = operands
    raw_scores = jnp.einsum('qhd,khd->hqk', queries, keys, precision=HIGHEST)
    scores = low_back(raw_scores) * HD ** (-0.5)
    live = jnp.arange(LENGTH, dtype=jnp.int32) < live_length
    scores = jnp.where(live[None, None, :], scores, NEGATIVE)
    top_score = lax.optimization_barrier(jnp.max(scores, axis=-1, keepdims=True))
    expo = jnp.exp(scores - top_score)
    weights = low(expo / lax.optimization_barrier(jnp.sum(expo, axis=-1, keepdims=True)))
    return jnp.einsum('hqk,khd->qhd', weights, values_seq, precision=HIGHEST)

def reference(tokens, qkv_weight, qkv_bias, output_weight, output_bias, first_gain, first_shift, inner_weight, inner_bias, outer_weight, outer_bias, second_gain, second_shift, cotangent, seq_lengths):
    row_total = tokens.shape[0]
    seq_total = row_total // LENGTH
    cosine, sine = rotary_tables(row_total)

    def forward(inputs, w_qkv_f, b_qkv_f, w_out_f, b_out_f, g_one, s_one, w_inner_f, b_inner_f, w_outer_f, b_outer_f, g_two, s_two):
        qkv_lin = low_back(jnp.einsum('nd,dce->nce', inputs, w_qkv_f, precision=HIGHEST) + b_qkv_f)
        queries = low(rotate(qkv_lin[:, 0].reshape(row_total, H, HD), cosine, sine))
        keys = low(rotate(qkv_lin[:, 1].reshape(row_total, H, HD), cosine, sine))
        values_all = low(qkv_lin[:, 2].reshape(row_total, H, HD))
        mixed = lax.map(jax.checkpoint(attend), (queries.reshape(seq_total, LENGTH, H, HD), keys.reshape(seq_total, LENGTH, H, HD), values_all.reshape(seq_total, LENGTH, H, HD), seq_lengths))
        mixed = low_back(low(mixed.reshape(row_total, D)))
        attended = low_back(jnp.dot(mixed, w_out_f, precision=HIGHEST)) + b_out_f
        first_normed = normalize(inputs + attended, g_one, s_one)
        inner_lin = low_back(jnp.dot(low(first_normed), w_inner_f, precision=HIGHEST) + b_inner_f)
        activated = low(jax.nn.gelu(inner_lin, approximate=False))
        outer_sum = low_back(jnp.dot(activated, w_outer_f, precision=HIGHEST)) + b_outer_f
        return normalize(first_normed + outer_sum, g_two, s_two)
    f32 = jnp.float32
    layer_value, pullback = jax.vjp(forward, tokens.astype(f32), qkv_weight.astype(f32), qkv_bias.astype(f32), output_weight.astype(f32), output_bias.astype(f32), first_gain.astype(f32), first_shift.astype(f32), inner_weight.astype(f32), inner_bias.astype(f32), outer_weight.astype(f32), outer_bias.astype(f32), second_gain.astype(f32), second_shift.astype(f32))
    places = jnp.arange(row_total, dtype=jnp.int32)
    live_rows = places % LENGTH < jnp.repeat(seq_lengths, LENGTH, total_repeat_length=row_total)
    grads = pullback(cotangent.astype(f32) * live_rows[:, None].astype(f32))
    return (layer_value.astype(jnp.bfloat16), grads[0], grads[1], grads[2], grads[3], grads[4], grads[5], grads[6], grads[7], grads[8], grads[9], grads[10], grads[11], grads[12])
```

```python
import functools
import math

import jax
import jax.numpy as jnp
import numpy as np
from jax import lax
from jax.experimental import pallas as pl
from jax.experimental.pallas import tpu as pltpu
from jax.sharding import PartitionSpec as P

HD = 64
HALF_DEPTH = HD // 2
LENGTH = 1024
EPSILON = 1e-12
NEGATIVE = -1e30
F32 = jnp.float32
BF16 = jnp.bfloat16
EXP_SCALE = HD ** (-0.5) * math.log2(math.e)

ERF_P = 0.52
ERF_C = (0.00514851, 0.23724269, 0.55266472, -0.39660497, 1.10267122, -0.61325166, 0.1121295)

NN = (((1,), (0,)), ((), ()))
NT = (((1,), (1,)), ((), ()))
TN = (((0,), (0,)), ((), ()))


def mm(a, b, dims):
    return lax.dot_general(a, b, dims, preferred_element_type=F32)


def rotary_tables():
    frequency = 10000.0 ** (-np.arange(HALF_DEPTH, dtype=np.float64) / HALF_DEPTH)
    angle = frequency[:, None] * np.arange(LENGTH, dtype=np.float64)[None, :]
    return np.cos(angle).astype(np.float32), np.sin(angle).astype(np.float32)


def call(body, outs, ins, grid=(), in_specs=None, out_specs=None, scratch=(), flops=0, name=None, vmem=None, trans=0):
    nbytes = sum(math.prod(a.shape) * a.dtype.itemsize for a in list(ins) + list(outs))
    whole = pl.BlockSpec(memory_space=pltpu.VMEM)
    return pl.pallas_call(
        body,
        out_shape=outs,
        grid=grid,
        in_specs=in_specs if in_specs is not None else [whole] * len(ins),
        out_specs=out_specs if out_specs is not None else [whole] * len(outs),
        scratch_shapes=scratch,
        compiler_params=pltpu.CompilerParams(vmem_limit_bytes=vmem or 40 << 20),
        cost_estimate=pl.CostEstimate(flops=flops, bytes_accessed=nbytes, transcendentals=trans),
        name=name,
    )(*ins)


def sds(shape, dtype):
    return jax.ShapeDtypeStruct(shape, dtype)


SMEM = pl.BlockSpec(memory_space=pltpu.SMEM)
VM = pl.BlockSpec(memory_space=pltpu.VMEM)


def rotate(v, cosine, sine):
    a, b = v[:HALF_DEPTH], v[HALF_DEPTH:]
    return jnp.concatenate([a * cosine - b * sine, b * cosine + a * sine], axis=0)


def unrotate(v, cosine, sine):
    a, b = v[:HALF_DEPTH], v[HALF_DEPTH:]
    return jnp.concatenate([a * cosine + b * sine, b * cosine - a * sine], axis=0)


def row_select(rows, columns):
    index = lax.broadcasted_iota(jnp.int32, (8, columns), 0)
    out = jnp.zeros((8, columns), F32)
    for i, r in enumerate(rows):
        if r is not None:
            out = jnp.where(index == i, r, out)
    return out


def augment(top, rows, total=2 * HD):
    columns = top.shape[1]
    tail = row_select(rows, columns)
    rest = jnp.zeros((total - HD - 8, columns), F32)
    return jnp.concatenate([top, tail, rest], axis=0)


def split3(v):
    high = v.astype(BF16).astype(F32)
    mid = (v - high).astype(BF16).astype(F32)
    return high, mid, v - high - mid


def mask_row(length):
    index = lax.broadcasted_iota(jnp.int32, (1, LENGTH), 1)
    return jnp.where(index < length, 0.0, NEGATIVE)


def attention_forward(heads, own, sc, x_ref, w_ref, b_ref, cos_ref, sin_ref, kv_ref, q_ref, o_ref, ob_ref, l_ref, kn_ref):
    half, length = sc[1], sc[2]
    width = heads * HD
    start = pl.multiple_of(half * own, own)
    kv = mm(w_ref[width:], x_ref[...], NT) + b_ref[width:]
    q = mm(w_ref[:width], x_ref[pl.ds(start, own), :], NT) + b_ref[:width]
    cosine, sine = cos_ref[...], sin_ref[...]
    own_cos, own_sin = cos_ref[:, pl.ds(start, own)], sin_ref[:, pl.ds(start, own)]
    mask = mask_row(length)
    one = jnp.ones((1, LENGTH), F32)
    kv_ref[width:] = kv[width:].astype(BF16)
    logs = []
    for h in range(heads):
        lo, hi = h * HD, (h + 1) * HD
        k_rot = rotate(kv[lo:hi], cosine, sine)
        kv_ref[lo:hi] = k_rot.astype(BF16)
        kn_ref[h] = jnp.transpose(augment(k_rot, (one, one, one, mask))).astype(BF16)
        q_rot = rotate(q[lo:hi], own_cos, own_sin)
        q_ref[lo:hi] = q_rot.astype(BF16)
        keys = kn_ref[h]
        v_aug = jnp.concatenate(
            [kv_ref[width + lo : width + hi], jnp.ones((16, LENGTH), BF16)], axis=0
        )
        row = []
        for c in range(0, own, 256):
            q_aug = augment(q_rot[:, c : c + 256], (None, None, None, jnp.ones((1, 256), F32)))
            s = mm(keys, q_aug.astype(BF16), NN)
            top = jnp.max(s, axis=0, keepdims=True)
            p = jnp.exp2((s - top) * EXP_SCALE).astype(BF16)
            o = mm(v_aug, p, NN)
            mass = o[HD : HD + 1]
            o = o[:HD] / mass
            o_ref[lo:hi, c : c + 256] = o
            ob_ref[lo:hi, c : c + 256] = o.astype(BF16)
            row.append(top + jnp.log2(mass) / EXP_SCALE)
        logs.append(jnp.concatenate(row, axis=1))
    l_ref[...] = row_select(logs, own)


def attention_backward(heads, own, sc, x_ref, kv_ref, q_ref, o_ref, do_ref, l_ref, kn_ref, cos_ref, sin_ref, dkv_ref, dq_ref, gw_ref, gb_ref):
    half, length = sc[1], sc[2]
    width = heads * HD
    start = pl.multiple_of(half * own, own)
    cosine, sine = cos_ref[...], sin_ref[...]
    own_cos, own_sin = cos_ref[:, pl.ds(start, own)], sin_ref[:, pl.ds(start, own)]
    mask = mask_row(length)
    one = jnp.ones((1, LENGTH), F32)
    own_one = jnp.ones((1, own), F32)
    tail_k = jnp.concatenate([row_select((one, one, one, mask), LENGTH), jnp.zeros((HD - 8, LENGTH), F32)], axis=0).astype(BF16)
    tail_v = jnp.concatenate([row_select((one, one, one), LENGTH), jnp.zeros((HD - 8, LENGTH), F32)], axis=0).astype(BF16)
    for h in range(heads):
        lo, hi = h * HD, (h + 1) * HD
        d_out = do_ref[lo:hi].astype(F32)
        delta = jnp.sum(d_out * o_ref[lo:hi], axis=0, keepdims=True)
        qn = jnp.transpose(augment(q_ref[lo:hi].astype(F32), (*split3(-l_ref[h : h + 1]), own_one))).astype(BF16)
        dn = jnp.transpose(augment(d_out, split3(-delta))).astype(BF16)
        k_aug = jnp.concatenate([kv_ref[lo:hi], tail_k], axis=0)
        v_aug = jnp.concatenate([kv_ref[width + lo : width + hi], tail_v], axis=0)
        keys = kn_ref[h]
        dk = dv = None
        dq = []
        for c in range(0, own, 256):
            p = jnp.exp2(mm(qn[c : c + 256], k_aug, NN) * EXP_SCALE)
            dp = mm(dn[c : c + 256], v_aug, NN)
            ds = (p * dp).astype(BF16)
            dq.append(mm(ds, keys, NN))
            dk_part = mm(q_ref[lo:hi, c : c + 256], ds, NN)
            dv_part = mm(do_ref[lo:hi, c : c + 256], p.astype(BF16), NN)
            dk = dk_part if dk is None else dk + dk_part
            dv = dv_part if dv is None else dv + dv_part
        dq_t = jnp.transpose(jnp.concatenate(dq, axis=0))[:HD]
        scale = HD ** (-0.5)
        dq_ref[lo:hi] = (unrotate(dq_t, own_cos, own_sin) * scale).astype(BF16)
        dkv_ref[lo:hi] = (unrotate(dk, cosine, sine) * scale).astype(BF16)
        dkv_ref[width + lo : width + hi] = dv.astype(BF16)
    gw_ref[:width] = mm(dq_ref[...], x_ref[pl.ds(start, own), :], NN).astype(gw_ref.dtype)
    gw_ref[width:] = mm(dkv_ref[...], x_ref[...], NN).astype(gw_ref.dtype)
    gb_ref[:width] = jnp.sum(dq_ref[...].astype(F32), axis=1, keepdims=True)
    gb_ref[width:] = jnp.sum(dkv_ref[...].astype(F32), axis=1, keepdims=True)


def norm_stats(v):
    centered = v - jnp.mean(v, axis=-1, keepdims=True)
    inverse = lax.rsqrt(jnp.mean(centered * centered, axis=-1, keepdims=True) + EPSILON)
    return centered * inverse, inverse


def norm_back(grad, hat, inverse, gain):
    scaled = grad * gain
    return inverse * (
        scaled
        - jnp.mean(scaled, axis=-1, keepdims=True)
        - hat * jnp.mean(scaled * hat, axis=-1, keepdims=True)
    )


def project_norm(*refs):
    sc, x_ref = refs[0], refs[1]
    o_refs, w_refs = refs[2:6], refs[6:10]
    bias_ref, gain_ref, shift_ref, n_ref, nt_ref, hat_ref, inv_ref = refs[10:]
    rows = hat_ref.shape[0]
    start = pl.multiple_of(sc[0] * rows, rows)
    total = x_ref[pl.ds(start, rows), :].astype(F32) + bias_ref[...]
    for o_ref, w_ref in zip(o_refs, w_refs):
        total = total + mm(o_ref[...], w_ref[...], TN)
    hat, inverse = norm_stats(total)
    n = hat * gain_ref[...] + shift_ref[...]
    hat_ref[...] = hat
    inv_ref[...] = inverse
    n_ref[...] = n.astype(BF16)
    nt_ref[...] = jnp.transpose(n).astype(BF16)


def gelu_parts(z):
    e = jnp.exp2(z * z * (-0.5 * math.log2(math.e)))
    t = 1.0 / (1.0 + jnp.abs(z) * (ERF_P / math.sqrt(2.0)))
    poly = jnp.full_like(z, 0.5 * ERF_C[-1])
    for c in ERF_C[-2::-1]:
        poly = poly * t + 0.5 * c
    tail = poly * e
    phi = jnp.where(z >= 0, 1.0 - tail, tail)
    return z * phi, phi + z * e * (1.0 / math.sqrt(2.0 * math.pi))


def ffn_forward(n_ref, wi_ref, bi_ref, wo_ref, f_in_ref, g_ref, d_ref, f_ref):
    z = mm(n_ref[...], wi_ref[...], NN) + bi_ref[...]
    g, d = gelu_parts(z)
    g = g.astype(BF16)
    g_ref[...] = g
    d_ref[...] = d
    part = mm(g, wo_ref[...], NN)

    @pl.when(pl.program_id(0) == 0)
    def _():
        f_ref[...] = part if f_in_ref is None else f_in_ref[...] + part

    @pl.when(pl.program_id(0) > 0)
    def _():
        f_ref[...] += part


def ffn_forward_first(n_ref, wi_ref, bi_ref, wo_ref, g_ref, d_ref, f_ref):
    ffn_forward(n_ref, wi_ref, bi_ref, wo_ref, None, g_ref, d_ref, f_ref)


def second_norm(sc, f_ref, hat_ref, cot_ref, g1_ref, s1_ref, ob_ref, g2_ref, s2_ref, out_ref, dr_ref, df_ref, small_ref):
    rows = f_ref.shape[0]
    first = hat_ref[...] * g1_ref[...] + s1_ref[...]
    hat, inverse = norm_stats(first + f_ref[...] + ob_ref[...])
    out_ref[...] = (hat * g2_ref[...] + s2_ref[...]).astype(BF16)
    place = lax.broadcasted_iota(jnp.int32, (rows, 1), 0) + sc[1] * rows
    grad = jnp.where(place < sc[2], cot_ref[...].astype(F32), 0.0)
    dr = norm_back(grad, hat, inverse, g2_ref[...])
    dr_ref[...] = dr
    df_ref[...] = dr.astype(BF16)
    sums = [jnp.sum(v, axis=0, keepdims=True) for v in (grad * hat, grad, dr)]
    small_ref[...] = row_select(sums, f_ref.shape[1])


def outer_grad(g_ref, df_ref, out_ref):
    out_ref[...] = mm(g_ref[...], df_ref[...], TN).astype(out_ref.dtype)


def ffn_backward(df_ref, wo_ref, d_ref, wi_ref, nt_ref, dn_in_ref, gi_ref, gb_ref, dn_ref):
    dz = (mm(df_ref[...], wo_ref[...], NT) * d_ref[...]).astype(BF16)
    gb_ref[...] = jnp.sum(dz.astype(F32), axis=0, keepdims=True)
    gi_ref[...] = mm(nt_ref[...], dz, NN).astype(gi_ref.dtype)
    part = mm(dz, wi_ref[...], NT)

    @pl.when(pl.program_id(0) == 0)
    def _():
        dn_ref[...] = dn_in_ref[...] + part

    @pl.when(pl.program_id(0) > 0)
    def _():
        dn_ref[...] += part


def first_norm_back(*refs):
    dn_ref, hat_ref, inv_ref, gain_ref = refs[:4]
    o_refs, w_refs = refs[4:8], refs[8:12]
    dr_ref, small_ref = refs[12:14]
    do_refs, go_refs = refs[14:18], refs[18:22]
    grad, hat = dn_ref[...], hat_ref[...]
    dr = norm_back(grad, hat, inv_ref[...], gain_ref[...])
    dr_ref[...] = dr
    low = dr.astype(BF16)
    sums = [jnp.sum(v, axis=0, keepdims=True) for v in (dr, grad * hat, grad)]
    small_ref[...] = row_select(sums, grad.shape[1])
    for o_ref, w_ref, do_ref, go_ref in zip(o_refs, w_refs, do_refs, go_refs):
        do_ref[...] = mm(w_ref[...], low, NT).astype(BF16)
        go_ref[...] = mm(o_ref[...], low, NN).astype(go_ref.dtype)


def token_grad_other(*refs):
    sc, refs = refs[0], refs[1:]
    dkv, w, out_ref = refs[:4], refs[4:8], refs[8]
    rows = out_ref.shape[0]
    start = pl.multiple_of((1 - sc[1]) * rows, rows)
    total = None
    for d_ref, w_ref in zip(dkv, w):
        part = mm(d_ref[:, pl.ds(start, rows)], w_ref[w_ref.shape[0] // 3 :], TN)
        total = part if total is None else total + part
    out_ref[...] = total.astype(BF16)


def token_grad_own(*refs):
    sc, refs = refs[0], refs[1:]
    dkv, dq, w, dr_ref, out_ref = refs[:4], refs[4:8], refs[8:12], refs[12], refs[13]
    rows = out_ref.shape[0]
    start = pl.multiple_of(sc[1] * rows, rows)
    total = dr_ref[...]
    for d_ref, q_ref, w_ref in zip(dkv, dq, w):
        width = q_ref.shape[0]
        total = total + mm(d_ref[:, pl.ds(start, rows)], w_ref[width:], TN)
        total = total + mm(q_ref[...], w_ref[:width], TN)
    out_ref[...] = total


def swap(v, axis, bit):
    size = lax.axis_size(axis)
    return lax.ppermute(v, axis, [(i, i ^ bit) for i in range(size)])


def collect(v):
    one = swap(v, "mp", 1)
    two = swap(v, "mp", 2)
    return [v, one, two, swap(two, "mp", 1)]


def reduce_grads(parts):
    one, three = swap(parts[1], "mp", 1), swap(parts[3], "mp", 1)
    mine = parts[0].astype(F32) + one.astype(F32)
    other = (parts[2].astype(F32) + three.astype(F32)).astype(BF16)
    total = mine + swap(other, "mp", 2).astype(F32)
    size, index = lax.axis_size("dp"), lax.axis_index("dp")
    stages = []
    bit = 1
    while bit < size:
        stages.append((bit, (index & bit) > 0))
        bit *= 2
    for bit, upper in stages:
        n = total.shape[0] // 2
        low, high = total[:n], total[n:]
        send = jnp.where(upper, low, high).astype(BF16)
        total = jnp.where(upper, high, low) + swap(send, "dp", bit).astype(F32)
    total = total.astype(BF16)
    for bit, upper in stages[::-1]:
        other = swap(total, "dp", bit)
        total = jnp.where(upper, jnp.concatenate([other, total]), jnp.concatenate([total, other]))
    return total.astype(F32)


def sum_everywhere(v):
    for axis in ("mp", "dp"):
        bit = 1
        while bit < lax.axis_size(axis):
            v = v + swap(v, axis, bit)
            bit *= 2
    return v


def on_device(
    tokens,
    qkv_weight,
    qkv_bias,
    output_weight,
    output_bias,
    first_gain,
    first_shift,
    inner_weight,
    inner_bias,
    outer_weight,
    outer_bias,
    second_gain,
    second_shift,
    cotangent,
    seq_lengths,
):
    depth = tokens.shape[1]
    own = cotangent.shape[0]
    width = qkv_weight.shape[2]
    heads = width // HD
    hidden = inner_weight.shape[1]
    me = lax.axis_index("mp")
    seq = me * own // LENGTH
    half = (me * own % LENGTH) // own
    length = jnp.sum(jnp.where(jnp.arange(seq_lengths.shape[0]) == seq, seq_lengths, 0))
    scalars = jnp.stack([me, half, length]).astype(jnp.int32)
    x_seq = lax.dynamic_slice_in_dim(tokens, seq * LENGTH, LENGTH, 0)
    cosine, sine = (jnp.asarray(t) for t in rotary_tables())

    w_own = jnp.transpose(qkv_weight, (1, 2, 0)).reshape(3 * width, depth)
    biases = jnp.concatenate([qkv_bias.reshape(-1), inner_bias])
    biases = jnp.pad(biases, (0, -biases.shape[0] % 1024)).reshape(-1, 128)
    bias_slots = [biases] + [swap(biases, "mp", r) for r in (1, 2, 3)]
    qkv_b = [b.reshape(-1)[: 3 * width].reshape(-1, 1) for b in bias_slots]
    inner_b = [b.reshape(-1)[3 * width : 3 * width + hidden].reshape(1, -1) for b in bias_slots]
    qkv_w = collect(w_own)
    output_w = collect(output_weight)
    inner_w = collect(inner_weight)
    outer_w = collect(outer_weight)
    rows = {n: v.reshape(1, -1) for n, v in dict(ob=output_bias, g1=first_gain, s1=first_shift, b2=outer_bias, g2=second_gain, s2=second_shift).items()}

    kv, q, o, ob, logs, keys = ([None] * 4 for _ in range(6))
    for r in range(4):
        kv[r], q[r], o[r], ob[r], logs[r], keys[r] = call(
            functools.partial(attention_forward, heads, own),
            [
                sds((2 * width, LENGTH), BF16),
                sds((width, own), BF16),
                sds((width, own), F32),
                sds((width, own), BF16),
                sds((8, own), F32),
                sds((heads, LENGTH, 2 * HD), BF16),
            ],
            [scalars, x_seq, qkv_w[r], qkv_b[r], cosine, sine],
            in_specs=[SMEM] + [VM] * 5,
            flops=2 * depth * width * (2 * LENGTH + own) + 4 * own * LENGTH * 256 * heads,
            name="attention_forward",
        )
    n_low, n_t, hat, inverse = call(
        project_norm,
        [sds((own, depth), BF16), sds((depth, own), BF16), sds((own, depth), F32), sds((own, 1), F32)],
        [scalars, tokens, *ob, *output_w, rows["ob"], rows["g1"], rows["s1"]],
        in_specs=[SMEM] + [VM] * 12,
        flops=2 * own * depth * depth,
        name="project_norm",
    )

    block = 256
    steps = hidden // block
    full = lambda shape: pl.BlockSpec(shape, lambda i: (0,) * len(shape))
    by_row = lambda columns: pl.BlockSpec((block, columns), lambda i: (i, 0))
    by_column = lambda count: pl.BlockSpec((count, block), lambda i: (0, i))
    g, d = [None] * 4, [None] * 4
    f = None
    for r in range(4):
        ins = [n_low, inner_w[r], inner_b[r], outer_w[r]] + ([] if f is None else [f])
        specs = [full((own, depth)), by_column(depth), by_column(1), by_row(depth)] + ([] if f is None else [full((own, depth))])
        g[r], d[r], f = call(
            ffn_forward_first if f is None else ffn_forward,
            [sds((own, hidden), BF16), sds((own, hidden), F32), sds((own, depth), F32)],
            ins,
            grid=(steps,),
            in_specs=specs,
            out_specs=[by_column(own), by_column(own), full((own, depth))],
            flops=4 * own * depth * hidden,
            name="ffn_forward",
        )
    layer_out, dr2, df, small2 = call(
        second_norm,
        [sds((own, depth), BF16), sds((own, depth), F32), sds((own, depth), BF16), sds((8, depth), F32)],
        [scalars, f, hat, cotangent, rows["g1"], rows["s1"], rows["b2"], rows["g2"], rows["s2"]],
        in_specs=[SMEM] + [VM] * 8,
        flops=40 * own * depth,
        name="second_norm",
    )
    keep = {0: F32, 1: BF16, 2: F32, 3: BF16}
    order = (1, 3, 2, 0)
    outer_g = [None] * 4
    for r in order:
        (outer_g[r],) = call(
            outer_grad,
            [sds((hidden, depth), keep[r])],
            [g[r], df],
            grid=(steps,),
            in_specs=[by_column(own), full((own, depth))],
            out_specs=[by_row(depth)],
            flops=2 * own * depth * hidden,
            name="outer_grad",
        )
    outer_weight_grad = reduce_grads(outer_g)
    inner_g, inner_bg = [None] * 4, [None] * 4
    dn = dr2
    for r in order:
        inner_g[r], inner_bg[r], dn = call(
            ffn_backward,
            [sds((depth, hidden), keep[r]), sds((1, hidden), F32), sds((own, depth), F32)],
            [df, outer_w[r], d[r], inner_w[r], n_t, dn],
            grid=(steps,),
            in_specs=[full((own, depth)), by_row(depth), by_column(own), by_column(depth), full((depth, own)), full((own, depth))],
            out_specs=[by_column(depth), by_column(1), full((own, depth))],
            flops=6 * own * depth * hidden,
            name="ffn_backward",
        )
    inner_weight_grad = reduce_grads(inner_g)
    dr1, small1, *rest = call(
        first_norm_back,
        [sds((own, depth), F32), sds((8, depth), F32)] + [sds((width, own), BF16)] * 4 + [sds((width, depth), keep[r]) for r in range(4)],
        [dn, hat, inverse, rows["g1"], *ob, *output_w],
        flops=4 * own * depth * depth,
        name="first_norm_back",
    )
    d_out, output_g = rest[:4], rest[4:]
    output_weight_grad = reduce_grads(output_g)

    dkv, dq, qkv_g, qkv_bg = ([None] * 4 for _ in range(4))
    for r in order:
        dkv[r], dq[r], qkv_g[r], qkv_bg[r] = call(
            functools.partial(attention_backward, heads, own),
            [
                sds((2 * width, LENGTH), BF16),
                sds((width, own), BF16),
                sds((3 * width, depth), keep[r]),
                sds((3 * width, 1), F32),
            ],
            [scalars, x_seq, kv[r], q[r], o[r], d_out[r], logs[r], keys[r], cosine, sine],
            in_specs=[SMEM] + [VM] * 9,
            flops=2 * depth * width * (2 * LENGTH + own) + 10 * own * LENGTH * 256 * heads,
            name="attention_backward",
        )
    qkv_weight_grad = reduce_grads(qkv_g)
    qkv_weight_grad = jnp.transpose(qkv_weight_grad.reshape(3, width, depth), (2, 0, 1))
    (other_tokens,) = call(
        token_grad_other,
        [sds((own, depth), BF16)],
        [scalars, *dkv, *qkv_w],
        in_specs=[SMEM] + [VM] * 8,
        flops=4 * own * depth * depth,
        name="token_grad_other",
    )
    (own_tokens,) = call(
        token_grad_own,
        [sds((own, depth), F32)],
        [scalars, *dkv, *dq, *qkv_w, dr1],
        in_specs=[SMEM] + [VM] * 13,
        flops=6 * own * depth * depth,
        name="token_grad_own",
    )
    tokens_grad = own_tokens + swap(other_tokens, "mp", 1).astype(F32)

    slots = jnp.stack([jnp.concatenate([b.reshape(-1), c.reshape(-1)]) for b, c in zip(inner_bg, qkv_bg)])
    place = jnp.arange(4)[:, None] == (jnp.arange(4) ^ me)[None, :]
    placed = jnp.sum(jnp.where(place[:, :, None], slots[None], 0.0), axis=1)
    small = jnp.concatenate([small2[:3].reshape(-1), small1[:3].reshape(-1), placed.reshape(-1)])
    count = small.shape[0]
    small = jnp.pad(small, (0, -count % 1024)).reshape(-1, 128)
    small = sum_everywhere(small).reshape(-1)[:count]
    vectors = small[: 6 * depth].reshape(6, depth)
    second_gain_grad, second_shift_grad, outer_bias_grad, output_bias_grad, first_gain_grad, first_shift_grad = vectors
    mine = lax.dynamic_index_in_dim(small[6 * depth :].reshape(4, -1), me, 0, keepdims=False)
    inner_bias_grad, qkv_bias_grad = mine[:hidden], mine[hidden:].reshape(3, width)
    return (
        layer_out,
        tokens_grad,
        qkv_weight_grad,
        qkv_bias_grad,
        output_weight_grad,
        output_bias_grad,
        first_gain_grad,
        first_shift_grad,
        inner_weight_grad,
        inner_bias_grad,
        outer_weight_grad,
        outer_bias_grad,
        second_gain_grad,
        second_shift_grad,
    )


def solution(mesh):
    return jax.shard_map(
        on_device,
        mesh=mesh,
        in_specs=(
            P("dp", None),
            P(None, None, "mp"),
            P(None, "mp"),
            P("mp", None),
            P(),
            P(),
            P(),
            P(None, "mp"),
            P("mp"),
            P("mp", None),
            P(),
            P(),
            P(),
            P(("dp", "mp"), None),
            P("dp"),
        ),
        out_specs=(
            P(("dp", "mp"), None),
            P(("dp", "mp"), None),
            P(None, None, "mp"),
            P(None, "mp"),
            P("mp", None),
            P(),
            P(),
            P(),
            P(None, "mp"),
            P("mp"),
            P("mp", None),
            P(),
            P(),
            P(),
        ),
        check_vma=False,
    )
```

```python
import functools
import math

import jax
import jax.numpy as jnp
import numpy as np
from jax import lax
from jax.experimental import pallas as pl
from jax.experimental.pallas import tpu as pltpu
from jax.sharding import PartitionSpec as P

HD = 64
HALF_DEPTH = HD // 2
LENGTH = 1024
EPSILON = 1e-12
NEGATIVE = -1e30
F32 = jnp.float32
BF16 = jnp.bfloat16
EXP_SCALE = HD ** (-0.5) * math.log2(math.e)

ERF_P = 0.52
ERF_C = (0.00514851, 0.23724269, 0.55266472, -0.39660497, 1.10267122, -0.61325166, 0.1121295)

NN = (((1,), (0,)), ((), ()))
NT = (((1,), (1,)), ((), ()))
TN = (((0,), (0,)), ((), ()))


def mm(a, b, dims):
    return lax.dot_general(a, b, dims, preferred_element_type=F32)


def rotary_tables():
    frequency = 10000.0 ** (-np.arange(HALF_DEPTH, dtype=np.float64) / HALF_DEPTH)
    angle = frequency[:, None] * np.arange(LENGTH, dtype=np.float64)[None, :]
    return np.cos(angle).astype(np.float32), np.sin(angle).astype(np.float32)


ROW_US = 0.0334
HOP_US = 2.0


class Program:
    def __init__(self, scalars):
        self.scalars = scalars
        self.tokens = []
        self.clock = 0.0
        self.links = {"x": 0.0, "y": 0.0, "z": 0.0, "m": 0.0}
        self.chunks = []

    def wait(self, *values):
        self.tokens += values

    def call(self, body, outs, ins, grid=(), in_specs=None, out_specs=None, flops=0, name=None, vmem=16, us=5.0):
        scalars = after(self.scalars, *self.tokens)
        nbytes = sum(math.prod(a.shape) * a.dtype.itemsize for a in list(ins) + list(outs))
        whole = pl.BlockSpec(memory_space=pltpu.VMEM)
        result = pl.pallas_call(
            body,
            out_shape=outs,
            grid=grid,
            in_specs=[pl.BlockSpec(memory_space=pltpu.SMEM)] + (in_specs if in_specs is not None else [whole] * len(ins)),
            out_specs=out_specs if out_specs is not None else [whole] * len(outs),
            compiler_params=pltpu.CompilerParams(vmem_limit_bytes=vmem << 20),
            cost_estimate=pl.CostEstimate(flops=flops // COST_SCALE, bytes_accessed=nbytes // COST_SCALE, transcendentals=0),
            name=name,
        )(scalars, *ins)
        self.tokens = [result[0]]
        self.clock += us
        self.service()
        return result

    def service(self, left=None):
        while True:
            waiting = [c for c in self.chunks if not c.finished]
            if not waiting or (left is not None and len(waiting) <= left):
                return
            chunk = min(waiting, key=lambda c: c.due)
            if chunk.due > self.clock and left is None:
                return
            if chunk.due == math.inf:
                return
            self.clock = max(self.clock, chunk.due)
            if chunk.received is not None:
                chunk.received = after(chunk.received, *self.tokens)
            elif chunk.stage == "start" and hasattr(chunk, "own") and self.tokens:
                chunk.own = after(chunk.own, *self.tokens)
            made = chunk.step()
            self.tokens = [made]
            rows = math.prod(made.shape[:-1])
            self.clock += 0.6 + rows / 768 + (2.7 if chunk.stage == 4 else 1.6)
            if not chunk.finished:
                chunk.due = self.transfer(chunk.stage, rows)
                if getattr(chunk, "zero", 0) is None:
                    chunk.arrives, chunk.due = chunk.due, math.inf

    def transfer(self, stage, rows):
        us = rows * ROW_US
        uses = {"x": {"x": us}, 1: {"y": us}, 2: {"z": us}, 4: {"m": 2 * us, "z": us}, "all": {"y": us / 2, "z": us, "m": us}, "share": {"y": us / 2, "z": us, "m": us}}.get(stage, {})
        start = max([self.clock - 1] + [self.links[n] for n in uses])
        for n, t in uses.items():
            self.links[n] = start + t
        return start + max(list(uses.values()) + [us / 6]) + HOP_US

    def finish(self, chunk):
        while not chunk.finished:
            self.service(len([c for c in self.chunks if not c.finished]) - 1)

    def add(self, chunk):
        chunk.due = self.clock
        self.chunks.append(chunk)
        self.service()

    def supply(self, chunk, zero):
        chunk.zero = zero
        if chunk not in self.chunks:
            self.add(chunk)
        else:
            chunk.due = max(self.clock, chunk.arrives)
            self.service()


COST_SCALE = 1 << 20
OUTER_ORDER = ("x", 1, 2, 4)
INNER_ORDER = (2, "x", 1, 4)
QKV_ORDER = ("x", "all")


def sds(shape, dtype):
    return jax.ShapeDtypeStruct(shape, dtype)


def rotate(v, cosine, sine):
    a, b = v[:HALF_DEPTH], v[HALF_DEPTH:]
    return jnp.concatenate([a * cosine - b * sine, b * cosine + a * sine], axis=0)


def unrotate(v, cosine, sine):
    a, b = v[:HALF_DEPTH], v[HALF_DEPTH:]
    return jnp.concatenate([a * cosine + b * sine, b * cosine - a * sine], axis=0)


def row_select(rows, columns):
    index = lax.broadcasted_iota(jnp.int32, (8, columns), 0)
    out = jnp.zeros((8, columns), F32)
    for i, r in enumerate(rows):
        if r is not None:
            out = jnp.where(index == i, r, out)
    return out


def augment(top, rows, total=2 * HD):
    columns = top.shape[1]
    tail = row_select(rows, columns)
    rest = jnp.zeros((total - HD - 8, columns), F32)
    return jnp.concatenate([top, tail, rest], axis=0)


def split3(v):
    high = v.astype(BF16).astype(F32)
    mid = (v - high).astype(BF16).astype(F32)
    return high, mid, v - high - mid


def mask_row(length):
    index = lax.broadcasted_iota(jnp.int32, (1, LENGTH), 1)
    return jnp.where(index < length, 0.0, NEGATIVE)


def attention_forward(heads, own, sc, x_ref, w_ref, b_ref, cos_ref, sin_ref, kv_ref, q_ref, o_ref, ob_ref, l_ref, kn_ref):
    half, length = sc[1], sc[2]
    width = heads * HD
    start = pl.multiple_of(half * own, own)
    kv = mm(w_ref[width:], x_ref[pl.ds(pl.multiple_of(sc[3] * LENGTH, LENGTH), LENGTH), :], NT)
    q = mm(w_ref[:width], x_ref[pl.ds(pl.multiple_of(sc[0] * own, own), own), :], NT)
    bias = jnp.transpose(jnp.broadcast_to(b_ref[0:1], (128, b_ref.shape[1])))[: 3 * width, :1]
    kv, q = kv + bias[width:], q + bias[:width]
    cosine, sine = cos_ref[...], sin_ref[...]
    own_cos, own_sin = cos_ref[:, pl.ds(start, own)], sin_ref[:, pl.ds(start, own)]
    mask = mask_row(length)
    one = jnp.ones((1, LENGTH), F32)
    kv_ref[width:] = kv[width:].astype(BF16)
    logs = []
    for h in range(heads):
        lo, hi = h * HD, (h + 1) * HD
        k_rot = rotate(kv[lo:hi], cosine, sine)
        kv_ref[lo:hi] = k_rot.astype(BF16)
        kn_ref[h] = jnp.transpose(augment(k_rot, (one, one, one, mask))).astype(BF16)
        q_rot = rotate(q[lo:hi], own_cos, own_sin)
        q_ref[lo:hi] = q_rot.astype(BF16)
        keys = kn_ref[h]
        v_aug = jnp.concatenate(
            [kv_ref[width + lo : width + hi], jnp.ones((16, LENGTH), BF16)], axis=0
        )
        row = []
        for c in range(0, own, 256):
            q_aug = augment(q_rot[:, c : c + 256], (None, None, None, jnp.ones((1, 256), F32)))
            s = mm(keys, q_aug.astype(BF16), NN)
            top = jnp.max(s, axis=0, keepdims=True)
            p = jnp.exp2((s - top) * EXP_SCALE).astype(BF16)
            o = mm(v_aug, p, NN)
            mass = o[HD : HD + 1]
            o = o[:HD] / mass
            o_ref[lo:hi, c : c + 256] = o
            ob_ref[lo:hi, c : c + 256] = o.astype(BF16)
            row.append(top + jnp.log2(mass) / EXP_SCALE)
        logs.append(jnp.concatenate(row, axis=1))
    l_ref[...] = row_select(logs, own)


def attention_backward(heads, own, arrives, sc, x_ref, kv_ref, q_ref, o_ref, do_ref, l_ref, kn_ref, cos_ref, sin_ref, *refs):
    arrived = refs[:arrives]
    dkv_ref, dq_ref, gw_ref, gb_ref = refs[arrives:]
    half, length = sc[1], sc[2]
    width = heads * HD
    start = pl.multiple_of(half * own, own)
    cosine, sine = cos_ref[...], sin_ref[...]
    own_cos, own_sin = cos_ref[:, pl.ds(start, own)], sin_ref[:, pl.ds(start, own)]
    mask = mask_row(length)
    one = jnp.ones((1, LENGTH), F32)
    own_one = jnp.ones((1, own), F32)
    tail_k = jnp.concatenate([row_select((one, one, one, mask), LENGTH), jnp.zeros((HD - 8, LENGTH), F32)], axis=0).astype(BF16)
    tail_v = jnp.concatenate([row_select((one, one, one), LENGTH), jnp.zeros((HD - 8, LENGTH), F32)], axis=0).astype(BF16)
    scale = HD ** (-0.5)
    for h in range(heads):
        lo, hi = h * HD, (h + 1) * HD
        d_out = do_ref[lo:hi].astype(F32)
        delta = jnp.sum(d_out * o_ref[lo:hi], axis=0, keepdims=True)
        qn = jnp.transpose(augment(q_ref[lo:hi].astype(F32), (*split3(-l_ref[h : h + 1]), own_one))).astype(BF16)
        dn = jnp.transpose(augment(d_out, split3(-delta))).astype(BF16)
        k_aug = jnp.concatenate([kv_ref[lo:hi], tail_k], axis=0)
        v_aug = jnp.concatenate([kv_ref[width + lo : width + hi], tail_v], axis=0)
        keys = kn_ref[h]
        dk = dv = None
        dq = []
        for c in range(0, own, 256):
            p = jnp.exp2(mm(qn[c : c + 256], k_aug, NN) * EXP_SCALE)
            dp = mm(dn[c : c + 256], v_aug, NN)
            ds = (p * dp).astype(BF16)
            dq.append(mm(ds, keys, NN))
            dk_part = mm(q_ref[lo:hi, c : c + 256], ds, NN)
            dv_part = mm(do_ref[lo:hi, c : c + 256], p.astype(BF16), NN)
            dk = dk_part if dk is None else dk + dk_part
            dv = dv_part if dv is None else dv + dv_part
        dq_t = jnp.transpose(jnp.concatenate(dq, axis=0))[:HD]
        dq_ref[lo:hi] = (unrotate(dq_t, own_cos, own_sin) * scale).astype(BF16)
        dkv_ref[lo:hi] = (unrotate(dk, cosine, sine) * scale).astype(BF16)
        dkv_ref[width + lo : width + hi] = dv.astype(BF16)
    gq = mm(dq_ref[...], x_ref[pl.ds(pl.multiple_of(sc[0] * own, own), own), :], NN)
    gkv = mm(dkv_ref[...], x_ref[pl.ds(pl.multiple_of(sc[3] * LENGTH, LENGTH), LENGTH), :], NN)
    if arrives:
        gq = gq + arrived[0][:width].astype(F32)
        gkv = gkv + arrived[0][width:].astype(F32)
    gw_ref[:width] = gq.astype(gw_ref.dtype)
    gw_ref[width:] = gkv.astype(gw_ref.dtype)
    gb_ref[:, :width] = mm(jnp.ones((8, own), BF16), dq_ref[...], NT)
    gb_ref[:, width:] = mm(jnp.ones((8, LENGTH), BF16), dkv_ref[...], NT)


def norm_stats(v):
    centered = v - jnp.mean(v, axis=-1, keepdims=True)
    inverse = lax.rsqrt(jnp.mean(centered * centered, axis=-1, keepdims=True) + EPSILON)
    return centered * inverse, inverse


def norm_back(grad, hat, inverse, gain):
    scaled = grad * gain
    return inverse * (
        scaled
        - jnp.mean(scaled, axis=-1, keepdims=True)
        - hat * jnp.mean(scaled * hat, axis=-1, keepdims=True)
    )


def project_norm(*refs):
    sc, x_ref = refs[0], refs[1]
    o_refs, w_refs = refs[2:6], refs[6:10]
    bias_ref, gain_ref, shift_ref, n_ref, nt_ref, hat_ref, inv_ref = refs[10:]
    rows = hat_ref.shape[0]
    start = pl.multiple_of(sc[0] * rows, rows)
    total = x_ref[pl.ds(start, rows), :].astype(F32) + bias_ref[...]
    for o_ref, w_ref in zip(o_refs, w_refs):
        total = total + mm(o_ref[...], w_ref[...], TN)
    hat, inverse = norm_stats(total)
    n = hat * gain_ref[...] + shift_ref[...]
    hat_ref[...] = hat
    inv_ref[...] = inverse
    n_ref[...] = n.astype(BF16)
    nt_ref[...] = jnp.transpose(n).astype(BF16)


def gelu_parts(z):
    e = jnp.exp2(z * z * (-0.5 * math.log2(math.e)))
    t = 1.0 / (1.0 + jnp.abs(z) * (ERF_P / math.sqrt(2.0)))
    poly = jnp.full_like(z, 0.5 * ERF_C[-1])
    for c in ERF_C[-2::-1]:
        poly = poly * t + 0.5 * c
    tail = poly * e
    phi = jnp.where(z >= 0, 1.0 - tail, tail)
    return z * phi, phi + z * e * (1.0 / math.sqrt(2.0 * math.pi))


def ffn_forward(block, sc, n_ref, wi_ref, bi_ref, wo_ref, *refs):
    g_ref, d_ref, f_ref = refs[-3:]
    total = refs[0][...] if len(refs) > 3 else None
    for c in range(0, wi_ref.shape[1], block):
        z = mm(n_ref[...], wi_ref[:, c : c + block], NN) + bi_ref[1:2, c : c + block]
        g, d = gelu_parts(z)
        g = g.astype(BF16)
        g_ref[:, c : c + block] = g
        d_ref[:, c : c + block] = d
        part = mm(g, wo_ref[c : c + block], NN)
        total = part if total is None else total + part
    f_ref[...] = total


def second_norm(sc, f_ref, hat_ref, cot_ref, g1_ref, s1_ref, ob_ref, g2_ref, s2_ref, out_ref, dr_ref, df_ref, small_ref):
    rows = f_ref.shape[0]
    first = hat_ref[...] * g1_ref[...] + s1_ref[...]
    hat, inverse = norm_stats(first + f_ref[...] + ob_ref[...])
    out_ref[...] = (hat * g2_ref[...] + s2_ref[...]).astype(BF16)
    place = lax.broadcasted_iota(jnp.int32, (rows, 1), 0) + sc[1] * rows
    grad = jnp.where(place < sc[2], cot_ref[...].astype(F32), 0.0)
    dr = norm_back(grad, hat, inverse, g2_ref[...])
    dr_ref[...] = dr
    df_ref[...] = dr.astype(BF16)
    sums = [jnp.sum(v, axis=0, keepdims=True) for v in (grad * hat, grad, dr)]
    small_ref[...] = row_select(sums, f_ref.shape[1])


def outer_odd(sc, one_ref, three_ref, df_ref, *out_refs):
    count = out_refs[0].shape[0] // 2
    df = df_ref[...]
    for j, g_ref in enumerate((one_ref, three_ref)):
        total = mm(g_ref[...], df, TN).astype(BF16)
        for k, out_ref in enumerate(out_refs):
            out_ref[j * count : (j + 1) * count] = total[k * count : (k + 1) * count]


def outer_even(sc, zero_ref, two_ref, df_ref, *refs):
    parts = len(refs) // 3
    arrived, out_refs = refs[:parts], refs[parts:]
    count = arrived[0].shape[0] // 2
    df = df_ref[...]
    for j, g_ref in enumerate((zero_ref, two_ref)):
        total = mm(g_ref[...], df, TN)
        for k in range(parts):
            out_ref = out_refs[2 * k + j]
            add = arrived[k][j * count : (j + 1) * count].astype(F32)
            out_ref[...] = (total[k * count : (k + 1) * count] + add).astype(out_ref.dtype)


def ffn_backward(block, sc, df_ref, wo_ref, d_ref, wi_ref, nt_ref, dn_in_ref, *refs):
    arrived, (gb_ref, dn_ref, gi_ref) = refs[:-3], refs[-3:]
    total = dn_in_ref[...]
    for c in range(0, d_ref.shape[1], block):
        at = slice(c, c + block)
        dz = (mm(df_ref[...], wo_ref[at], NT) * d_ref[:, at]).astype(BF16)
        gb_ref[:, at] = jnp.sum(dz.astype(F32), axis=0, keepdims=True)
        piece = mm(nt_ref[...], dz, NN)
        for ref in arrived:
            piece = piece + ref[:, at].astype(F32)
        gi_ref[:, at] = piece.astype(gi_ref.dtype)
        total = total + mm(dz, wi_ref[:, at], NT)
    dn_ref[...] = total


def first_norm_back(sc, *refs):
    dn_ref, hat_ref, inv_ref, gain_ref = refs[:4]
    o_refs, w_refs = refs[4:8], refs[8:12]
    dr_ref, small_ref = refs[12:14]
    do_refs, odd_ref, two_ref, zero_ref = refs[14:18], refs[18], refs[19], refs[20]
    grad, hat = dn_ref[...], hat_ref[...]
    dr = norm_back(grad, hat, inv_ref[...], gain_ref[...])
    dr_ref[...] = dr
    low = dr.astype(BF16)
    sums = [jnp.sum(v, axis=0, keepdims=True) for v in (dr, grad * hat, grad)]
    small_ref[...] = row_select(sums, grad.shape[1])
    count = two_ref.shape[0]
    for r in range(4):
        do_refs[r][...] = mm(w_refs[r][...], low, NT).astype(BF16)
        part = mm(o_refs[r][...], low, NN)
        if r % 2:
            odd_ref[(r // 2) * count : (r // 2 + 1) * count] = part.astype(BF16)
        else:
            (two_ref if r else zero_ref)[...] = part


def token_grad(sc, *refs):
    dkv, dq, w, dr_ref = refs[:4], refs[4:8], refs[8:12], refs[12]
    own_ref, other_ref = refs[13:]
    rows = own_ref.shape[0]
    mine = pl.multiple_of(sc[1] * rows, rows)
    others = pl.multiple_of((1 - sc[1]) * rows, rows)
    total, other = dr_ref[...], None
    for d_ref, q_ref, w_ref in zip(dkv, dq, w):
        width = q_ref.shape[0]
        part = mm(d_ref[:, pl.ds(others, rows)], w_ref[width:], TN)
        other = part if other is None else other + part
        total = total + mm(d_ref[:, pl.ds(mine, rows)], w_ref[width:], TN)
        total = total + mm(q_ref[...], w_ref[:width], TN)
    own_ref[...] = total
    other_ref[...] = other.astype(BF16)


def pack_small(sc, small2, small1, *refs):
    inner, qkv, out_ref = refs[:4], refs[4:8], refs[8]
    out_ref[...] = jnp.zeros(out_ref.shape, F32)
    out_ref[0:3] = small2[0:3]
    out_ref[3:6] = small1[0:3]
    for r in range(4):
        out_ref[pl.ds(8 + (sc[0] ^ r), 1), :] = inner[r][...]
        out_ref[pl.ds(12 + (sc[0] ^ r), 1), pl.ds(0, qkv[r].shape[1])] = qkv[r][0:1]


def swap(v, axis, bit):
    size = lax.axis_size(axis)
    return lax.ppermute(v, axis, [(i, i ^ bit) for i in range(size)])


def after(v, *others):
    return lax.optimization_barrier((v, *others))[0]


def dp_upper(bit):
    return (lax.axis_index("dp") & bit) > 0


class Chunk:
    def __init__(self, order, two):
        size = lax.axis_size("dp")
        bits = [1 << i for i in range(size.bit_length() - 1)]
        if "all" not in order:
            order = [b for b in order if b == "x" or b in bits]
            order += [b for b in bits if b not in order]
        self.order = list(order)
        self.last = [b for b in self.order if b != "x"][-1]
        self.back = ["share"] if "all" in order else [b for b in self.order[::-1] if b not in ("x", self.last)]
        self.two, self.zero = two, None
        self.received = self.total = self.result = None
        self.stage = "start"
        self.finished = False

    def first(self):
        return self.order[0] == "x"

    def merged(self):
        if self.stage == "start":
            return jnp.stack([self.zero.astype(F32), self.two.astype(F32)])
        arrived = self.received.astype(F32)
        if self.stage == "x" and self.total is None:
            return (self.zero.astype(F32) + arrived)[None]
        if self.stage == "all":
            return jnp.sum(arrived.reshape(lax.axis_size("dp"), -1, arrived.shape[-1]), axis=0)[None]
        return self.total + arrived.reshape(self.total.shape)

    def step(self):
        if self.order:
            if self.stage == "start" and self.first():
                total = None
            else:
                total = self.merged()
            self.stage = self.order.pop(0)
            if self.stage == "x":
                send = self.two if total is None else total[1]
                self.total = None if total is None else total[:1]
                send = send.astype(BF16)
                self.received = swap(send, "mp", 2)
            elif self.stage == "all":
                send = total[0].astype(BF16)
                self.received = lax.all_to_all(send, "dp", 0, 0, tiled=True)
            elif self.stage == self.last:
                send = total[0].astype(BF16)
                self.total = send.astype(F32)[None]
                self.received = swap(send, "dp", self.stage)
            else:
                upper = dp_upper(self.stage)
                n = total.shape[1] // 2
                low, high = total[:, :n], total[:, n:]
                send = jnp.where(upper, low, high).astype(BF16).reshape(-1, total.shape[-1])
                self.total = jnp.where(upper, high, low)
                self.received = swap(send, "dp", self.stage)
            return send
        if self.back:
            if self.stage == self.last:
                self.held = self.merged()[0].astype(BF16)
            else:
                self.held = self.joined()
            self.stage = self.back.pop(0)
            if self.stage == "share":
                size = lax.axis_size("dp")
                self.held = jnp.broadcast_to(self.held[None], (size, *self.held.shape)).reshape(-1, self.held.shape[-1])
                self.received = lax.all_to_all(self.held, "dp", 0, 0, tiled=True)
            else:
                self.received = swap(self.held, "dp", self.stage)
            return self.held
        self.result = (self.received if self.stage == "share" else self.joined()).astype(F32)
        self.finished = True
        return self.result

    def joined(self):
        pair = (self.held, self.received)
        return jnp.where(dp_upper(self.stage), jnp.concatenate(pair[::-1]), jnp.concatenate(pair))


class Everywhere:
    def __init__(self, v):
        self.own, self.received = v, None
        self.stages = [(axis, 1 << i) for axis in ("mp", "dp") for i in range(lax.axis_size(axis).bit_length() - 1)]
        self.finished = False
        self.stage = "small"

    def step(self):
        if self.received is not None:
            self.own = self.own + self.received
        if self.stages:
            self.received = swap(self.own, *self.stages.pop(0))
        else:
            self.finished = True
        return self.own


class Gather:
    def __init__(self, own, bit):
        self.own, self.bit = own, bit
        self.received = None
        self.stage = "start"
        self.finished = False

    def step(self):
        if self.stage == "start":
            self.held = half_of(self.own, self.bit)
            self.stage, self.received = "x", swap(self.held, "mp", 2)
            return self.held
        if self.stage == "x":
            self.held = self.received
            self.stage, self.received = self.bit, swap(self.held, "dp", self.bit)
            return self.held
        self.two = join_halves(self.held, self.received, self.bit)
        self.stage = "core"
        self.three = swap(self.two, "mp", 1)
        self.finished = True
        return self.two


def half_of(v, bit):
    n = v.shape[0] // 2
    return lax.dynamic_slice_in_dim(v, jnp.where(dp_upper(bit), n, 0), n, 0)


def join_halves(mine, other, bit):
    return jnp.where(dp_upper(bit), jnp.concatenate([other, mine]), jnp.concatenate([mine, other]))


def on_device(
    tokens,
    qkv_weight,
    qkv_bias,
    output_weight,
    output_bias,
    first_gain,
    first_shift,
    inner_weight,
    inner_bias,
    outer_weight,
    outer_bias,
    second_gain,
    second_shift,
    cotangent,
    seq_lengths,
):
    depth = tokens.shape[1]
    own = cotangent.shape[0]
    width = qkv_weight.shape[2]
    heads = width // HD
    hidden = inner_weight.shape[1]
    me = lax.axis_index("mp")
    seq = me * own // LENGTH
    half = (me * own % LENGTH) // own
    length = jnp.sum(jnp.where(jnp.arange(seq_lengths.shape[0]) == seq, seq_lengths, 0))
    scalars = jnp.stack([me, half, length, seq]).astype(jnp.int32)
    cosine, sine = (jnp.asarray(t) for t in rotary_tables())
    run = Program(scalars)

    qkv_w, output_w, inner_w, outer_w = ([v] + [None] * 3 for v in (jnp.transpose(qkv_weight, (1, 2, 0)).reshape(3 * width, depth), output_weight, inner_weight, outer_weight))
    qkv_gather, output_gather, inner_gather, outer_gather = Gather(qkv_w[0], 1), Gather(output_w[0], 1), Gather(inner_w[0], 2), Gather(outer_w[0], 1)
    run.add(qkv_gather)
    biases = jnp.concatenate([jnp.pad(qkv_bias.reshape(1, -1), ((0, 0), (0, hidden - 3 * width))), inner_bias.reshape(1, -1), jnp.zeros((6, hidden), F32)])
    bias_one = swap(biases, "mp", 1)
    bias_pair = swap(jnp.concatenate([biases, bias_one]), "mp", 2)
    bias_slots = [biases, bias_one, bias_pair[:8], bias_pair[8:]]
    rows = {n: v.reshape(1, -1) for n, v in dict(ob=output_bias, g1=first_gain, s1=first_shift, b2=outer_bias, g2=second_gain, s2=second_shift).items()}
    qkv_w[1], output_w[1] = swap(qkv_w[0], "mp", 1), swap(output_w[0], "mp", 1)

    kv, q, o, ob, logs, keys = ([None] * 4 for _ in range(6))

    def attend(r):
        kv[r], q[r], o[r], ob[r], logs[r], keys[r] = run.call(
            functools.partial(attention_forward, heads, own),
            [
                sds((2 * width, LENGTH), BF16),
                sds((width, own), BF16),
                sds((width, own), F32),
                sds((width, own), BF16),
                sds((8, own), F32),
                sds((heads, LENGTH, 2 * HD), BF16),
            ],
            [tokens, qkv_w[r], bias_slots[r], cosine, sine],
            flops=2 * depth * width * (2 * LENGTH + own) + 4 * own * LENGTH * 256 * heads,
            name="attention_forward",
            us=6.0,
        )

    attend(0)
    run.wait(qkv_w[1], output_w[1])
    for gather in (output_gather, inner_gather, outer_gather):
        run.add(gather)
    attend(1)
    inner_w[1], outer_w[1] = (swap(after(w[0], kv[1]), "mp", 1) for w in (inner_w, outer_w))
    run.finish(qkv_gather)
    qkv_w[2], qkv_w[3] = qkv_gather.two, qkv_gather.three
    attend(2)
    attend(3)
    run.finish(output_gather)
    output_w[2], output_w[3] = output_gather.two, output_gather.three
    n_low, n_t, hat, inverse = run.call(
        project_norm,
        [sds((own, depth), BF16), sds((depth, own), BF16), sds((own, depth), F32), sds((own, 1), F32)],
        [tokens, *ob, *output_w, rows["ob"], rows["g1"], rows["s1"]],
        flops=2 * own * depth * depth,
        name="project_norm",
    )

    block = 256
    g, d = [None] * 4, [None] * 4

    def feed(r, *f):
        g[r], d[r], f = run.call(
            functools.partial(ffn_forward, block),
            [sds((own, hidden), BF16), sds((own, hidden), F32), sds((own, depth), F32)],
            [n_low, inner_w[r], bias_slots[r], outer_w[r], *f],
            flops=4 * own * depth * hidden,
            name="ffn_forward",
            us=5.4,
        )
        return f

    f = feed(0)
    f = feed(1, f)
    for gather in (inner_gather, outer_gather):
        run.finish(gather)
    inner_w[2:], outer_w[2:] = ([v.two, v.three] for v in (inner_gather, outer_gather))
    f = feed(2, f)
    f = feed(3, f)
    layer_out, dr2, df, small2 = run.call(
        second_norm,
        [sds((own, depth), BF16), sds((own, depth), F32), sds((own, depth), BF16), sds((8, depth), F32)],
        [f, hat, cotangent, rows["g1"], rows["s1"], rows["b2"], rows["g2"], rows["s2"]],
        flops=40 * own * depth,
        name="second_norm",
    )
    odd = run.call(
        outer_odd,
        [sds((2 * hidden, depth), BF16)],
        [g[1], g[3], df],
        flops=4 * own * depth * hidden,
        name="outer_odd",
        us=3.7,
    )
    arrived = swap(odd[0], "mp", 1)
    inner_g, inner_bg = [None] * 4, [None] * 4
    dn = dr2

    def feed_back(r, dn, *arrived):
        inner_bg[r], dn, inner_g[r] = run.call(
            functools.partial(ffn_backward, block),
            [sds((1, hidden), F32), sds((own, depth), F32), sds((depth, hidden), BF16 if r % 2 or (r == 2 and inner_sum.first()) else F32)],
            [df, outer_w[r], d[r], inner_w[r], n_t, dn, *arrived],
            flops=6 * own * depth * hidden,
            name="ffn_backward",
            us=5.4,
        )
        return dn

    outer_sum, inner_sum, qkv_sum = Chunk(OUTER_ORDER, None), Chunk(INNER_ORDER, None), Chunk(QKV_ORDER, None)
    dn = feed_back(3, dn)
    zero, outer_sum.two = run.call(
        outer_even,
        [sds((hidden, depth), F32), sds((hidden, depth), BF16 if outer_sum.first() else F32)],
        [g[0], g[2], df, arrived],
        flops=4 * own * depth * hidden,
        name="outer_even",
        us=3.0,
    )
    run.supply(outer_sum, zero)
    three = swap(inner_g[3], "mp", 1)
    dn = feed_back(1, dn)
    one = swap(inner_g[1], "mp", 1)
    dn = feed_back(2, dn, three)
    inner_sum.two = inner_g[2]
    if inner_sum.first():
        run.add(inner_sum)
    dn = feed_back(0, dn, one)
    run.supply(inner_sum, inner_g[0])
    dr1, small1, *rest = run.call(
        first_norm_back,
        [sds((own, depth), F32), sds((8, depth), F32)] + [sds((width, own), BF16)] * 4 + [sds((2 * width, depth), BF16)] + [sds((width, depth), F32)] * 2,
        [dn, hat, inverse, rows["g1"], *ob, *output_w],
        flops=4 * own * depth * depth,
        name="first_norm_back",
        us=3.9,
    )
    d_out = rest[:4]
    output_odd, output_two, output_zero = swap(rest[4], "mp", 1), rest[5], rest[6]

    dkv, dq, qkv_g, qkv_bg = ([None] * 4 for _ in range(4))

    def attend_back(r, *arrived):
        dkv[r], dq[r], qkv_g[r], qkv_bg[r] = run.call(
            functools.partial(attention_backward, heads, own, len(arrived)),
            [
                sds((2 * width, LENGTH), BF16),
                sds((width, own), BF16),
                sds((3 * width, depth), F32 if r == 0 else BF16),
                sds((8, 3 * width), F32),
            ],
            [tokens, kv[r], q[r], o[r], d_out[r], logs[r], keys[r], cosine, sine, *arrived],
            flops=2 * depth * width * (2 * LENGTH + own) + 10 * own * LENGTH * 256 * heads,
            name="attention_backward",
            us=5.4,
        )

    attend_back(3)
    three = swap(qkv_g[3], "mp", 1)
    attend_back(1)
    one = swap(qkv_g[1], "mp", 1)
    attend_back(2, three)
    output_two = (output_two + output_odd[width:].astype(F32)).astype(BF16)
    qkv_sum.two = jnp.concatenate([qkv_g[2], output_two])
    run.add(qkv_sum)
    attend_back(0, one)
    run.supply(qkv_sum, jnp.concatenate([qkv_g[0], output_zero + output_odd[:width].astype(F32)]))
    own_tokens, other_tokens = run.call(
        token_grad,
        [sds((own, depth), F32), sds((own, depth), BF16)],
        [*dkv, *dq, *qkv_w, dr1],
        flops=10 * own * depth * depth,
        name="token_grad",
        us=7.0,
    )
    token_swap = swap(other_tokens, "mp", 1)
    (packed,) = run.call(
        pack_small,
        [sds((16, depth), F32)],
        [small2, small1, *inner_bg, *qkv_bg],
        flops=1 << 20,
        name="pack_small",
        us=0.6,
    )
    small_sum = Everywhere(packed)
    run.add(small_sum)
    run.service(0)
    tokens_grad = own_tokens + token_swap.astype(F32)
    small = small_sum.own
    outer_weight_grad, inner_weight_grad = outer_sum.result, inner_sum.result
    output_weight_grad = qkv_sum.result[3 * width :]
    qkv_weight_grad = jnp.transpose(qkv_sum.result[: 3 * width].reshape(3, width, depth), (2, 0, 1))
    second_gain_grad, second_shift_grad, outer_bias_grad, output_bias_grad, first_gain_grad, first_shift_grad = (small[i] for i in range(6))
    inner_bias_grad = lax.dynamic_index_in_dim(small, 8 + me, 0, keepdims=False)
    qkv_bias_grad = lax.dynamic_index_in_dim(small, 12 + me, 0, keepdims=False)[: 3 * width].reshape(3, width)
    return (
        layer_out,
        tokens_grad,
        qkv_weight_grad,
        qkv_bias_grad,
        output_weight_grad,
        output_bias_grad,
        first_gain_grad,
        first_shift_grad,
        inner_weight_grad,
        inner_bias_grad,
        outer_weight_grad,
        outer_bias_grad,
        second_gain_grad,
        second_shift_grad,
    )


def solution(mesh):
    return jax.shard_map(
        on_device,
        mesh=mesh,
        in_specs=(
            P("dp", None),
            P(None, None, "mp"),
            P(None, "mp"),
            P("mp", None),
            P(),
            P(),
            P(),
            P(None, "mp"),
            P("mp"),
            P("mp", None),
            P(),
            P(),
            P(),
            P(("dp", "mp"), None),
            P("dp"),
        ),
        out_specs=(
            P(("dp", "mp"), None),
            P(("dp", "mp"), None),
            P(None, None, "mp"),
            P(None, "mp"),
            P("mp", None),
            P(),
            P(),
            P(),
            P(None, "mp"),
            P("mp"),
            P("mp", None),
            P(),
            P(),
            P(),
        ),
        check_vma=False,
    )
```

```python
import functools
import math

import jax
import jax.numpy as jnp
import numpy as np
from jax import lax
from jax.experimental import pallas as pl
from jax.experimental.pallas import tpu as pltpu
from jax.sharding import PartitionSpec as P

HD = 64
FORWARD_CHUNK = 512
BACKWARD_CHUNK = 256
HALF_DEPTH = HD // 2
LENGTH = 1024
EPSILON = 1e-12
NEGATIVE = -1e30
F32 = jnp.float32
BF16 = jnp.bfloat16
EXP_SCALE = HD ** (-0.5) * math.log2(math.e)

ERF_P = 0.52
ERF_C = (0.00514851, 0.23724269, 0.55266472, -0.39660497, 1.10267122, -0.61325166, 0.1121295)

NN = (((1,), (0,)), ((), ()))
NT = (((1,), (1,)), ((), ()))
TN = (((0,), (0,)), ((), ()))


def mm(a, b, dims):
    return lax.dot_general(a, b, dims, preferred_element_type=F32)


def rotary_tables():
    frequency = 10000.0 ** (-np.arange(HALF_DEPTH, dtype=np.float64) / HALF_DEPTH)
    angle = frequency[:, None] * np.arange(LENGTH, dtype=np.float64)[None, :]
    return np.concatenate([np.cos(angle), np.sin(angle)]).astype(np.float32)


ROW_US = 0.0334
HOP_US = 3.0


class Program:
    def __init__(self, scalars):
        self.scalars = scalars
        self.tokens = []
        self.clock = 0.0
        self.links = {"x": 0.0, "y": 0.0, "z": 0.0, "m": 0.0}
        self.chunks = []
        self.hold = False

    def wait(self, *values):
        self.tokens += values

    def call(self, body, outs, ins, grid=(), in_specs=None, out_specs=None, flops=0, name=None, vmem=16, us=5.0, scratch=()):
        scalars = after(self.scalars, *self.tokens)
        nbytes = sum(math.prod(a.shape) * a.dtype.itemsize for a in list(ins) + list(outs))
        whole = pl.BlockSpec(memory_space=pltpu.VMEM)
        result = pl.pallas_call(
            body,
            out_shape=outs,
            grid=grid,
            in_specs=[pl.BlockSpec(memory_space=pltpu.SMEM)] + (in_specs if in_specs is not None else [whole] * len(ins)),
            out_specs=out_specs if out_specs is not None else [whole] * len(outs),
            scratch_shapes=scratch,
            compiler_params=pltpu.CompilerParams(vmem_limit_bytes=vmem << 20),
            cost_estimate=pl.CostEstimate(flops=flops // COST_SCALE, bytes_accessed=nbytes // COST_SCALE, transcendentals=0),
            name=name,
        )(scalars, *ins)
        self.tokens = [result[0]]
        self.clock += us
        if not self.hold:
            self.service()
        return result

    def service(self, left=None):
        while True:
            waiting = [c for c in self.chunks if not c.finished]
            if not waiting or (left is not None and len(waiting) <= left):
                return
            chunk = min(waiting, key=lambda c: c.due)
            if chunk.due > self.clock and left is None:
                return
            if chunk.due == math.inf:
                return
            self.take(chunk)

    def take(self, chunk):
        self.clock = max(self.clock, chunk.due)
        if chunk.received is not None:
            chunk.received = after(chunk.received, *self.tokens)
        elif chunk.stage == "start" and hasattr(chunk, "own") and self.tokens:
            chunk.own = after(chunk.own, *self.tokens)
        made = chunk.step()
        self.tokens = [made]
        rows = math.prod(made.shape[:-1])
        self.clock += 0.6 + rows / 768 + (2.7 if chunk.stage == 4 else 1.6)
        if not chunk.finished or chunk.stage == "x":
            chunk.due = self.transfer(chunk.stage, rows)
            if getattr(chunk, "zero", 0) is None:
                chunk.arrives, chunk.due = chunk.due, math.inf


    def transfer(self, stage, rows):
        us = rows * ROW_US
        uses = {"x": {"x": us}, 1: {"y": us}, 2: {"z": us}, 4: {"m": 2 * us, "z": us}, "all": {"y": us / 2, "z": us, "m": us}, "share": {"y": us / 2, "z": us, "m": us}}.get(stage, {})
        start = max([self.clock - 1] + [self.links[n] for n in uses])
        for n, t in uses.items():
            self.links[n] = start + t
        return start + max(list(uses.values()) + [us / 13]) + (HOP_US if uses else 1.0)

    def finish(self, chunk):
        while not chunk.finished:
            self.take(chunk)

    def add(self, chunk):
        chunk.due = self.clock
        self.chunks.append(chunk)
        self.service()

    def supply(self, chunk, zero):
        chunk.zero = zero
        if chunk not in self.chunks:
            self.add(chunk)
        else:
            chunk.due = max(self.clock, chunk.arrives)
            self.service()


COST_SCALE = 16
OUTER_ORDER = (1, "x", 2, 4)
INNER_ORDER = (2, "x", 1, 4)
QKV_ORDER = (1, 2, 4)


def sds(shape, dtype):
    return jax.ShapeDtypeStruct(shape, dtype)


def rotate(v, cosine, sine):
    a, b = v[:HALF_DEPTH], v[HALF_DEPTH:]
    return jnp.concatenate([a * cosine - b * sine, b * cosine + a * sine], axis=0)


def unrotate(v, cosine, sine):
    a, b = v[:HALF_DEPTH], v[HALF_DEPTH:]
    return jnp.concatenate([a * cosine + b * sine, b * cosine - a * sine], axis=0)


def row_select(rows, columns):
    index = lax.broadcasted_iota(jnp.int32, (8, columns), 0)
    out = jnp.zeros((8, columns), F32)
    for i, r in enumerate(rows):
        if r is not None:
            out = jnp.where(index == i, r, out)
    return out


def augment(top, rows, total=2 * HD):
    columns = top.shape[1]
    tail = row_select(rows, columns)
    rest = jnp.zeros((total - HD - 8, columns), F32)
    return jnp.concatenate([top, tail, rest], axis=0)


def split3(v):
    high = v.astype(BF16).astype(F32)
    mid = (v - high).astype(BF16).astype(F32)
    return high, mid, v - high - mid


def mask_row(length):
    index = lax.broadcasted_iota(jnp.int32, (1, LENGTH), 1)
    return jnp.where(index < length, 0.0, NEGATIVE)


def place_of(sc, own, mine):
    half, seq = sc[0] % 2, sc[0] // 2
    seq = seq if mine else 1 - seq
    return pl.multiple_of(half * own, own), pl.multiple_of((1 - half) * own, own), pl.multiple_of(seq * LENGTH, LENGTH), sc[1 + seq]


def attention_forward(heads, own, mine, sc, x_ref, w_ref, b_ref, wo_ref, table_ref, kv_ref, q_ref, o_ref, ob_ref, l_ref, kn_ref, keep_ref, give_ref, k_ref, s_ref):
    near, far, start, length = place_of(sc, own, mine)
    width = heads * HD
    x = x_ref[pl.ds(start, LENGTH), :]
    bias = jnp.transpose(jnp.broadcast_to(b_ref[0:1], (128, b_ref.shape[1])))[: 3 * width, :1]
    kv = mm(w_ref[width:], x, NT) + bias[width:]
    q = mm(w_ref[:width], x, NT) + bias[:width]
    cosine, sine = table_ref[:HALF_DEPTH], table_ref[HALF_DEPTH:]
    mask = mask_row(length)
    one = jnp.ones((1, LENGTH), F32)
    kv_ref[width:] = kv[width:].astype(BF16)
    k_ref[...], s_ref[...] = kv[:width], q
    l_ref[...] = jnp.zeros(l_ref.shape, F32)

    def head(h, carry):
        at = pl.ds(pl.multiple_of(h * HD, HD), HD)
        v_at = pl.ds(pl.multiple_of(width + h * HD, HD), HD)
        k_rot = rotate(k_ref[at, :], cosine, sine)
        kv_ref[at, :] = k_rot.astype(BF16)
        kn_ref[h] = jnp.transpose(augment(k_rot, (one, one, one, mask))).astype(BF16)
        q_rot = rotate(s_ref[at, :], cosine, sine)
        q_ref[at, :] = q_rot.astype(BF16)
        keys = kn_ref[h]
        v_aug = jnp.concatenate([kv_ref[v_at, :], jnp.ones((16, LENGTH), BF16)], axis=0)
        for c in range(0, LENGTH, FORWARD_CHUNK):
            q_aug = augment(q_rot[:, c : c + FORWARD_CHUNK], (None, None, None, jnp.ones((1, FORWARD_CHUNK), F32)))
            s = mm(keys, q_aug.astype(BF16), NN)
            top = jnp.max(s, axis=0, keepdims=True)
            p = jnp.exp2((s - top) * EXP_SCALE).astype(BF16)
            o = mm(v_aug, p, NN)
            mass = o[HD : HD + 1]
            o = o[:HD] / mass
            o_ref[at, c : c + FORWARD_CHUNK] = o
            ob_ref[at, c : c + FORWARD_CHUNK] = o.astype(BF16)
            l_ref[pl.ds(h, 1), c : c + FORWARD_CHUNK] = top + jnp.log2(mass) / EXP_SCALE
        return carry

    lax.fori_loop(0, heads, head, 0)
    keep_ref[...] = mm(ob_ref[:, pl.ds(near, own)], wo_ref[...], TN)
    give_ref[...] = mm(ob_ref[:, pl.ds(far, own)], wo_ref[...], TN).astype(give_ref.dtype)


def attention_backward(heads, own, mine, sc, x_ref, kv_ref, q_ref, o_ref, ob_ref, l_ref, kn_ref, near_ref, far_ref, wo_ref, table_ref, *refs):
    before, (dy_ref, gw_ref, gb_ref), (da_ref, do_ref) = refs[:-5], refs[-5:-2], refs[-2:]
    near, far, start, length = place_of(sc, own, mine)
    width = heads * HD
    da_ref[pl.ds(near, own), :] = near_ref[...]
    da_ref[pl.ds(far, own), :] = far_ref[...]
    do_ref[...] = mm(wo_ref[...], da_ref[...], NT).astype(BF16)
    cosine, sine = table_ref[:HALF_DEPTH], table_ref[HALF_DEPTH:]
    mask = mask_row(length)
    one = jnp.ones((1, LENGTH), F32)
    zeros = jnp.zeros((HD - 8, LENGTH), F32)
    tail_k = jnp.concatenate([row_select((one, one, one, mask), LENGTH), zeros], axis=0).astype(BF16)
    tail_v = jnp.concatenate([row_select((one, one, one), LENGTH), zeros], axis=0).astype(BF16)
    scale = HD ** (-0.5)
    def head(h, carry):
        at = pl.ds(pl.multiple_of(h * HD, HD), HD)
        k_at = pl.ds(pl.multiple_of(width + h * HD, HD), HD)
        v_at = pl.ds(pl.multiple_of(2 * width + h * HD, HD), HD)
        d_out = do_ref[at, :].astype(F32)
        delta = jnp.sum(d_out * o_ref[at, :], axis=0, keepdims=True)
        qn = jnp.transpose(augment(q_ref[at, :].astype(F32), (*split3(-l_ref[pl.ds(h, 1), :]), one))).astype(BF16)
        dn = jnp.transpose(augment(d_out, split3(-delta))).astype(BF16)
        k_aug = jnp.concatenate([kv_ref[at, :], tail_k], axis=0)
        v_aug = jnp.concatenate([kv_ref[k_at, :], tail_v], axis=0)
        keys = kn_ref[h]
        dk = dv = None
        dq = []
        for c in range(0, LENGTH, BACKWARD_CHUNK):
            p = jnp.exp2(mm(qn[c : c + BACKWARD_CHUNK], k_aug, NN) * EXP_SCALE)
            dp = mm(dn[c : c + BACKWARD_CHUNK], v_aug, NN)
            ds = (p * dp).astype(BF16)
            dq.append(mm(ds, keys, NN))
            dk_part = mm(q_ref[at, c : c + BACKWARD_CHUNK], ds, NN)
            dv_part = mm(do_ref[at, c : c + BACKWARD_CHUNK], p.astype(BF16), NN)
            dk = dk_part if dk is None else dk + dk_part
            dv = dv_part if dv is None else dv + dv_part
        dq_t = jnp.transpose(jnp.concatenate(dq, axis=0))[:HD]
        dy_ref[at, :] = (unrotate(dq_t, cosine, sine) * scale).astype(BF16)
        dy_ref[k_at, :] = (unrotate(dk, cosine, sine) * scale).astype(BF16)
        dy_ref[v_at, :] = dv.astype(BF16)
        return carry

    lax.fori_loop(0, heads, head, 0)
    gw = mm(dy_ref[...], x_ref[pl.ds(start, LENGTH), :], NN)
    go = mm(ob_ref[...], da_ref[...], NN)
    gb = mm(jnp.ones((8, LENGTH), BF16), dy_ref[...], NT)
    if before:
        gw, go, gb = gw + before[0][: 3 * width], go + before[0][3 * width :], gb + before[1][...]
    gw_ref[: 3 * width] = gw
    gw_ref[3 * width :] = go
    gb_ref[...] = gb


def norm_stats(v):
    centered = v - jnp.mean(v, axis=-1, keepdims=True)
    inverse = lax.rsqrt(jnp.mean(centered * centered, axis=-1, keepdims=True) + EPSILON)
    return centered * inverse, inverse


def norm_back(grad, hat, inverse, gain):
    scaled = grad * gain
    return inverse * (
        scaled
        - jnp.mean(scaled, axis=-1, keepdims=True)
        - hat * jnp.mean(scaled * hat, axis=-1, keepdims=True)
    )


def row_blocks(rows, step, block=128):
    def body(i, carry):
        step(pl.ds(pl.multiple_of(i * block, block), block))
        return carry

    lax.fori_loop(0, rows // block, body, 0)


def project_norm(sc, x_ref, keep_ref, core_ref, far_ref, bias_ref, gain_ref, shift_ref, n_ref, nt_ref, hat_ref, inv_ref):
    rows = hat_ref.shape[0]
    start = pl.multiple_of(sc[0] * rows, rows)

    def step(at):
        total = x_ref[pl.ds(pl.multiple_of(start + at.start, at.size), at.size), :].astype(F32) + bias_ref[...]
        total = total + (keep_ref[at, :] + core_ref[at, :].astype(F32) + far_ref[at, :].astype(F32))
        hat, inverse = norm_stats(total)
        n = hat * gain_ref[...] + shift_ref[...]
        hat_ref[at, :] = hat
        inv_ref[at, :] = inverse
        n_ref[at, :] = n.astype(BF16)
        nt_ref[:, at] = jnp.transpose(n).astype(BF16)

    row_blocks(rows, step)


def gelu_parts(z):
    e = jnp.exp2(z * z * (-0.5 * math.log2(math.e)))
    t = 1.0 / (1.0 + jnp.abs(z) * (ERF_P / math.sqrt(2.0)))
    poly = jnp.full_like(z, 0.5 * ERF_C[-1])
    for c in ERF_C[-2::-1]:
        poly = poly * t + 0.5 * c
    tail = poly * e
    phi = jnp.where(z >= 0, 1.0 - tail, tail)
    return z * phi, phi + z * e * (1.0 / math.sqrt(2.0 * math.pi))


def ffn_forward(block, sc, n_ref, wi_ref, bi_ref, wo_ref, *refs):
    g_ref, d_ref, f_ref = refs[-3:]

    def step(at):
        z = mm(n_ref[at, :], wi_ref[...], NN) + bi_ref[1:2]
        g, d = gelu_parts(z)
        g = g.astype(BF16)
        g_ref[at, :] = g
        d_ref[at, :] = d
        part = mm(g, wo_ref[...], NN)
        f_ref[at, :] = part + refs[0][at, :] if len(refs) > 3 else part

    row_blocks(n_ref.shape[0], step, block)


def add_sums(small_ref, at, values):
    @pl.when(at.start == 0)
    def _():
        small_ref[...] = jnp.zeros(small_ref.shape, F32)

    small_ref[...] += row_select([jnp.sum(v, axis=0, keepdims=True) for v in values], small_ref.shape[1])


def second_norm(sc, f_ref, hat_ref, cot_ref, g1_ref, s1_ref, ob_ref, g2_ref, s2_ref, out_ref, dr_ref, df_ref, small_ref):
    rows = f_ref.shape[0]

    def step(at):
        first = hat_ref[at, :] * g1_ref[...] + s1_ref[...]
        hat, inverse = norm_stats(first + f_ref[at, :] + ob_ref[...])
        out_ref[at, :] = (hat * g2_ref[...] + s2_ref[...]).astype(BF16)
        place = lax.broadcasted_iota(jnp.int32, (at.size, 1), 0) + at.start + (sc[0] % 2) * rows
        grad = jnp.where(place < sc[1 + sc[0] // 2], cot_ref[at, :].astype(F32), 0.0)
        dr = norm_back(grad, hat, inverse, g2_ref[...])
        dr_ref[at, :] = dr
        df_ref[at, :] = dr.astype(BF16)
        add_sums(small_ref, at, (grad * hat, grad, dr))

    row_blocks(rows, step)


def outer_odd(sc, one_ref, three_ref, df_ref, *out_refs):
    count = out_refs[0].shape[0] // 2
    df = df_ref[...]
    for j, g_ref in enumerate((one_ref, three_ref)):
        total = mm(g_ref[...], df, TN).astype(BF16)
        for k, out_ref in enumerate(out_refs):
            out_ref[j * count : (j + 1) * count] = total[k * count : (k + 1) * count]


def outer_even(sc, zero_ref, two_ref, df_ref, *refs):
    parts = len(refs) // 3
    arrived, out_refs = refs[:parts], refs[parts:]
    count = arrived[0].shape[0] // 2
    df = df_ref[...]
    for j, g_ref in enumerate((zero_ref, two_ref)):
        total = mm(g_ref[...], df, TN)
        for k in range(parts):
            out_ref = out_refs[2 * k + j]
            add = arrived[k][j * count : (j + 1) * count].astype(F32)
            out_ref[...] = (total[k * count : (k + 1) * count] + add).astype(out_ref.dtype)


def ffn_backward(block, sc, df_ref, wo_ref, d_ref, wi_ref, nt_ref, dn_in_ref, *refs):
    arrived, (gb_ref, dn_ref, gi_ref, dz_ref) = refs[:-4], refs[-4:]

    def step(at):
        dz = (mm(df_ref[at, :], wo_ref[...], NT) * d_ref[at, :]).astype(BF16)
        dz_ref[at, :] = dz
        dn_ref[at, :] = dn_in_ref[at, :] + mm(dz, wi_ref[...], NT)

    row_blocks(dn_ref.shape[0], step, block)
    gb_ref[...] = jnp.sum(dz_ref[...].astype(F32), axis=0, keepdims=True)
    total = mm(nt_ref[...], dz_ref[...], NN)
    for ref in arrived:
        total = total + ref[...].astype(F32)
    gi_ref[...] = total.astype(gi_ref.dtype)


def first_norm_back(sc, dn_ref, hat_ref, inv_ref, gain_ref, dr_ref, low_ref, small_ref):
    def step(at):
        grad, hat = dn_ref[at, :], hat_ref[at, :]
        dr = norm_back(grad, hat, inv_ref[at, :], gain_ref[...])
        dr_ref[at, :] = dr
        low_ref[at, :] = dr.astype(BF16)
        add_sums(small_ref, at, (dr, grad * hat, grad))

    row_blocks(dn_ref.shape[0], step)


def token_grad(own, sc, dy_ref, w_ref, *refs):
    before, (keep_ref, give_ref) = refs[:-2], refs[-2:]
    near, far, _, _ = place_of(sc, own, True)
    total = mm(dy_ref[:, pl.ds(near, own)], w_ref[...], TN)
    for ref in before:
        total = total + ref[...]
    keep_ref[...] = total
    give_ref[...] = mm(dy_ref[:, pl.ds(far, own)], w_ref[...], TN).astype(BF16)


def pack_small(sc, small2, small1, *refs):
    inner, qkv, out_ref = refs[:4], refs[4], refs[5]
    out_ref[...] = jnp.zeros(out_ref.shape, F32)
    out_ref[0:3] = small2[0:3]
    out_ref[3:6] = small1[0:3]
    for r in range(4):
        out_ref[pl.ds(8 + (sc[0] ^ r), 1), :] = inner[r][...]
    out_ref[pl.ds(12 + sc[0], 1), pl.ds(0, qkv.shape[1])] = qkv[0:1]


def swap(v, axis, bit):
    size = lax.axis_size(axis)
    return lax.ppermute(v, axis, [(i, i ^ bit) for i in range(size)])


def after(v, *others):
    return lax.optimization_barrier((v, *others))[0]


def dp_upper(bit):
    return (lax.axis_index("dp") & bit) > 0


class Chunk:
    def __init__(self, order, two):
        size = lax.axis_size("dp")
        bits = [1 << i for i in range(size.bit_length() - 1)]
        if "all" not in order:
            order = [b for b in order if b == "x" or b in bits]
            order += [b for b in bits if b not in order]
        self.order = list(order)
        self.last = [b for b in self.order if b != "x"][-1]
        self.back = ["share"] if "all" in order else [b for b in self.order[::-1] if b not in ("x", self.last)]
        self.two, self.zero = two, None
        self.received = self.total = self.result = None
        self.stage = "start"
        self.finished = False

    def first(self):
        return self.order[0] == "x"

    def merged(self):
        if self.stage == "start":
            return jnp.stack([v.astype(F32) for v in (self.zero, self.two) if v is not None])
        arrived = self.received.astype(F32)
        if self.stage == "x" and self.total is None:
            return (self.zero.astype(F32) + arrived)[None]
        if self.stage == "all":
            return jnp.sum(arrived.reshape(lax.axis_size("dp"), -1, arrived.shape[-1]), axis=0)[None]
        return self.total + arrived.reshape(self.total.shape)

    def step(self):
        if self.order:
            if self.stage == "start" and self.first():
                total = None
            else:
                total = self.merged()
            self.stage = self.order.pop(0)
            if self.stage == "x":
                send = self.two if total is None else total[1]
                self.total = None if total is None else total[:1]
                send = send.astype(BF16)
                self.received = swap(send, "mp", 2)
            elif self.stage == "all":
                send = total[0].astype(BF16)
                self.received = lax.all_to_all(send, "dp", 0, 0, tiled=True)
            elif self.stage == self.last:
                send = total[0].astype(BF16)
                self.total = send.astype(F32)[None]
                self.received = swap(send, "dp", self.stage)
            else:
                upper = dp_upper(self.stage)
                n = total.shape[1] // 2
                low, high = total[:, :n], total[:, n:]
                send = jnp.where(upper, low, high).astype(BF16).reshape(-1, total.shape[-1])
                self.total = jnp.where(upper, high, low)
                self.received = swap(send, "dp", self.stage)
            return send
        if self.back:
            if self.stage == self.last:
                self.held = self.merged()[0].astype(BF16)
            else:
                self.held = self.joined()
            self.stage = self.back.pop(0)
            if self.stage == "share":
                size = lax.axis_size("dp")
                self.held = jnp.broadcast_to(self.held[None], (size, *self.held.shape)).reshape(-1, self.held.shape[-1])
                self.received = lax.all_to_all(self.held, "dp", 0, 0, tiled=True)
            else:
                self.received = swap(self.held, "dp", self.stage)
            return self.held
        self.result = (self.received if self.stage == "share" else self.joined()).astype(F32)
        self.finished = True
        return self.result

    def joined(self):
        pair = (self.held, self.received)
        return jnp.where(dp_upper(self.stage), jnp.concatenate(pair[::-1]), jnp.concatenate(pair))


class Everywhere:
    def __init__(self, v):
        self.own, self.received = v, None
        self.stages = [(axis, 1 << i) for axis in ("mp", "dp") for i in range(lax.axis_size(axis).bit_length() - 1)]
        self.finished = False
        self.stage = "small"

    def step(self):
        if self.received is not None:
            self.own = self.own + self.received
        if self.stages:
            self.received = swap(self.own, *self.stages.pop(0))
        else:
            self.finished = True
        return self.own


class Exchange:
    def __init__(self):
        self.finished = False
        self.stage = "core"

    def begin(self, run, keep, give):
        self.keep = keep
        self.received = swap(give, "mp", 1)
        run.chunks.append(self)
        self.due = run.transfer("core", give.shape[0] * give.dtype.itemsize // 2)

    def step(self):
        made = (self.keep + self.received.astype(F32)).astype(BF16)
        self.received = swap(made, "mp", 2)
        self.stage = "x"
        self.finished = True
        return made


class Gather:
    def __init__(self, own, bits):
        self.own, self.bits = own, list(bits)
        self.received = None
        self.stage = "start"
        self.finished = False

    def step(self):
        if self.stage == "start":
            self.held = self.own
            for bit in self.bits[::-1]:
                self.held = half_of(self.held, bit)
            self.stage, self.received = "x", swap(self.held, "mp", 2)
            return self.held
        if self.stage == "x":
            self.held = self.received
        else:
            self.held = join_halves(self.held, self.received, self.stage)
        if self.bits:
            self.stage = self.bits.pop(0)
            self.received = swap(self.held, "dp", self.stage)
            return self.held
        self.two, self.stage = self.held, "core"
        self.three = swap(self.two, "mp", 1)
        self.finished = True
        return self.two


def half_of(v, bit):
    n = v.shape[0] // 2
    return lax.dynamic_slice_in_dim(v, jnp.where(dp_upper(bit), n, 0), n, 0)


def join_halves(mine, other, bit):
    return jnp.where(dp_upper(bit), jnp.concatenate([other, mine]), jnp.concatenate([mine, other]))


def on_device(
    tokens,
    qkv_weight,
    qkv_bias,
    output_weight,
    output_bias,
    first_gain,
    first_shift,
    inner_weight,
    inner_bias,
    outer_weight,
    outer_bias,
    second_gain,
    second_shift,
    cotangent,
    seq_lengths,
):
    depth = tokens.shape[1]
    own = cotangent.shape[0]
    width = qkv_weight.shape[2]
    heads = width // HD
    hidden = inner_weight.shape[1]
    me = lax.axis_index("mp")
    scalars = jnp.concatenate([me[None].astype(jnp.int32), seq_lengths])
    table = jnp.asarray(rotary_tables())
    run = Program(scalars)

    biases = jnp.concatenate([jnp.pad(qkv_bias.reshape(1, -1), ((0, 0), (0, hidden - 3 * width))), inner_bias.reshape(1, -1), jnp.zeros((6, hidden), F32)])
    bias_one = swap(biases, "mp", 1)
    inner_w, outer_w = [inner_weight, None, None, None], [outer_weight, None, None, None]
    inner_w[1], outer_w[1] = swap(inner_weight, "mp", 1), swap(outer_weight, "mp", 1)
    inner_gather, outer_gather = Gather(inner_weight, (1, 2)), Gather(outer_weight, (2, 1))
    run.add(inner_gather)
    run.add(outer_gather)
    bias_pair = swap(after(jnp.concatenate([biases, bias_one]), *run.tokens), "mp", 2)
    bias_slots = [biases, bias_one, bias_pair[:8], bias_pair[8:]]
    qkv_w = jnp.transpose(qkv_weight, (1, 2, 0)).reshape(3 * width, depth)
    rows = {n: v.reshape(1, -1) for n, v in dict(ob=output_bias, g1=first_gain, s1=first_shift, b2=outer_bias, g2=second_gain, s2=second_shift).items()}

    kv, q, o, ob, logs, keys = ([None] * 2 for _ in range(6))

    def attend(mine):
        kv[mine], q[mine], o[mine], ob[mine], logs[mine], keys[mine], keep, give = run.call(
            functools.partial(attention_forward, heads, own, mine),
            [
                sds((2 * width, LENGTH), BF16),
                sds((width, LENGTH), BF16),
                sds((width, LENGTH), F32),
                sds((width, LENGTH), BF16),
                sds((8, LENGTH), F32),
                sds((heads, LENGTH, 2 * HD), BF16),
                sds((own, depth), F32),
                sds((own, depth), BF16 if mine else F32),
            ],
            [tokens, qkv_w, biases, output_weight, table],
            flops=2 * depth * width * 4 * LENGTH + 4 * LENGTH * LENGTH * 256 * heads,
            name="attention_forward",
            us=8.7,
            scratch=[pltpu.VMEM((width, LENGTH), F32)] * 2,
        )
        return keep, give

    run.wait(inner_w[1], outer_w[1], bias_one)
    run.clock += 3.0
    far_sum = Exchange()
    run.hold = True
    keep, give = attend(0)
    run.hold = False
    for gather in (inner_gather, outer_gather):
        gather.received = after(gather.received, *run.tokens)
    far_sum.begin(run, keep, after(give, bias_pair, inner_gather.received, outer_gather.received))
    run.finish(far_sum)
    far = far_sum.received
    run.clock = max(run.clock, inner_gather.due, outer_gather.due)
    run.service()
    run.clock = max(run.clock, inner_gather.due, outer_gather.due)
    run.service()
    keep, give = attend(1)
    core = swap(give, "mp", 1)
    run.clock = max(run.clock, far_sum.due)
    run.wait(far, core)
    run.service()
    n_low, n_t, hat, inverse = run.call(
        project_norm,
        [sds((own, depth), BF16), sds((depth, own), BF16), sds((own, depth), F32), sds((own, 1), F32)],
        [tokens, keep, core, far, rows["ob"], rows["g1"], rows["s1"]],
        flops=40 * own * depth,
        name="project_norm",
        us=2.0,
    )

    block = 512
    g, d = [None] * 4, [None] * 4

    def feed(r, *f):
        g[r], d[r], f = run.call(
            functools.partial(ffn_forward, block),
            [sds((own, hidden), BF16), sds((own, hidden), F32), sds((own, depth), F32)],
            [n_low, inner_w[r], bias_slots[r], outer_w[r], *f],
            flops=4 * own * depth * hidden,
            name="ffn_forward",
            us=3.0,
        )
        return f

    f = feed(0)
    f = feed(1, f)
    for gather in (inner_gather, outer_gather):
        run.finish(gather)
    inner_w[2:], outer_w[2:] = ([v.two, v.three] for v in (inner_gather, outer_gather))
    f = feed(2, f)
    f = feed(3, f)
    layer_out, dr2, df, small2 = run.call(
        second_norm,
        [sds((own, depth), BF16), sds((own, depth), F32), sds((own, depth), BF16), sds((8, depth), F32)],
        [f, hat, cotangent, rows["g1"], rows["s1"], rows["b2"], rows["g2"], rows["s2"]],
        flops=40 * own * depth,
        name="second_norm",
        us=2.7,
    )
    odd = run.call(
        outer_odd,
        [sds((2 * hidden, depth), BF16)],
        [g[1], g[3], df],
        flops=4 * own * depth * hidden,
        name="outer_odd",
        us=1.9,
    )
    arrived = swap(odd[0], "mp", 1)
    inner_g, inner_bg = [None] * 4, [None] * 4
    dn = dr2

    def feed_back(r, dn, *arrived):
        inner_bg[r], dn, inner_g[r] = run.call(
            functools.partial(ffn_backward, block),
            [sds((1, hidden), F32), sds((own, depth), F32), sds((depth, hidden), BF16 if r % 2 or (r == 2 and inner_sum.first()) else F32)],
            [df, outer_w[r], d[r], inner_w[r], n_t, dn, *arrived],
            flops=6 * own * depth * hidden,
            name="ffn_backward",
            us=2.6,
            scratch=[pltpu.VMEM((own, hidden), BF16)],
        )
        return dn

    outer_sum, inner_sum = Chunk(OUTER_ORDER, None), Chunk(INNER_ORDER, None)
    dn = feed_back(3, dn)
    zero, outer_sum.two = run.call(
        outer_even,
        [sds((hidden, depth), F32), sds((hidden, depth), BF16 if outer_sum.first() else F32)],
        [g[0], g[2], df, arrived],
        flops=4 * own * depth * hidden,
        name="outer_even",
        us=2.4,
    )
    run.supply(outer_sum, zero)
    three = swap(inner_g[3], "mp", 1)
    dn = feed_back(1, dn)
    one = swap(inner_g[1], "mp", 1)
    dn = feed_back(2, dn, three)
    inner_sum.two = inner_g[2]
    if inner_sum.first():
        run.add(inner_sum)
    dn = feed_back(0, dn, one)
    run.supply(inner_sum, inner_g[0])
    dr1, low, small1 = run.call(
        first_norm_back,
        [sds((own, depth), F32), sds((own, depth), BF16), sds((8, depth), F32)],
        [dn, hat, inverse, rows["g1"]],
        flops=40 * own * depth,
        name="first_norm_back",
        us=1.9,
    )

    low_far = swap(low, "mp", 2)
    low_due = run.transfer("x", own)
    run.clock += 1.5
    low_core = swap(low, "mp", 1)
    attention_sum = Chunk(QKV_ORDER, None)

    def attend_back(mine, near, far, *before):
        return run.call(
            functools.partial(attention_backward, heads, own, mine),
            [sds((3 * width, LENGTH), BF16), sds((4 * width, depth), F32), sds((8, 3 * width), F32)],
            [tokens, kv[mine], q[mine], o[mine], ob[mine], logs[mine], keys[mine], near, far, output_weight, table, *before],
            flops=2 * depth * width * 5 * LENGTH + 10 * LENGTH * LENGTH * 256 * heads,
            name="attention_backward",
            us=11.0,
            scratch=[pltpu.VMEM((LENGTH, depth), BF16), pltpu.VMEM((width, LENGTH), BF16)],
        )

    def token_part(dy, *before):
        return run.call(
            functools.partial(token_grad, own),
            [sds((own, depth), F32), sds((own, depth), BF16)],
            [dy, qkv_w, *before],
            flops=6 * own * depth * depth,
            name="token_grad",
            us=2.4,
        )

    dy, *sums = attend_back(1, low, low_core)
    own_keep, own_give = token_part(dy, dr1)
    own_core = swap(own_give, "mp", 1)
    run.clock = max(run.clock, low_due)
    low_far = after(low_far, *run.tokens)
    low_far_core = swap(low_far, "mp", 1)
    run.wait(low_far, own_core)
    run.service()
    run.clock += 1.5
    dy, gw, qkv_bg = attend_back(0, low_far, low_far_core, *sums)
    run.supply(attention_sum, gw)
    far_keep, far_give = token_part(dy)
    token_far = Exchange()
    token_far.begin(run, far_keep, far_give)
    (packed,) = run.call(
        pack_small,
        [sds((16, depth), F32)],
        [small2, small1, *inner_bg, qkv_bg],
        flops=1 << 20,
        name="pack_small",
        us=0.6,
    )
    small_sum = Everywhere(packed)
    run.add(small_sum)
    run.service(0)
    tokens_grad = own_keep + (own_core.astype(F32) + token_far.received.astype(F32))
    small = small_sum.own
    outer_weight_grad, inner_weight_grad = outer_sum.result, inner_sum.result
    output_weight_grad = attention_sum.result[3 * width :]
    qkv_weight_grad = jnp.transpose(attention_sum.result[: 3 * width].reshape(3, width, depth), (2, 0, 1))
    second_gain_grad, second_shift_grad, outer_bias_grad, output_bias_grad, first_gain_grad, first_shift_grad = (small[i] for i in range(6))
    inner_bias_grad = lax.dynamic_index_in_dim(small, 8 + me, 0, keepdims=False)
    qkv_bias_grad = lax.dynamic_index_in_dim(small, 12 + me, 0, keepdims=False)[: 3 * width].reshape(3, width)
    return (
        layer_out,
        tokens_grad,
        qkv_weight_grad,
        qkv_bias_grad,
        output_weight_grad,
        output_bias_grad,
        first_gain_grad,
        first_shift_grad,
        inner_weight_grad,
        inner_bias_grad,
        outer_weight_grad,
        outer_bias_grad,
        second_gain_grad,
        second_shift_grad,
    )


def solution(mesh):
    return jax.shard_map(
        on_device,
        mesh=mesh,
        in_specs=(
            P("dp", None),
            P(None, None, "mp"),
            P(None, "mp"),
            P("mp", None),
            P(),
            P(),
            P(),
            P(None, "mp"),
            P("mp"),
            P("mp", None),
            P(),
            P(),
            P(),
            P(("dp", "mp"), None),
            P("dp"),
        ),
        out_specs=(
            P(("dp", "mp"), None),
            P(("dp", "mp"), None),
            P(None, None, "mp"),
            P(None, "mp"),
            P("mp", None),
            P(),
            P(),
            P(),
            P(None, "mp"),
            P("mp"),
            P("mp", None),
            P(),
            P(),
            P(),
        ),
        check_vma=False,
    )
```

```python
import functools
import math

import jax
import jax.numpy as jnp
import numpy as np
from jax import lax
from jax.experimental import pallas as pl
from jax.experimental.pallas import tpu as pltpu
from jax.sharding import PartitionSpec as P

HD = 64
FORWARD_CHUNK = 512
BACKWARD_CHUNK = 256
HALF_DEPTH = HD // 2
LENGTH = 1024
EPSILON = 1e-12
NEGATIVE = -1e30
F32 = jnp.float32
BF16 = jnp.bfloat16
EXP_SCALE = HD ** (-0.5) * math.log2(math.e)

ERF_P = 0.52
ERF_C = (0.00514851, 0.23724269, 0.55266472, -0.39660497, 1.10267122, -0.61325166, 0.1121295)

NN = (((1,), (0,)), ((), ()))
NT = (((1,), (1,)), ((), ()))
TN = (((0,), (0,)), ((), ()))


def mm(a, b, dims):
    return lax.dot_general(a, b, dims, preferred_element_type=F32)


def rotary_tables():
    frequency = 10000.0 ** (-np.arange(HALF_DEPTH, dtype=np.float64) / HALF_DEPTH)
    angle = frequency[:, None] * np.arange(LENGTH, dtype=np.float64)[None, :]
    return np.concatenate([np.cos(angle), np.sin(angle)]).astype(np.float32)


ROW_US = 0.0334
HOP_US = 3.0


class Program:
    def __init__(self, scalars):
        self.scalars = scalars
        self.tokens = []
        self.clock = 0.0
        self.links = {"x": 0.0, "y": 0.0, "z": 0.0, "m": 0.0}
        self.chunks = []
        self.hold = False

    def wait(self, *values):
        self.tokens += values

    def call(self, body, outs, ins, grid=(), in_specs=None, out_specs=None, flops=0, name=None, vmem=16, us=5.0, scratch=()):
        scalars = after(self.scalars, *self.tokens)
        nbytes = sum(math.prod(a.shape) * a.dtype.itemsize for a in list(ins) + list(outs))
        whole = pl.BlockSpec(memory_space=pltpu.VMEM)
        result = pl.pallas_call(
            body,
            out_shape=outs,
            grid=grid,
            in_specs=[pl.BlockSpec(memory_space=pltpu.SMEM)] + (in_specs if in_specs is not None else [whole] * len(ins)),
            out_specs=out_specs if out_specs is not None else [whole] * len(outs),
            scratch_shapes=scratch,
            compiler_params=pltpu.CompilerParams(vmem_limit_bytes=vmem << 20),
            cost_estimate=pl.CostEstimate(flops=flops // COST_SCALE, bytes_accessed=nbytes // COST_SCALE, transcendentals=0),
            name=name,
        )(scalars, *ins)
        self.tokens = [result[0]]
        self.clock += us
        if not self.hold:
            self.service()
        return result

    def service(self, left=None):
        while True:
            waiting = [c for c in self.chunks if not c.finished]
            if not waiting or (left is not None and len(waiting) <= left):
                return
            chunk = min(waiting, key=lambda c: c.due)
            if chunk.due > self.clock and left is None:
                return
            if chunk.due == math.inf:
                return
            self.take(chunk)

    def take(self, chunk):
        self.clock = max(self.clock, chunk.due)
        if chunk.received is not None:
            chunk.received = after(chunk.received, *self.tokens)
        elif chunk.stage == "start" and hasattr(chunk, "own") and self.tokens:
            chunk.own = after(chunk.own, *self.tokens)
        made = chunk.step()
        self.tokens = [made]
        rows = math.prod(made.shape[:-1])
        self.clock += 0.6 + rows / 768 + (2.7 if chunk.stage == 4 else 1.6)
        if not chunk.finished or chunk.stage == "x":
            chunk.due = self.transfer(chunk.stage, rows)


    def transfer(self, stage, rows):
        us = rows * ROW_US
        uses = {"x": {"x": us}, 1: {"y": us}, 2: {"z": us}, 4: {"m": 2 * us, "z": us}, "all": {"y": us / 2, "z": us, "m": us}, "share": {"y": us / 2, "z": us, "m": us}}.get(stage, {})
        start = max([self.clock - 1] + [self.links[n] for n in uses])
        for n, t in uses.items():
            self.links[n] = start + t
        return start + max(list(uses.values()) + [us / 13]) + (HOP_US if uses else 1.0)

    def finish(self, chunk):
        while not chunk.finished:
            self.take(chunk)

    def add(self, chunk):
        chunk.due = self.clock
        self.chunks.append(chunk)
        self.service()

COST_SCALE = 16
OUTER_ORDER = (1, "x", 2, 4)
INNER_ORDER = (2, "x", 1, 4)
QKV_ORDER = (1, 2, 4)


def sds(shape, dtype):
    return jax.ShapeDtypeStruct(shape, dtype)


ANY = pl.BlockSpec(memory_space=pl.ANY)
VM = pl.BlockSpec(memory_space=pltpu.VMEM)


def rotate(v, cosine, sine):
    a, b = v[:HALF_DEPTH], v[HALF_DEPTH:]
    return jnp.concatenate([a * cosine - b * sine, b * cosine + a * sine], axis=0)


def unrotate(v, cosine, sine):
    a, b = v[:HALF_DEPTH], v[HALF_DEPTH:]
    return jnp.concatenate([a * cosine + b * sine, b * cosine - a * sine], axis=0)


def row_select(rows, columns):
    index = lax.broadcasted_iota(jnp.int32, (8, columns), 0)
    out = jnp.zeros((8, columns), F32)
    for i, r in enumerate(rows):
        if r is not None:
            out = jnp.where(index == i, r, out)
    return out


def augment(top, rows, total=2 * HD):
    columns = top.shape[1]
    tail = row_select(rows, columns)
    rest = jnp.zeros((total - HD - 8, columns), F32)
    return jnp.concatenate([top, tail, rest], axis=0)


def split3(v):
    high = v.astype(BF16).astype(F32)
    mid = (v - high).astype(BF16).astype(F32)
    return high, mid, v - high - mid


def mask_row(length):
    index = lax.broadcasted_iota(jnp.int32, (1, LENGTH), 1)
    return jnp.where(index < length, 0.0, NEGATIVE)


def place_of(sc, own, mine):
    me = lax.axis_index("mp")
    half, seq = me % 2, me // 2
    seq = seq if mine else 1 - seq
    return pl.multiple_of(half * own, own), pl.multiple_of((1 - half) * own, own), pl.multiple_of(seq * LENGTH, LENGTH), sc[seq]


def divide(total_ref, bit, slot, send_ref, keep_ref):
    n = total_ref.shape[0] // 2
    upper = (lax.axis_index("dp") & bit) > 0
    kept, sent = jnp.where(upper, n, 0), jnp.where(upper, 0, n)
    keep_ref[slot] = total_ref[pl.ds(pl.multiple_of(kept, n), n), :]
    send_ref[slot * n : (slot + 1) * n] = total_ref[pl.ds(pl.multiple_of(sent, n), n), :].astype(BF16)


def attention_forward(heads, own, mine, sc, tokens_ref, w_ref, b_ref, wo_ref, table_ref, kv_ref, q_ref, o_ref, ob_ref, l_ref, kn_ref, keep_ref, give_ref, k_ref, s_ref, x_ref, sem):
    near, far, start, length = place_of(sc, own, mine)
    width = heads * HD
    copy = pltpu.make_async_copy(tokens_ref.at[pl.ds(start, LENGTH), :], x_ref, sem)
    copy.start()
    bias = jnp.concatenate([jnp.transpose(jnp.broadcast_to(b_ref[i : i + 1], (128, width)))[:, :1] for i in range(3)])
    copy.wait()
    x = x_ref[...]
    kv = mm(w_ref[width:], x, NT) + bias[width:]
    q = mm(w_ref[:width], x, NT) + bias[:width]
    cosine, sine = table_ref[:HALF_DEPTH], table_ref[HALF_DEPTH:]
    mask = mask_row(length)
    one = jnp.ones((1, LENGTH), F32)
    kv_ref[width:] = kv[width:].astype(BF16)
    k_ref[...], s_ref[...] = kv[:width], q
    l_ref[...] = jnp.zeros(l_ref.shape, F32)

    def head(h, carry):
        at = pl.ds(pl.multiple_of(h * HD, HD), HD)
        v_at = pl.ds(pl.multiple_of(width + h * HD, HD), HD)
        k_rot = rotate(k_ref[at, :], cosine, sine)
        kv_ref[at, :] = k_rot.astype(BF16)
        kn_ref[h] = jnp.transpose(augment(k_rot, (one, one, one, mask))).astype(BF16)
        q_rot = rotate(s_ref[at, :], cosine, sine)
        q_ref[at, :] = q_rot.astype(BF16)
        keys = kn_ref[h]
        v_aug = jnp.concatenate([kv_ref[v_at, :], jnp.ones((16, LENGTH), BF16)], axis=0)
        for c in range(0, LENGTH, FORWARD_CHUNK):
            q_aug = augment(q_rot[:, c : c + FORWARD_CHUNK], (None, None, None, jnp.ones((1, FORWARD_CHUNK), F32)))
            s = mm(keys, q_aug.astype(BF16), NN)
            top = jnp.max(s, axis=0, keepdims=True)
            p = jnp.exp2((s - top) * EXP_SCALE).astype(BF16)
            o = mm(v_aug, p, NN)
            mass = o[HD : HD + 1]
            o = o[:HD] / mass
            o_ref[at, c : c + FORWARD_CHUNK] = o
            ob_ref[at, c : c + FORWARD_CHUNK] = o.astype(BF16)
            l_ref[pl.ds(h, 1), c : c + FORWARD_CHUNK] = top + jnp.log2(mass) / EXP_SCALE
        return carry

    lax.fori_loop(0, heads, head, 0)
    keep_ref[...] = mm(ob_ref[:, pl.ds(near, own)], wo_ref[...], TN)
    give_ref[...] = mm(ob_ref[:, pl.ds(far, own)], wo_ref[...], TN).astype(give_ref.dtype)


def attention_backward(heads, own, mine, bit, sc, tokens_ref, kv_ref, q_ref, o_ref, ob_ref, l_ref, kn_ref, near_ref, far_ref, wo_ref, table_ref, *refs):
    before, outs, (da_ref, do_ref, x_ref, sum_ref, sem) = refs[: 0 if mine else 8], refs[0 if mine else 8 : -5], refs[-5:]
    dy_ref, gb_ref = outs[:2]
    near, far, start, length = place_of(sc, own, mine)
    copy = pltpu.make_async_copy(tokens_ref.at[pl.ds(start, LENGTH), :], x_ref, sem)
    copy.start()
    width = heads * HD
    da_ref[pl.ds(near, own), :] = near_ref[...]
    da_ref[pl.ds(far, own), :] = far_ref[...]
    do_ref[...] = mm(wo_ref[...], da_ref[...], NT).astype(BF16)
    cosine, sine = table_ref[:HALF_DEPTH], table_ref[HALF_DEPTH:]
    mask = mask_row(length)
    one = jnp.ones((1, LENGTH), F32)
    zeros = jnp.zeros((HD - 8, LENGTH), F32)
    tail_k = jnp.concatenate([row_select((one, one, one, mask), LENGTH), zeros], axis=0).astype(BF16)
    tail_v = jnp.concatenate([row_select((one, one, one), LENGTH), zeros], axis=0).astype(BF16)
    scale = HD ** (-0.5)
    def head(h, carry):
        at = pl.ds(pl.multiple_of(h * HD, HD), HD)
        k_at = pl.ds(pl.multiple_of(width + h * HD, HD), HD)
        v_at = pl.ds(pl.multiple_of(2 * width + h * HD, HD), HD)
        d_out = do_ref[at, :].astype(F32)
        delta = jnp.sum(d_out * o_ref[at, :], axis=0, keepdims=True)
        qn = jnp.transpose(augment(q_ref[at, :].astype(F32), (*split3(-l_ref[pl.ds(h, 1), :]), one))).astype(BF16)
        dn = jnp.transpose(augment(d_out, split3(-delta))).astype(BF16)
        k_aug = jnp.concatenate([kv_ref[at, :], tail_k], axis=0)
        v_aug = jnp.concatenate([kv_ref[k_at, :], tail_v], axis=0)
        keys = kn_ref[h]
        dk = dv = None
        dq = []
        for c in range(0, LENGTH, BACKWARD_CHUNK):
            p = jnp.exp2(mm(qn[c : c + BACKWARD_CHUNK], k_aug, NN) * EXP_SCALE)
            dp = mm(dn[c : c + BACKWARD_CHUNK], v_aug, NN)
            ds = (p * dp).astype(BF16)
            dq.append(mm(ds, keys, NN))
            dk_part = mm(q_ref[at, c : c + BACKWARD_CHUNK], ds, NN)
            dv_part = mm(do_ref[at, c : c + BACKWARD_CHUNK], p.astype(BF16), NN)
            dk = dk_part if dk is None else dk + dk_part
            dv = dv_part if dv is None else dv + dv_part
        dq_t = jnp.transpose(jnp.concatenate(dq, axis=0))[:HD]
        dy_ref[at, :] = (unrotate(dq_t, cosine, sine) * scale).astype(BF16)
        dy_ref[k_at, :] = (unrotate(dk, cosine, sine) * scale).astype(BF16)
        dy_ref[v_at, :] = dv.astype(BF16)
        return carry

    lax.fori_loop(0, heads, head, 0)
    copy.wait()
    gw = mm(dy_ref[...], x_ref[...], NN)
    go = mm(ob_ref[...], da_ref[...], NN)
    gb = mm(jnp.ones((8, LENGTH), BF16), dy_ref[...], NT)
    if before:
        gw, go, gb = gw + before[0][: 3 * width], go + before[0][3 * width :], gb + before[1][...]
    gb_ref[...] = gb
    total_ref = outs[2] if mine else sum_ref
    total_ref[: 3 * width] = gw
    total_ref[3 * width :] = go
    if not mine:
        divide(sum_ref, bit, 0, outs[2], outs[3])
        pack_small(outs[4], outs[2], gb, *before[2:])


def norm_stats(v):
    centered = v - jnp.mean(v, axis=-1, keepdims=True)
    inverse = lax.rsqrt(jnp.mean(centered * centered, axis=-1, keepdims=True) + EPSILON)
    return centered * inverse, inverse


def norm_back(grad, hat, inverse, gain):
    scaled = grad * gain
    return inverse * (
        scaled
        - jnp.mean(scaled, axis=-1, keepdims=True)
        - hat * jnp.mean(scaled * hat, axis=-1, keepdims=True)
    )


def row_blocks(rows, step, block=128):
    def body(i, carry):
        step(pl.ds(pl.multiple_of(i * block, block), block))
        return carry

    lax.fori_loop(0, rows // block, body, 0)


def project_norm(sc, tokens_ref, keep_ref, core_ref, far_ref, bias_ref, gain_ref, shift_ref, n_ref, nt_ref, hat_ref, inv_ref, x_ref, sem):
    rows = hat_ref.shape[0]
    copy = pltpu.make_async_copy(tokens_ref.at[pl.ds(pl.multiple_of(lax.axis_index("mp") * rows, rows), rows), :], x_ref, sem)
    copy.start()
    copy.wait()

    def step(at):
        total = x_ref[at, :].astype(F32) + bias_ref[...]
        total = total + (keep_ref[at, :] + core_ref[at, :].astype(F32) + far_ref[at, :].astype(F32))
        hat, inverse = norm_stats(total)
        n = hat * gain_ref[...] + shift_ref[...]
        hat_ref[at, :] = hat
        inv_ref[at, :] = inverse
        n_ref[at, :] = n.astype(BF16)
        nt_ref[:, at] = jnp.transpose(n).astype(BF16)

    row_blocks(rows, step)


def gelu_parts(z):
    e = jnp.exp2(z * z * (-0.5 * math.log2(math.e)))
    t = 1.0 / (1.0 + jnp.abs(z) * (ERF_P / math.sqrt(2.0)))
    poly = jnp.full_like(z, 0.5 * ERF_C[-1])
    for c in ERF_C[-2::-1]:
        poly = poly * t + 0.5 * c
    tail = poly * e
    phi = jnp.where(z >= 0, 1.0 - tail, tail)
    return z * phi, phi + z * e * (1.0 / math.sqrt(2.0 * math.pi))


def ffn_forward(block, sc, n_ref, wi_ref, bi_ref, wo_ref, *refs):
    g_ref, d_ref, f_ref = refs[-3:]

    def step(at):
        z = mm(n_ref[at, :], wi_ref[...], NN) + bi_ref[...]
        g, d = gelu_parts(z)
        g = g.astype(BF16)
        g_ref[at, :] = g
        d_ref[at, :] = d
        part = mm(g, wo_ref[...], NN)
        f_ref[at, :] = part + refs[0][at, :] if len(refs) > 3 else part

    row_blocks(n_ref.shape[0], step, block)


def add_sums(small_ref, at, values):
    @pl.when(at.start == 0)
    def _():
        small_ref[...] = jnp.zeros(small_ref.shape, F32)

    small_ref[...] += row_select([jnp.sum(v, axis=0, keepdims=True) for v in values], small_ref.shape[1])


def second_norm(sc, f_ref, hat_ref, cot_ref, g1_ref, s1_ref, ob_ref, g2_ref, s2_ref, out_ref, dr_ref, df_ref, small_ref):
    rows = f_ref.shape[0]

    def step(at):
        first = hat_ref[at, :] * g1_ref[...] + s1_ref[...]
        hat, inverse = norm_stats(first + f_ref[at, :] + ob_ref[...])
        out_ref[at, :] = (hat * g2_ref[...] + s2_ref[...]).astype(BF16)
        me = lax.axis_index("mp")
        place = lax.broadcasted_iota(jnp.int32, (at.size, 1), 0) + at.start + (me % 2) * rows
        grad = jnp.where(place < sc[me // 2], cot_ref[at, :].astype(F32), 0.0)
        dr = norm_back(grad, hat, inverse, g2_ref[...])
        dr_ref[at, :] = dr
        df_ref[at, :] = dr.astype(BF16)
        add_sums(small_ref, at, (grad * hat, grad, dr))

    row_blocks(rows, step)


def outer_odd(sc, one_ref, three_ref, df_ref, *out_refs):
    count = out_refs[0].shape[0] // 2
    df = df_ref[...]
    for j, g_ref in enumerate((one_ref, three_ref)):
        total = mm(g_ref[...], df, TN).astype(BF16)
        for k, out_ref in enumerate(out_refs):
            out_ref[j * count : (j + 1) * count] = total[k * count : (k + 1) * count]


def outer_even(bit, sc, zero_ref, two_ref, df_ref, arrived_ref, send_ref, keep_ref, sum_ref):
    count = sum_ref.shape[0]
    df = df_ref[...]
    for j, g_ref in enumerate((zero_ref, two_ref)):
        sum_ref[...] = mm(g_ref[...], df, TN) + arrived_ref[j * count : (j + 1) * count].astype(F32)
        divide(sum_ref, bit, j, send_ref, keep_ref)


def ffn_backward(slot, bit, sc, df_ref, wo_ref, d_ref, wi_ref, nt_ref, dn_in_ref, *refs):
    arrived, outs, (dz_ref, sum_ref) = refs[: {0: 2}.get(slot, 1 - slot % 2)], refs[{0: 2}.get(slot, 1 - slot % 2) : -2], refs[-2:]
    gb_ref, dn_ref = outs[:2]
    dz = (mm(df_ref[...], wo_ref[...], NT) * d_ref[...]).astype(BF16)
    dz_ref[...] = dz
    dn_ref[...] = dn_in_ref[...] + mm(dz, wi_ref[...], NT)
    gb_ref[...] = jnp.sum(dz_ref[...].astype(F32), axis=0, keepdims=True)
    total = mm(nt_ref[...], dz_ref[...], NN)
    if slot % 2 == 0:
        total = total + arrived[0][...].astype(F32)
    if slot:
        outs[2][...] = total.astype(outs[2].dtype)
    else:
        sum_ref[...] = total
        divide(sum_ref, bit, 0, outs[2], outs[3])
        divide(arrived[1], bit, 1, outs[2], outs[3])


def first_norm_back(sc, dn_ref, hat_ref, inv_ref, gain_ref, dr_ref, low_ref, small_ref):
    def step(at):
        grad, hat = dn_ref[at, :], hat_ref[at, :]
        dr = norm_back(grad, hat, inv_ref[at, :], gain_ref[...])
        dr_ref[at, :] = dr
        low_ref[at, :] = dr.astype(BF16)
        add_sums(small_ref, at, (dr, grad * hat, grad))

    row_blocks(dn_ref.shape[0], step)


def token_grad(own, sc, dy_ref, w_ref, *refs):
    before, (keep_ref, give_ref) = refs[:-2], refs[-2:]
    near, far, _, _ = place_of(sc, own, True)
    total = mm(dy_ref[:, pl.ds(near, own)], w_ref[...], TN)
    for ref in before:
        total = total + ref[...]
    keep_ref[...] = total
    give_ref[...] = mm(dy_ref[:, pl.ds(far, own)], w_ref[...], TN).astype(BF16)


def pack_small(out_ref, send_ref, qkv, small2, small1, *inner):
    me = lax.axis_index("mp")
    out_ref[...] = jnp.zeros(out_ref.shape, F32)
    out_ref[0:3] = small2[0:3]
    out_ref[3:6] = small1[0:3]
    for r in range(4):
        out_ref[pl.ds(8 + (me ^ r), 1), :] = inner[r][...]
    out_ref[pl.ds(12 + me, 1), pl.ds(0, qkv.shape[1])] = qkv[0:1]
    count = out_ref.shape[0]
    for i, part in enumerate(split3(out_ref[...])):
        at = send_ref.shape[0] - (3 - i) * count
        send_ref[at : at + count] = part.astype(BF16)


def swap(v, axis, bit):
    size = lax.axis_size(axis)
    return lax.ppermute(v, axis, [(i, i ^ bit) for i in range(size)])


def after(v, *others):
    return lax.optimization_barrier((v, *others))[0]


def dp_upper(bit):
    return (lax.axis_index("dp") & bit) > 0


def parts3(v):
    high = lax.reduce_precision(v, 8, 7)
    mid = lax.reduce_precision(v - high, 8, 7)
    return high, mid, v - high - mid


class Chunk:
    def __init__(self, order):
        size = lax.axis_size("dp")
        bits = [1 << i for i in range(size.bit_length() - 1)]
        self.order = [b for b in order if b == "x" or b in bits]
        self.order += [b for b in bits if b not in order]
        self.last = [b for b in self.order if b != "x"][-1]
        self.back = [b for b in self.order[::-1] if b not in ("x", self.last)]
        self.bit = self.order[0]
        self.received = self.total = self.result = self.rider = None
        self.stage = "start"
        self.finished = False

    def begin(self, run, send, keep, rider=None):
        self.stage = self.order.pop(0)
        self.received = self.exchange(send)
        self.total, self.rider = keep, rider
        self.rows = math.prod(keep.shape[:-1])
        run.clock += 1.6
        self.due = run.transfer(self.stage, self.received.shape[0])
        run.chunks.append(self)

    def exchange(self, send):
        self.rows = send.shape[0]
        if self.rider is not None:
            send = jnp.concatenate([send] + [v.astype(BF16) for v in parts3(self.rider)])
        return swap(send, "mp" if self.stage == "x" else "dp", 2 if self.stage == "x" else self.stage)

    def merged(self):
        arrived = self.received[: self.rows].astype(F32)
        if self.rider is not None:
            parts = self.received[self.rows :].astype(F32).reshape(3, *self.rider.shape)
            self.rider = self.rider + (parts[0] + parts[1] + parts[2])
        return self.total + arrived.reshape(self.total.shape)

    def step(self):
        if self.order:
            total = self.merged()
            self.stage = self.order.pop(0)
            if self.stage == "x":
                send, self.total = total[1].astype(BF16), total[:1]
            elif self.stage == self.last:
                send = total.reshape(-1, total.shape[-1]).astype(BF16)
                self.total = send.astype(F32).reshape(total.shape)
            else:
                upper = dp_upper(self.stage)
                n = total.shape[1] // 2
                low, high = total[:, :n], total[:, n:]
                send = jnp.where(upper, low, high).astype(BF16).reshape(-1, total.shape[-1])
                self.total = jnp.where(upper, high, low)
            self.received = self.exchange(send)
            return send
        if self.back:
            if self.total is not None:
                self.held = self.merged()[0].astype(BF16)
                self.ridden, self.rider, self.total = self.rider, None, None
            else:
                self.held = self.joined()
            self.stage = self.back.pop(0)
            self.received = swap(self.held, "dp", self.stage)
            return self.held
        self.result = self.joined()
        self.finished = True
        return self.result

    def joined(self):
        pair = (self.held, self.received)
        return jnp.where(dp_upper(self.stage), jnp.concatenate(pair[::-1]), jnp.concatenate(pair))


class Everywhere:
    def __init__(self, v):
        self.own, self.received = v, None
        self.stages = [1, 2]
        self.finished = False
        self.stage = "start"

    def step(self):
        if self.received is not None:
            self.own = self.own + self.received
        if self.stages:
            bit = self.stages.pop(0)
            self.stage = {1: "core", 2: "x"}[bit]
            self.received = swap(self.own, "mp", bit)
        else:
            self.finished, self.stage = True, "end"
        return self.own


class Exchange:
    def __init__(self):
        self.finished = False
        self.stage = "core"

    def begin(self, run, keep, give):
        self.keep = keep
        self.received = swap(give, "mp", 1)
        run.chunks.append(self)
        self.due = run.transfer("core", give.shape[0] * give.dtype.itemsize // 2)

    def step(self):
        made = (self.keep + self.received.astype(F32)).astype(BF16)
        self.received = swap(made, "mp", 2)
        self.stage = "x"
        self.finished = True
        return made


class Gather:
    def __init__(self, own, bits):
        self.own, self.bits = own, list(bits)
        self.received = None
        self.stage = "start"
        self.finished = False

    def step(self):
        if self.stage == "start":
            self.held = self.own
            for bit in self.bits[::-1]:
                self.held = half_of(self.held, bit)
            self.stage, self.received = "x", swap(self.held, "mp", 2)
            return self.held
        if self.stage == "x":
            self.held = self.received
        else:
            self.held = join_halves(self.held, self.received, self.stage)
        if self.bits:
            self.stage = self.bits.pop(0)
            self.received = swap(self.held, "dp", self.stage)
            return self.held
        self.two, self.stage = self.held, "core"
        self.three = swap(self.two, "mp", 1)
        self.finished = True
        return self.two


def half_of(v, bit):
    n = v.shape[0] // 2
    return lax.dynamic_slice_in_dim(v, jnp.where(dp_upper(bit), n, 0), n, 0)


def join_halves(mine, other, bit):
    return jnp.where(dp_upper(bit), jnp.concatenate([other, mine]), jnp.concatenate([mine, other]))


def on_device(
    tokens,
    qkv_weight,
    qkv_bias,
    output_weight,
    output_bias,
    first_gain,
    first_shift,
    inner_weight,
    inner_bias,
    outer_weight,
    outer_bias,
    second_gain,
    second_shift,
    cotangent,
    seq_lengths,
):
    depth = tokens.shape[1]
    own = cotangent.shape[0]
    width = qkv_weight.shape[2]
    heads = width // HD
    hidden = inner_weight.shape[1]
    me = lax.axis_index("mp")
    table = jnp.asarray(rotary_tables())
    run = Program(seq_lengths)

    bias_one = swap(inner_bias, "mp", 1)
    inner_w, outer_w = [inner_weight, None, None, None], [outer_weight, None, None, None]
    inner_w[1], outer_w[1] = swap(inner_weight, "mp", 1), swap(outer_weight, "mp", 1)
    inner_gather, outer_gather = Gather(inner_weight, (1, 2)), Gather(outer_weight, (2, 1))
    run.add(inner_gather)
    run.add(outer_gather)
    qkv_w = jnp.transpose(qkv_weight, (1, 2, 0)).reshape(3 * width, depth)
    rows = {n: v.reshape(1, -1) for n, v in dict(ob=output_bias, g1=first_gain, s1=first_shift, b2=outer_bias, g2=second_gain, s2=second_shift).items()}

    kv, q, o, ob, logs, keys = ([None] * 2 for _ in range(6))

    def attend(mine):
        kv[mine], q[mine], o[mine], ob[mine], logs[mine], keys[mine], keep, give = run.call(
            functools.partial(attention_forward, heads, own, mine),
            [
                sds((2 * width, LENGTH), BF16),
                sds((width, LENGTH), BF16),
                sds((width, LENGTH), F32),
                sds((width, LENGTH), BF16),
                sds((8, LENGTH), F32),
                sds((heads, LENGTH, 2 * HD), BF16),
                sds((own, depth), F32),
                sds((own, depth), BF16 if mine else F32),
            ],
            [tokens, qkv_w, qkv_bias, output_weight, table],
            in_specs=[ANY] + [VM] * 4,
            flops=2 * depth * width * 4 * LENGTH + 4 * LENGTH * LENGTH * 256 * heads,
            name="attention_forward",
            us=8.7,
            scratch=[pltpu.VMEM((width, LENGTH), F32)] * 2 + [pltpu.VMEM((LENGTH, depth), BF16), pltpu.SemaphoreType.DMA],
        )
        return keep, give

    run.wait(inner_w[1], outer_w[1], bias_one)
    run.clock += 3.0
    far_sum = Exchange()
    run.hold = True
    keep, give = attend(0)
    run.hold = False
    for gather in (inner_gather, outer_gather):
        gather.received = after(gather.received, *run.tokens)
    bias_pair = swap(jnp.stack([after(inner_bias, kv[0]), bias_one]), "mp", 2)
    bias_slots = [inner_bias.reshape(1, -1), bias_one.reshape(1, -1), bias_pair[:1], bias_pair[1:]]
    far_sum.begin(run, keep, after(give, inner_gather.received, outer_gather.received))
    run.finish(far_sum)
    far = far_sum.received
    run.clock = max(run.clock, inner_gather.due, outer_gather.due)
    run.service()
    run.clock = max(run.clock, inner_gather.due, outer_gather.due)
    run.service()
    keep, give = attend(1)
    core = swap(give, "mp", 1)
    run.clock = max(run.clock, far_sum.due)
    run.wait(far, core, bias_pair)
    run.service()
    n_low, n_t, hat, inverse = run.call(
        project_norm,
        [sds((own, depth), BF16), sds((depth, own), BF16), sds((own, depth), F32), sds((own, 1), F32)],
        [tokens, keep, core, far, rows["ob"], rows["g1"], rows["s1"]],
        in_specs=[ANY] + [VM] * 6,
        scratch=[pltpu.VMEM((own, depth), BF16), pltpu.SemaphoreType.DMA],
        flops=40 * own * depth,
        name="project_norm",
        us=2.0,
    )

    block = 512
    g, d = [None] * 4, [None] * 4

    def feed(r, *f):
        g[r], d[r], f = run.call(
            functools.partial(ffn_forward, block),
            [sds((own, hidden), BF16), sds((own, hidden), F32), sds((own, depth), F32)],
            [n_low, inner_w[r], bias_slots[r], outer_w[r], *f],
            flops=4 * own * depth * hidden,
            name="ffn_forward",
            us=3.0,
        )
        return f

    f = feed(0)
    f = feed(1, f)
    for gather in (inner_gather, outer_gather):
        run.finish(gather)
    inner_w[2:], outer_w[2:] = ([v.two, v.three] for v in (inner_gather, outer_gather))
    f = feed(2, f)
    f = feed(3, f)
    layer_out, dr2, df, small2 = run.call(
        second_norm,
        [sds((own, depth), BF16), sds((own, depth), F32), sds((own, depth), BF16), sds((8, depth), F32)],
        [f, hat, cotangent, rows["g1"], rows["s1"], rows["b2"], rows["g2"], rows["s2"]],
        flops=40 * own * depth,
        name="second_norm",
        us=2.7,
    )
    odd = run.call(
        outer_odd,
        [sds((2 * hidden, depth), BF16)],
        [g[1], g[3], df],
        flops=4 * own * depth * hidden,
        name="outer_odd",
        us=1.9,
    )
    arrived = swap(odd[0], "mp", 1)
    inner_g, inner_bg = [None] * 4, [None] * 4
    dn = dr2

    def feed_back(r, dn, *arrived):
        divided = [sds((depth, hidden), BF16), sds((2, depth // 2, hidden), F32)]
        inner_bg[r], dn, *inner_g[r] = run.call(
            functools.partial(ffn_backward, r, inner_sum.bit),
            [sds((1, hidden), F32), sds((own, depth), F32)] + (divided if r == 0 else [sds((depth, hidden), F32 if r == 2 else BF16)]),
            [df, outer_w[r], d[r], inner_w[r], n_t, dn, *arrived],
            flops=6 * own * depth * hidden,
            name="ffn_backward",
            us=2.6 if r else 3.0,
            scratch=[pltpu.VMEM((own, hidden), BF16), pltpu.VMEM((depth, hidden), F32)],
        )
        return dn

    outer_sum, inner_sum, attention_sum = Chunk(OUTER_ORDER), Chunk(INNER_ORDER), Chunk(QKV_ORDER)
    dn = feed_back(3, dn)
    send, kept = run.call(
        functools.partial(outer_even, outer_sum.bit),
        [sds((hidden, depth), BF16), sds((2, hidden // 2, depth), F32)],
        [g[0], g[2], df, arrived],
        flops=4 * own * depth * hidden,
        name="outer_even",
        us=2.4,
        scratch=[pltpu.VMEM((hidden, depth), F32)],
    )
    outer_sum.begin(run, send, kept)
    three = swap(inner_g[3][0], "mp", 1)
    dn = feed_back(1, dn)
    one = swap(inner_g[1][0], "mp", 1)
    dn = feed_back(2, dn, three)
    dn = feed_back(0, dn, one, inner_g[2][0])
    dr1, low, small1 = run.call(
        first_norm_back,
        [sds((own, depth), F32), sds((own, depth), BF16), sds((8, depth), F32)],
        [dn, hat, inverse, rows["g1"]],
        flops=40 * own * depth,
        name="first_norm_back",
        us=1.9,
    )

    low_far = swap(low, "mp", 2)
    low_due = run.transfer("x", own)
    run.clock += 1.5
    inner_sum.begin(run, *inner_g[0])
    low_core = swap(low, "mp", 1)

    def attend_back(mine, near, far, *before):
        divided = [sds((2 * width + 48, depth), BF16), sds((1, 2 * width, depth), F32), sds((16, depth), F32)]
        return run.call(
            functools.partial(attention_backward, heads, own, mine, attention_sum.bit),
            [sds((3 * width, LENGTH), BF16), sds((8, 3 * width), F32)] + ([sds((4 * width, depth), F32)] if mine else divided),
            [tokens, kv[mine], q[mine], o[mine], ob[mine], logs[mine], keys[mine], near, far, output_weight, table, *before],
            in_specs=[ANY] + [VM] * (10 + len(before)),
            flops=2 * depth * width * 5 * LENGTH + 10 * LENGTH * LENGTH * 256 * heads,
            name="attention_backward",
            us=11.0 if mine else 12.0,
            scratch=[pltpu.VMEM((LENGTH, depth), BF16), pltpu.VMEM((width, LENGTH), BF16), pltpu.VMEM((LENGTH, depth), BF16), pltpu.VMEM((4 * width, depth), F32), pltpu.SemaphoreType.DMA],
        )

    def token_part(dy, *before):
        return run.call(
            functools.partial(token_grad, own),
            [sds((own, depth), F32), sds((own, depth), BF16)],
            [dy, qkv_w, *before],
            flops=6 * own * depth * depth,
            name="token_grad",
            us=2.4,
        )

    run.hold = True
    dy, bias_sum, weight_sum = attend_back(1, low, low_core)
    own_keep, own_give = token_part(dy, dr1)
    own_core = swap(own_give, "mp", 1)
    run.hold = False
    run.take(outer_sum)
    run.clock = max(run.clock, low_due)
    low_far = after(low_far, *run.tokens)
    low_far_core = swap(low_far, "mp", 1)
    run.tokens = [low_far]
    run.wait(own_core)
    run.service()
    run.clock += 1.5
    dy, _, send, kept, packed = attend_back(0, low_far, low_far_core, weight_sum, bias_sum, small2, small1, *inner_bg)
    attention_sum.begin(run, send, kept, packed)
    far_keep, far_give = token_part(dy)
    token_far = Exchange()
    token_far.begin(run, far_keep, far_give)
    while not hasattr(attention_sum, "ridden"):
        run.take(min([c for c in run.chunks if not c.finished], key=lambda c: c.due))
    small_sum = Everywhere(attention_sum.ridden)
    run.add(small_sum)
    run.service(0)
    tokens_grad = own_keep + (own_core.astype(F32) + token_far.received.astype(F32))
    small = small_sum.own
    outer_weight_grad, inner_weight_grad = outer_sum.result.astype(F32), inner_sum.result.astype(F32)
    output_weight_grad = attention_sum.result[3 * width :].astype(F32)
    qkv_weight_grad = jnp.transpose(attention_sum.result[: 3 * width].astype(F32).reshape(3, width, depth), (2, 0, 1))
    second_gain_grad, second_shift_grad, outer_bias_grad, output_bias_grad, first_gain_grad, first_shift_grad = (small[i] for i in range(6))
    inner_bias_grad = lax.dynamic_index_in_dim(small, 8 + me, 0, keepdims=False)
    qkv_bias_grad = lax.dynamic_index_in_dim(small, 12 + me, 0, keepdims=False)[: 3 * width].reshape(3, width)
    return (
        layer_out,
        tokens_grad,
        qkv_weight_grad,
        qkv_bias_grad,
        output_weight_grad,
        output_bias_grad,
        first_gain_grad,
        first_shift_grad,
        inner_weight_grad,
        inner_bias_grad,
        outer_weight_grad,
        outer_bias_grad,
        second_gain_grad,
        second_shift_grad,
    )


def solution(mesh):
    return jax.shard_map(
        on_device,
        mesh=mesh,
        in_specs=(
            P("dp", None),
            P(None, None, "mp"),
            P(None, "mp"),
            P("mp", None),
            P(),
            P(),
            P(),
            P(None, "mp"),
            P("mp"),
            P("mp", None),
            P(),
            P(),
            P(),
            P(("dp", "mp"), None),
            P("dp"),
        ),
        out_specs=(
            P(("dp", "mp"), None),
            P(("dp", "mp"), None),
            P(None, None, "mp"),
            P(None, "mp"),
            P("mp", None),
            P(),
            P(),
            P(),
            P(None, "mp"),
            P("mp"),
            P("mp", None),
            P(),
            P(),
            P(),
        ),
        check_vma=False,
    )
```

```python
import functools
import math

import jax
import jax.numpy as jnp
import numpy as np
from jax import lax
from jax.experimental import pallas as pl
from jax.experimental.pallas import tpu as pltpu
from jax.sharding import PartitionSpec as P

HD = 64
FORWARD_CHUNK = 512
BACKWARD_CHUNK = 256
HALF_DEPTH = HD // 2
LENGTH = 1024
EPSILON = 1e-12
NEGATIVE = -1e30
F32 = jnp.float32
BF16 = jnp.bfloat16
EXP_SCALE = HD ** (-0.5) * math.log2(math.e)

ERF_P = 0.52
ERF_C = (0.00514851, 0.23724269, 0.55266472, -0.39660497, 1.10267122, -0.61325166, 0.1121295)

NN = (((1,), (0,)), ((), ()))
NT = (((1,), (1,)), ((), ()))
TN = (((0,), (0,)), ((), ()))


def mm(a, b, dims):
    return lax.dot_general(a, b, dims, preferred_element_type=F32)


def rotary_tables():
    frequency = 10000.0 ** (-np.arange(HALF_DEPTH, dtype=np.float64) / HALF_DEPTH)
    angle = frequency[:, None] * np.arange(LENGTH, dtype=np.float64)[None, :]
    return np.concatenate([np.cos(angle), np.sin(angle)]).astype(np.float32)


ROW_US = 0.038
HOP_US = 4.0


class Program:
    def __init__(self, scalars):
        self.scalars = scalars
        self.tokens = []
        self.clock = 0.0
        self.links = {"x": 0.0, "y": 0.0, "z": 0.0, "m": 0.0}
        self.chunks = []
        self.hold = False

    def wait(self, *values):
        self.tokens += values

    def call(self, body, outs, ins, grid=(), in_specs=None, out_specs=None, flops=0, name=None, vmem=16, us=5.0, scratch=()):
        scalars = after(self.scalars, *self.tokens)
        nbytes = sum(math.prod(a.shape) * a.dtype.itemsize for a in list(ins) + list(outs))
        whole = pl.BlockSpec(memory_space=pltpu.VMEM)
        result = pl.pallas_call(
            body,
            out_shape=outs,
            grid=grid,
            in_specs=[pl.BlockSpec(memory_space=pltpu.SMEM)] + (in_specs if in_specs is not None else [whole] * len(ins)),
            out_specs=out_specs if out_specs is not None else [whole] * len(outs),
            scratch_shapes=scratch,
            compiler_params=pltpu.CompilerParams(vmem_limit_bytes=vmem << 20),
            cost_estimate=pl.CostEstimate(flops=flops // COST_SCALE, bytes_accessed=nbytes // COST_SCALE, transcendentals=0),
            name=name,
        )(scalars, *ins)
        self.tokens = [result[0]]
        self.clock += us
        if not self.hold:
            self.service()
        return result

    def service(self, left=None):
        while True:
            waiting = [c for c in self.chunks if not c.finished]
            if not waiting or (left is not None and len(waiting) <= left):
                return
            chunk = min(waiting, key=lambda c: c.due)
            if chunk.due > self.clock and left is None:
                return
            if chunk.due == math.inf:
                return
            self.take(chunk)

    def take(self, chunk):
        self.clock = max(self.clock, chunk.due)
        if chunk.received is not None:
            chunk.received = after(chunk.received, *self.tokens)
        elif chunk.stage == "start" and hasattr(chunk, "own") and self.tokens:
            chunk.own = after(chunk.own, *self.tokens)
        made = chunk.step()
        self.tokens = [made]
        rows = math.prod(made.shape[:-1])
        self.clock += 0.6 + rows / 768 + (2.7 if chunk.stage == 4 else 1.6)
        if not chunk.finished or chunk.stage == "x":
            chunk.due = self.transfer(chunk.stage, rows)


    def transfer(self, stage, rows):
        us = rows * ROW_US
        uses = {"x": {"x": us}, 1: {"y": us}, 2: {"z": us}, 4: {"m": 2.0 * us, "z": 1.0 * us}, "all": {"y": us / 2, "z": us, "m": us}, "share": {"y": us / 2, "z": us, "m": us}}.get(stage, {})
        start = max([self.clock - 1] + [self.links[n] for n in uses])
        for n, t in uses.items():
            self.links[n] = start + t
        return start + max(list(uses.values()) + [us / 13]) + (HOP_US if uses else 1.0)

    def finish(self, chunk):
        while not chunk.finished:
            self.take(chunk)

    def add(self, chunk):
        chunk.due = self.clock
        self.chunks.append(chunk)
        self.service()

COST_SCALE = 16
OUTER_ORDER = (1, 'x', 2, 4)
INNER_ORDER = (2, 'x', 1, 4)
QKV_ORDER = (1, 2, 4)


def sds(shape, dtype):
    return jax.ShapeDtypeStruct(shape, dtype)


ANY = pl.BlockSpec(memory_space=pltpu.HBM)
VM = pl.BlockSpec(memory_space=pltpu.VMEM)


def rotate(v, cosine, sine):
    a, b = v[:HALF_DEPTH], v[HALF_DEPTH:]
    return jnp.concatenate([a * cosine - b * sine, b * cosine + a * sine], axis=0)


def unrotate(v, cosine, sine):
    a, b = v[:HALF_DEPTH], v[HALF_DEPTH:]
    return jnp.concatenate([a * cosine + b * sine, b * cosine - a * sine], axis=0)


def row_select(rows, columns):
    index = lax.broadcasted_iota(jnp.int32, (8, columns), 0)
    out = jnp.zeros((8, columns), F32)
    for i, r in enumerate(rows):
        if r is not None:
            out = jnp.where(index == i, r, out)
    return out


def augment(top, rows, total=2 * HD):
    columns = top.shape[1]
    tail = row_select(rows, columns)
    rest = jnp.zeros((total - HD - 8, columns), F32)
    return jnp.concatenate([top, tail, rest], axis=0)


def split3(v):
    high = v.astype(BF16).astype(F32)
    mid = (v - high).astype(BF16).astype(F32)
    return high, mid, v - high - mid


def mask_row(length):
    index = lax.broadcasted_iota(jnp.int32, (1, LENGTH), 1)
    return jnp.where(index < length, 0.0, NEGATIVE)


def place_of(sc, own, mine):
    me = lax.axis_index("mp")
    half, seq = me % 2, me // 2
    seq = seq if mine else 1 - seq
    return pl.multiple_of(half * own, own), pl.multiple_of((1 - half) * own, own), pl.multiple_of(seq * LENGTH, LENGTH), sc[seq]


def divide(total_ref, bit, slot, send_ref, keep_ref):
    n = total_ref.shape[0] // 2
    upper = (lax.axis_index("dp") & bit) > 0
    kept, sent = jnp.where(upper, n, 0), jnp.where(upper, 0, n)
    keep_ref[slot] = total_ref[pl.ds(pl.multiple_of(kept, n), n), :]
    send_ref[slot * n : (slot + 1) * n] = total_ref[pl.ds(pl.multiple_of(sent, n), n), :].astype(BF16)


def attention_forward(heads, own, mine, sc, tokens_ref, w_ref, b_ref, wo_ref, angles_ref, kv_ref, q_ref, o_ref, ob_ref, l_ref, kn_ref, keep_ref, give_ref, k_ref, s_ref, x_ref, table_ref, sem, table_sem):
    near, far, start, length = place_of(sc, own, mine)
    width = heads * HD
    copy = pltpu.make_async_copy(tokens_ref.at[pl.ds(start, LENGTH), :], x_ref, sem)
    copy.start()
    table_copy = pltpu.make_async_copy(angles_ref, table_ref, table_sem)
    table_copy.start()
    bias = jnp.concatenate([jnp.transpose(jnp.broadcast_to(b_ref[i : i + 1], (128, width)))[:, :1] for i in range(3)])
    copy.wait()
    x = x_ref[...]
    kv = mm(w_ref[width:], x, NT) + bias[width:]
    q = mm(w_ref[:width], x, NT) + bias[:width]
    table_copy.wait()
    cosine, sine = table_ref[:HALF_DEPTH], table_ref[HALF_DEPTH:]
    mask = mask_row(length)
    one = jnp.ones((1, LENGTH), F32)
    kv_ref[width:] = kv[width:].astype(BF16)
    k_ref[...], s_ref[...] = kv[:width], q
    l_ref[...] = jnp.zeros(l_ref.shape, F32)

    def head(h, carry):
        at = pl.ds(pl.multiple_of(h * HD, HD), HD)
        v_at = pl.ds(pl.multiple_of(width + h * HD, HD), HD)
        k_rot = rotate(k_ref[at, :], cosine, sine)
        kv_ref[at, :] = k_rot.astype(BF16)
        kn_ref[h] = jnp.transpose(augment(k_rot, (one, one, one, mask))).astype(BF16)
        q_rot = rotate(s_ref[at, :], cosine, sine)
        q_ref[at, :] = q_rot.astype(BF16)
        keys = kn_ref[h]
        v_aug = jnp.concatenate([kv_ref[v_at, :], jnp.ones((16, LENGTH), BF16)], axis=0)
        for c in range(0, LENGTH, FORWARD_CHUNK):
            q_aug = augment(q_rot[:, c : c + FORWARD_CHUNK], (None, None, None, jnp.ones((1, FORWARD_CHUNK), F32)))
            s = mm(keys, q_aug.astype(BF16), NN)
            top = jnp.max(s, axis=0, keepdims=True)
            p = jnp.exp2((s - top) * EXP_SCALE).astype(BF16)
            o = mm(v_aug, p, NN)
            mass = o[HD : HD + 1]
            o = o[:HD] / mass
            o_ref[at, c : c + FORWARD_CHUNK] = o
            ob_ref[at, c : c + FORWARD_CHUNK] = o.astype(BF16)
            l_ref[pl.ds(h, 1), c : c + FORWARD_CHUNK] = top + jnp.log2(mass) / EXP_SCALE
        return carry

    lax.fori_loop(0, heads, head, 0)
    keep_ref[...] = mm(ob_ref[:, pl.ds(near, own)], wo_ref[...], TN)
    give_ref[...] = mm(ob_ref[:, pl.ds(far, own)], wo_ref[...], TN).astype(give_ref.dtype)


def attention_backward(heads, own, mine, bit, sc, tokens_ref, kv_ref, q_ref, o_ref, ob_ref, l_ref, kn_ref, near_ref, far_ref, wo_ref, table_ref, *refs):
    before, outs, (da_ref, do_ref, x_ref, sum_ref, sem) = refs[: 0 if mine else 8], refs[0 if mine else 8 : -5], refs[-5:]
    dy_ref, gb_ref = outs[:2]
    near, far, start, length = place_of(sc, own, mine)
    copy = pltpu.make_async_copy(tokens_ref.at[pl.ds(start, LENGTH), :], x_ref, sem)
    copy.start()
    width = heads * HD
    da_ref[pl.ds(near, own), :] = near_ref[...]
    da_ref[pl.ds(far, own), :] = far_ref[...]
    do_ref[...] = mm(wo_ref[...], da_ref[...], NT).astype(BF16)
    cosine, sine = table_ref[:HALF_DEPTH], table_ref[HALF_DEPTH:]
    mask = mask_row(length)
    one = jnp.ones((1, LENGTH), F32)
    zeros = jnp.zeros((HD - 8, LENGTH), F32)
    tail_k = jnp.concatenate([row_select((one, one, one, mask), LENGTH), zeros], axis=0).astype(BF16)
    tail_v = jnp.concatenate([row_select((one, one, one), LENGTH), zeros], axis=0).astype(BF16)
    scale = HD ** (-0.5)
    def head(h, carry):
        at = pl.ds(pl.multiple_of(h * HD, HD), HD)
        k_at = pl.ds(pl.multiple_of(width + h * HD, HD), HD)
        v_at = pl.ds(pl.multiple_of(2 * width + h * HD, HD), HD)
        d_out = do_ref[at, :].astype(F32)
        delta = jnp.sum(d_out * o_ref[at, :], axis=0, keepdims=True)
        qn = jnp.transpose(augment(q_ref[at, :].astype(F32), (*split3(-l_ref[pl.ds(h, 1), :]), one))).astype(BF16)
        dn = jnp.transpose(augment(d_out, split3(-delta))).astype(BF16)
        k_aug = jnp.concatenate([kv_ref[at, :], tail_k], axis=0)
        v_aug = jnp.concatenate([kv_ref[k_at, :], tail_v], axis=0)
        keys = kn_ref[h]
        dk = dv = None
        dq = []
        for c in range(0, LENGTH, BACKWARD_CHUNK):
            p = jnp.exp2(mm(qn[c : c + BACKWARD_CHUNK], k_aug, NN) * EXP_SCALE)
            dp = mm(dn[c : c + BACKWARD_CHUNK], v_aug, NN)
            ds = (p * dp).astype(BF16)
            dq.append(mm(ds, keys, NN))
            dk_part = mm(q_ref[at, c : c + BACKWARD_CHUNK], ds, NN)
            dv_part = mm(do_ref[at, c : c + BACKWARD_CHUNK], p.astype(BF16), NN)
            dk = dk_part if dk is None else dk + dk_part
            dv = dv_part if dv is None else dv + dv_part
        dq_t = jnp.transpose(jnp.concatenate(dq, axis=0))[:HD]
        dy_ref[at, :] = (unrotate(dq_t, cosine, sine) * scale).astype(BF16)
        dy_ref[k_at, :] = (unrotate(dk, cosine, sine) * scale).astype(BF16)
        dy_ref[v_at, :] = dv.astype(BF16)
        return carry

    lax.fori_loop(0, heads, head, 0)
    copy.wait()
    gw = mm(dy_ref[...], x_ref[...], NN)
    go = mm(ob_ref[...], da_ref[...], NN)
    gb = mm(jnp.ones((8, LENGTH), BF16), dy_ref[...], NT)
    if before:
        gw, go, gb = gw + before[0][: 3 * width], go + before[0][3 * width :], gb + before[1][...]
    gb_ref[...] = gb
    total_ref = outs[2] if mine else sum_ref
    total_ref[: 3 * width] = gw
    total_ref[3 * width :] = go
    if not mine:
        divide(sum_ref, bit, 0, outs[2], outs[3])
        pack_small(outs[4], outs[2], gb, *before[2:])


def norm_stats(v):
    centered = v - jnp.mean(v, axis=-1, keepdims=True)
    inverse = lax.rsqrt(jnp.mean(centered * centered, axis=-1, keepdims=True) + EPSILON)
    return centered * inverse, inverse


def norm_back(grad, hat, inverse, gain):
    scaled = grad * gain
    return inverse * (
        scaled
        - jnp.mean(scaled, axis=-1, keepdims=True)
        - hat * jnp.mean(scaled * hat, axis=-1, keepdims=True)
    )


def row_blocks(rows, step, block=128):
    def body(i, carry):
        step(pl.ds(pl.multiple_of(i * block, block), block))
        return carry

    lax.fori_loop(0, rows // block, body, 0)


def project_norm(sc, tokens_ref, keep_ref, core_ref, far_ref, bias_ref, gain_ref, shift_ref, n_ref, nt_ref, hat_ref, inv_ref, x_ref, sem):
    rows = hat_ref.shape[0]
    copy = pltpu.make_async_copy(tokens_ref.at[pl.ds(pl.multiple_of(lax.axis_index("mp") * rows, rows), rows), :], x_ref, sem)
    copy.start()
    copy.wait()

    def step(at):
        total = x_ref[at, :].astype(F32) + bias_ref[...]
        total = total + (keep_ref[at, :] + core_ref[at, :].astype(F32) + far_ref[at, :].astype(F32))
        hat, inverse = norm_stats(total)
        n = hat * gain_ref[...] + shift_ref[...]
        hat_ref[at, :] = hat
        inv_ref[at, :] = inverse
        n_ref[at, :] = n.astype(BF16)
        nt_ref[:, at] = jnp.transpose(n).astype(BF16)

    row_blocks(rows, step)


def gelu_parts(z):
    e = jnp.exp2(z * z * (-0.5 * math.log2(math.e)))
    t = 1.0 / (1.0 + jnp.abs(z) * (ERF_P / math.sqrt(2.0)))
    poly = jnp.full_like(z, 0.5 * ERF_C[-1])
    for c in ERF_C[-2::-1]:
        poly = poly * t + 0.5 * c
    tail = poly * e
    phi = jnp.where(z >= 0, 1.0 - tail, tail)
    return z * phi, phi + z * e * (1.0 / math.sqrt(2.0 * math.pi))


def ffn_forward(block, sc, n_ref, wi_ref, bi_ref, wo_ref, *refs):
    g_ref, d_ref, f_ref = refs[-3:]

    def step(at):
        z = mm(n_ref[at, :], wi_ref[...], NN) + bi_ref[...]
        g, d = gelu_parts(z)
        g = g.astype(BF16)
        g_ref[at, :] = g
        d_ref[at, :] = d
        part = mm(g, wo_ref[...], NN)
        f_ref[at, :] = part + refs[0][at, :] if len(refs) > 3 else part

    row_blocks(n_ref.shape[0], step, block)


def add_sums(small_ref, at, values):
    @pl.when(at.start == 0)
    def _():
        small_ref[...] = jnp.zeros(small_ref.shape, F32)

    small_ref[...] += row_select([jnp.sum(v, axis=0, keepdims=True) for v in values], small_ref.shape[1])


def second_norm(sc, f_ref, hat_ref, cot_ref, g1_ref, s1_ref, ob_ref, g2_ref, s2_ref, out_ref, dr_ref, df_ref, small_ref):
    rows = f_ref.shape[0]

    def step(at):
        first = hat_ref[at, :] * g1_ref[...] + s1_ref[...]
        hat, inverse = norm_stats(first + f_ref[at, :] + ob_ref[...])
        out_ref[at, :] = (hat * g2_ref[...] + s2_ref[...]).astype(BF16)
        me = lax.axis_index("mp")
        place = lax.broadcasted_iota(jnp.int32, (at.size, 1), 0) + at.start + (me % 2) * rows
        grad = jnp.where(place < sc[me // 2], cot_ref[at, :].astype(F32), 0.0)
        dr = norm_back(grad, hat, inverse, g2_ref[...])
        dr_ref[at, :] = dr
        df_ref[at, :] = dr.astype(BF16)
        add_sums(small_ref, at, (grad * hat, grad, dr))

    row_blocks(rows, step)


def outer_odd(sc, one_ref, three_ref, df_ref, *out_refs):
    count = out_refs[0].shape[0] // 2
    df = df_ref[...]
    for j, g_ref in enumerate((one_ref, three_ref)):
        total = mm(g_ref[...], df, TN).astype(BF16)
        for k, out_ref in enumerate(out_refs):
            out_ref[j * count : (j + 1) * count] = total[k * count : (k + 1) * count]


def outer_even(bit, sc, zero_ref, two_ref, df_ref, arrived_ref, send_ref, keep_ref, sum_ref):
    count = sum_ref.shape[0]
    df = df_ref[...]
    for j, g_ref in enumerate((zero_ref, two_ref)):
        sum_ref[...] = mm(g_ref[...], df, TN) + arrived_ref[j * count : (j + 1) * count].astype(F32)
        divide(sum_ref, bit, j, send_ref, keep_ref)


def ffn_backward(slot, bit, sc, df_ref, wo_ref, d_ref, wi_ref, nt_ref, dn_in_ref, *refs):
    arrived, outs, (dz_ref, sum_ref) = refs[: {0: 2}.get(slot, 1 - slot % 2)], refs[{0: 2}.get(slot, 1 - slot % 2) : -2], refs[-2:]
    gb_ref, dn_ref = outs[:2]
    dz = (mm(df_ref[...], wo_ref[...], NT) * d_ref[...]).astype(BF16)
    dz_ref[...] = dz
    dn_ref[...] = dn_in_ref[...] + mm(dz, wi_ref[...], NT)
    gb_ref[...] = jnp.sum(dz_ref[...].astype(F32), axis=0, keepdims=True)
    total = mm(nt_ref[...], dz_ref[...], NN)
    if slot % 2 == 0:
        total = total + arrived[0][...].astype(F32)
    if slot:
        outs[2][...] = total.astype(outs[2].dtype)
    else:
        sum_ref[...] = total
        divide(sum_ref, bit, 0, outs[2], outs[3])
        divide(arrived[1], bit, 1, outs[2], outs[3])


def first_norm_back(sc, dn_ref, hat_ref, inv_ref, gain_ref, dr_ref, low_ref, small_ref):
    def step(at):
        grad, hat = dn_ref[at, :], hat_ref[at, :]
        dr = norm_back(grad, hat, inv_ref[at, :], gain_ref[...])
        dr_ref[at, :] = dr
        low_ref[at, :] = dr.astype(BF16)
        add_sums(small_ref, at, (dr, grad * hat, grad))

    row_blocks(dn_ref.shape[0], step)


def token_grad(own, sc, dy_ref, w_ref, *refs):
    before, (keep_ref, give_ref) = refs[:-2], refs[-2:]
    near, far, _, _ = place_of(sc, own, True)
    total = mm(dy_ref[:, pl.ds(near, own)], w_ref[...], TN)
    for ref in before:
        total = total + ref[...]
    keep_ref[...] = total
    give_ref[...] = mm(dy_ref[:, pl.ds(far, own)], w_ref[...], TN).astype(BF16)


def pack_small(out_ref, send_ref, qkv, small2, small1, *inner):
    me = lax.axis_index("mp")
    out_ref[...] = jnp.zeros(out_ref.shape, F32)
    out_ref[0:3] = small2[0:3]
    out_ref[3:6] = small1[0:3]
    for r in range(4):
        out_ref[pl.ds(8 + (me ^ r), 1), :] = inner[r][...]
    out_ref[pl.ds(12 + me, 1), pl.ds(0, qkv.shape[1])] = qkv[0:1]
    count = out_ref.shape[0]
    for i, part in enumerate(split3(out_ref[...])):
        at = send_ref.shape[0] - (3 - i) * count
        send_ref[at : at + count] = part.astype(BF16)


def swap(v, axis, bit):
    size = lax.axis_size(axis)
    return lax.ppermute(v, axis, [(i, i ^ bit) for i in range(size)])


def after(v, *others):
    return lax.optimization_barrier((v, *others))[0]


def dp_upper(bit):
    return (lax.axis_index("dp") & bit) > 0


def parts3(v):
    high = lax.reduce_precision(v, 8, 7)
    mid = lax.reduce_precision(v - high, 8, 7)
    return high, mid, v - high - mid


class Chunk:
    def __init__(self, order, cut=None):
        size = lax.axis_size("dp")
        bits = [1 << i for i in range(size.bit_length() - 1)]
        self.order = [b for b in order if b == "x" or b in bits]
        self.order += [b for b in bits if b not in order]
        self.last = [b for b in self.order if b != "x"][-1]
        self.back = [b for b in self.order[::-1] if b not in ("x", self.last)]
        self.bit = self.order[0]
        self.received = self.total = self.result = self.rider = None
        self.cut = cut
        self.stage = "start"
        self.finished = False

    def begin(self, run, send, keep, rider=None):
        self.stage = self.order.pop(0)
        self.received = self.exchange(send)
        self.total, self.rider = keep, rider
        self.rows = math.prod(keep.shape[:-1])
        run.clock += 1.6
        self.due = run.transfer(self.stage, self.received.shape[0])
        run.chunks.append(self)

    def exchange(self, send):
        self.rows = send.shape[0]
        if self.rider is not None:
            send = jnp.concatenate([send] + [v.astype(BF16) for v in parts3(self.rider)])
        return swap(send, "mp" if self.stage == "x" else "dp", 2 if self.stage == "x" else self.stage)

    def merged(self):
        arrived = self.received[: self.rows].astype(F32)
        if self.rider is not None:
            parts = self.received[self.rows :].astype(F32).reshape(3, *self.rider.shape)
            self.rider = self.rider + (parts[0] + parts[1] + parts[2])
        return self.total + arrived.reshape(self.total.shape)

    def step(self):
        if self.order:
            total = self.merged()
            self.stage = self.order.pop(0)
            if self.stage == "x":
                send, self.total = total[1].astype(BF16), total[:1]
            elif self.stage == self.last:
                send = total.reshape(-1, total.shape[-1]).astype(BF16)
                self.total = send.astype(F32).reshape(total.shape)
            else:
                upper = dp_upper(self.stage)
                n = total.shape[1] // 2
                low, high = total[:, :n], total[:, n:]
                send = jnp.where(upper, low, high).astype(BF16).reshape(-1, total.shape[-1])
                self.total = jnp.where(upper, high, low)
            self.received = self.exchange(send)
            return send
        if self.back:
            if self.total is not None:
                self.held = self.merged()[0].astype(BF16)
                self.ridden, self.rider, self.total = self.rider, None, None
            else:
                self.held = self.joined()
            self.stage = self.back.pop(0)
            self.received = swap(self.held, "dp", self.stage)
            return self.held
        self.finished = True
        if self.cut is None:
            self.result = self.joined().astype(F32)
            return self.result
        upper = dp_upper(self.stage)
        first, second = jnp.where(upper, self.received, self.held), jnp.where(upper, self.held, self.received)
        rest = self.cut - first.shape[0]
        self.result = jnp.concatenate([first, second[:rest]]).astype(F32), second[rest:].astype(F32)
        return self.result[0]

    def joined(self):
        pair = (self.held, self.received)
        return jnp.where(dp_upper(self.stage), jnp.concatenate(pair[::-1]), jnp.concatenate(pair))


class Everywhere:
    def __init__(self, v):
        self.own, self.received = v, None
        self.stages = [1, 2]
        self.finished = False
        self.stage = "start"

    def step(self):
        if self.received is not None:
            self.own = self.own + self.received
        if self.stages:
            bit = self.stages.pop(0)
            self.stage = {1: "core", 2: "x"}[bit]
            self.received = swap(self.own, "mp", bit)
        else:
            self.finished, self.stage = True, "end"
        return self.own


class Exchange:
    def __init__(self):
        self.finished = False
        self.stage = "core"

    def begin(self, run, keep, give):
        self.keep = keep
        self.received = swap(give, "mp", 1)
        run.chunks.append(self)
        self.due = run.transfer("core", give.shape[0] * give.dtype.itemsize // 2)

    def step(self):
        made = (self.keep + self.received.astype(F32)).astype(BF16)
        self.received = swap(made, "mp", 2)
        self.stage = "x"
        self.finished = True
        return made


class Gather:
    def __init__(self, own, bits):
        self.own, self.bits = own, list(bits)
        self.received = None
        self.stage = "start"
        self.finished = False

    def step(self):
        if self.stage == "start":
            self.held = self.own
            for bit in self.bits[::-1]:
                self.held = half_of(self.held, bit)
            self.stage, self.received = "x", swap(self.held, "mp", 2)
            return self.held
        if self.stage == "x":
            self.held = self.received
        else:
            self.held = join_halves(self.held, self.received, self.stage)
        if self.bits:
            self.stage = self.bits.pop(0)
            self.received = swap(self.held, "dp", self.stage)
            return self.held
        self.two, self.stage = self.held, "core"
        self.three = swap(self.two, "mp", 1)
        self.finished = True
        return self.two


def half_of(v, bit):
    n = v.shape[0] // 2
    return lax.dynamic_slice_in_dim(v, jnp.where(dp_upper(bit), n, 0), n, 0)


def join_halves(mine, other, bit):
    return jnp.where(dp_upper(bit), jnp.concatenate([other, mine]), jnp.concatenate([mine, other]))


def on_device(
    tokens,
    qkv_weight,
    qkv_bias,
    output_weight,
    output_bias,
    first_gain,
    first_shift,
    inner_weight,
    inner_bias,
    outer_weight,
    outer_bias,
    second_gain,
    second_shift,
    cotangent,
    seq_lengths,
):
    depth = tokens.shape[1]
    own = cotangent.shape[0]
    width = qkv_weight.shape[2]
    heads = width // HD
    hidden = inner_weight.shape[1]
    me = lax.axis_index("mp")
    table = jnp.asarray(rotary_tables())
    run = Program(seq_lengths)

    bias_one = swap(inner_bias, "mp", 1)
    inner_w, outer_w = [inner_weight, None, None, None], [outer_weight, None, None, None]
    inner_w[1], outer_w[1] = swap(inner_weight, "mp", 1), swap(outer_weight, "mp", 1)
    inner_gather, outer_gather = Gather(inner_weight, (1, 2)), Gather(outer_weight, (2, 1))
    run.add(inner_gather)
    run.add(outer_gather)
    qkv_w = jnp.transpose(qkv_weight, (1, 2, 0)).reshape(3 * width, depth)
    rows = {n: v.reshape(1, -1) for n, v in dict(ob=output_bias, g1=first_gain, s1=first_shift, b2=outer_bias, g2=second_gain, s2=second_shift).items()}

    kv, q, o, ob, logs, keys = ([None] * 2 for _ in range(6))

    def attend(mine):
        kv[mine], q[mine], o[mine], ob[mine], logs[mine], keys[mine], keep, give = run.call(
            functools.partial(attention_forward, heads, own, mine),
            [
                sds((2 * width, LENGTH), BF16),
                sds((width, LENGTH), BF16),
                sds((width, LENGTH), F32),
                sds((width, LENGTH), BF16),
                sds((8, LENGTH), F32),
                sds((heads, LENGTH, 2 * HD), BF16),
                sds((own, depth), F32),
                sds((own, depth), BF16 if mine else F32),
            ],
            [tokens, qkv_w, qkv_bias, output_weight, table],
            in_specs=[ANY, VM, VM, VM, ANY],
            flops=2 * depth * width * 4 * LENGTH + 4 * LENGTH * LENGTH * 256 * heads,
            name="attention_forward",
            us=8.7,
            scratch=[pltpu.VMEM((width, LENGTH), F32)] * 2 + [pltpu.VMEM((LENGTH, depth), BF16), pltpu.VMEM((HD, LENGTH), F32), pltpu.SemaphoreType.DMA, pltpu.SemaphoreType.DMA],
        )
        return keep, give

    run.wait(inner_w[1], outer_w[1], bias_one)
    run.clock += 3.0
    far_sum = Exchange()
    run.hold = True
    keep, give = attend(0)
    run.hold = False
    for gather in (inner_gather, outer_gather):
        gather.received = after(gather.received, *run.tokens)
    bias_pair = swap(jnp.stack([after(inner_bias, kv[0]), bias_one]), "mp", 2)
    bias_slots = [inner_bias.reshape(1, -1), bias_one.reshape(1, -1), bias_pair[:1], bias_pair[1:]]
    far_sum.begin(run, keep, after(give, inner_gather.received, outer_gather.received))
    run.finish(far_sum)
    far = far_sum.received
    run.clock = max(run.clock, inner_gather.due, outer_gather.due)
    run.service()
    run.hold = True
    keep, give = attend(1)
    run.hold = False
    for gather in (inner_gather, outer_gather):
        gather.received = after(gather.received, *run.tokens)
    core = swap(after(give, inner_gather.received, outer_gather.received), "mp", 1)
    run.clock = max(run.clock, inner_gather.due, outer_gather.due)
    run.service()
    run.clock = max(run.clock, far_sum.due)
    run.wait(far, core)
    run.service()
    n_low, n_t, hat, inverse = run.call(
        project_norm,
        [sds((own, depth), BF16), sds((depth, own), BF16), sds((own, depth), F32), sds((own, 1), F32)],
        [tokens, keep, core, far, rows["ob"], rows["g1"], rows["s1"]],
        in_specs=[ANY] + [VM] * 6,
        scratch=[pltpu.VMEM((own, depth), BF16), pltpu.SemaphoreType.DMA],
        flops=40 * own * depth,
        name="project_norm",
        us=2.0,
    )

    block = 512
    g, d = [None] * 4, [None] * 4

    def feed(r, *f):
        g[r], d[r], f = run.call(
            functools.partial(ffn_forward, block),
            [sds((own, hidden), BF16), sds((own, hidden), F32), sds((own, depth), F32)],
            [n_low, inner_w[r], bias_slots[r], outer_w[r], *f],
            flops=4 * own * depth * hidden,
            name="ffn_forward",
            us=3.0,
        )
        return f

    run.hold = True
    f = feed(0)
    run.wait(bias_pair)
    f = feed(1, f)
    run.hold = False
    for gather in (inner_gather, outer_gather):
        run.finish(gather)
    inner_w[2:], outer_w[2:] = ([v.two, v.three] for v in (inner_gather, outer_gather))
    f = feed(2, f)
    f = feed(3, f)
    layer_out, dr2, df, small2 = run.call(
        second_norm,
        [sds((own, depth), BF16), sds((own, depth), F32), sds((own, depth), BF16), sds((8, depth), F32)],
        [f, hat, cotangent, rows["g1"], rows["s1"], rows["b2"], rows["g2"], rows["s2"]],
        flops=40 * own * depth,
        name="second_norm",
        us=2.7,
    )
    odd = run.call(
        outer_odd,
        [sds((2 * hidden, depth), BF16)],
        [g[1], g[3], df],
        flops=4 * own * depth * hidden,
        name="outer_odd",
        us=1.9,
    )
    arrived = swap(odd[0], "mp", 1)
    inner_g, inner_bg = [None] * 4, [None] * 4
    dn = dr2

    def feed_back(r, dn, *arrived):
        divided = [sds((depth, hidden), BF16), sds((2, depth // 2, hidden), F32)]
        inner_bg[r], dn, *inner_g[r] = run.call(
            functools.partial(ffn_backward, r, inner_sum.bit),
            [sds((1, hidden), F32), sds((own, depth), F32)] + (divided if r == 0 else [sds((depth, hidden), F32 if r == 2 else BF16)]),
            [df, outer_w[r], d[r], inner_w[r], n_t, dn, *arrived],
            flops=6 * own * depth * hidden,
            name="ffn_backward",
            us=2.6 if r else 3.0,
            scratch=[pltpu.VMEM((own, hidden), BF16), pltpu.VMEM((depth, hidden), F32)],
        )
        return dn

    outer_sum, inner_sum, attention_sum = Chunk(OUTER_ORDER), Chunk(INNER_ORDER), Chunk(QKV_ORDER, 3 * width)
    dn = feed_back(3, dn)
    send, kept = run.call(
        functools.partial(outer_even, outer_sum.bit),
        [sds((hidden, depth), BF16), sds((2, hidden // 2, depth), F32)],
        [g[0], g[2], df, arrived],
        flops=4 * own * depth * hidden,
        name="outer_even",
        us=2.4,
        scratch=[pltpu.VMEM((hidden, depth), F32)],
    )
    outer_sum.begin(run, send, kept)
    three = swap(inner_g[3][0], "mp", 1)
    dn = feed_back(1, dn)
    one = swap(inner_g[1][0], "mp", 1)
    dn = feed_back(2, dn, three)
    dn = feed_back(0, dn, one, inner_g[2][0])
    dr1, low, small1 = run.call(
        first_norm_back,
        [sds((own, depth), F32), sds((own, depth), BF16), sds((8, depth), F32)],
        [dn, hat, inverse, rows["g1"]],
        flops=40 * own * depth,
        name="first_norm_back",
        us=1.9,
    )

    low_far = swap(low, "mp", 2)
    low_due = run.transfer("x", own)
    run.clock += 1.5
    inner_sum.begin(run, *inner_g[0])
    low_core = swap(low, "mp", 1)

    def attend_back(mine, near, far, *before):
        divided = [sds((2 * width + 48, depth), BF16), sds((1, 2 * width, depth), F32), sds((16, depth), F32)]
        return run.call(
            functools.partial(attention_backward, heads, own, mine, attention_sum.bit),
            [sds((3 * width, LENGTH), BF16), sds((8, 3 * width), F32)] + ([sds((4 * width, depth), F32)] if mine else divided),
            [tokens, kv[mine], q[mine], o[mine], ob[mine], logs[mine], keys[mine], near, far, output_weight, table, *before],
            in_specs=[ANY] + [VM] * (10 + len(before)),
            flops=2 * depth * width * 5 * LENGTH + 10 * LENGTH * LENGTH * 256 * heads,
            name="attention_backward",
            us=11.0 if mine else 12.0,
            scratch=[pltpu.VMEM((LENGTH, depth), BF16), pltpu.VMEM((width, LENGTH), BF16), pltpu.VMEM((LENGTH, depth), BF16), pltpu.VMEM((4 * width, depth), F32), pltpu.SemaphoreType.DMA],
        )

    def token_part(dy, *before):
        return run.call(
            functools.partial(token_grad, own),
            [sds((own, depth), F32), sds((own, depth), BF16)],
            [dy, qkv_w, *before],
            flops=6 * own * depth * depth,
            name="token_grad",
            us=2.4,
        )

    run.hold = True
    dy, bias_sum, weight_sum = attend_back(1, low, low_core)
    own_keep, own_give = token_part(dy, dr1)
    own_core = swap(own_give, "mp", 1)
    run.hold = False
    run.take(outer_sum)
    run.clock = max(run.clock, low_due)
    low_far = after(low_far, *run.tokens)
    low_far_core = swap(low_far, "mp", 1)
    run.tokens = [low_far]
    run.wait(own_core)
    run.service()
    run.clock += 1.5
    dy, _, send, kept, packed = attend_back(0, low_far, low_far_core, weight_sum, bias_sum, small2, small1, *inner_bg)
    attention_sum.begin(run, send, kept, packed)
    far_keep, far_give = token_part(dy)
    token_far = Exchange()
    token_far.begin(run, far_keep, far_give)
    while not hasattr(attention_sum, "ridden"):
        run.take(min([c for c in run.chunks if not c.finished], key=lambda c: c.due))
    small_sum = Everywhere(attention_sum.ridden)
    run.add(small_sum)
    run.service(0)
    tokens_grad = own_keep + (own_core.astype(F32) + token_far.received.astype(F32))
    small = small_sum.own
    outer_weight_grad, inner_weight_grad = outer_sum.result, inner_sum.result
    qkv_weight_grad, output_weight_grad = attention_sum.result
    qkv_weight_grad = jnp.transpose(qkv_weight_grad.reshape(3, width, depth), (2, 0, 1))
    second_gain_grad, second_shift_grad, outer_bias_grad, output_bias_grad, first_gain_grad, first_shift_grad = (small[i] for i in range(6))
    inner_bias_grad = lax.dynamic_index_in_dim(small, 8 + me, 0, keepdims=False)
    qkv_bias_grad = lax.dynamic_index_in_dim(small, 12 + me, 0, keepdims=False)[: 3 * width].reshape(3, width)
    return (
        layer_out,
        tokens_grad,
        qkv_weight_grad,
        qkv_bias_grad,
        output_weight_grad,
        output_bias_grad,
        first_gain_grad,
        first_shift_grad,
        inner_weight_grad,
        inner_bias_grad,
        outer_weight_grad,
        outer_bias_grad,
        second_gain_grad,
        second_shift_grad,
    )


def solution(mesh):
    return jax.shard_map(
        on_device,
        mesh=mesh,
        in_specs=(
            P("dp", None),
            P(None, None, "mp"),
            P(None, "mp"),
            P("mp", None),
            P(),
            P(),
            P(),
            P(None, "mp"),
            P("mp"),
            P("mp", None),
            P(),
            P(),
            P(),
            P(("dp", "mp"), None),
            P("dp"),
        ),
        out_specs=(
            P(("dp", "mp"), None),
            P(("dp", "mp"), None),
            P(None, None, "mp"),
            P(None, "mp"),
            P("mp", None),
            P(),
            P(),
            P(),
            P(None, "mp"),
            P("mp"),
            P("mp", None),
            P(),
            P(),
            P(),
        ),
        check_vma=False,
    )
```

```python
import functools
import math

import jax
import jax.numpy as jnp
import numpy as np
from jax import lax
from jax.experimental import pallas as pl
from jax.experimental.pallas import tpu as pltpu
from jax.sharding import PartitionSpec as P

HD = 64
FORWARD_CHUNK = 512
BACKWARD_CHUNK = 256
HALF_DEPTH = HD // 2
LENGTH = 1024
EPSILON = 1e-12
NEGATIVE = -1e30
F32 = jnp.float32
BF16 = jnp.bfloat16
EXP_SCALE = HD ** (-0.5) * math.log2(math.e)

ERF_P = 0.52
ERF_C = (0.00514851, 0.23724269, 0.55266472, -0.39660497, 1.10267122, -0.61325166, 0.1121295)

NN = (((1,), (0,)), ((), ()))
NT = (((1,), (1,)), ((), ()))
TN = (((0,), (0,)), ((), ()))


def mm(a, b, dims):
    return lax.dot_general(a, b, dims, preferred_element_type=F32)


def rotary_tables():
    frequency = 10000.0 ** (-np.arange(HALF_DEPTH, dtype=np.float64) / HALF_DEPTH)
    angle = frequency[:, None] * np.arange(LENGTH, dtype=np.float64)[None, :]
    return np.concatenate([np.cos(angle), np.sin(angle)]).astype(np.float32)


ROW_US = 0.038
HOP_US = 4.0


class Program:
    def __init__(self, scalars):
        self.scalars = scalars
        self.tokens = []
        self.clock = 0.0
        self.links = {"x": 0.0, "y": 0.0, "z": 0.0, "m": 0.0}
        self.chunks = []
        self.hold = False

    def wait(self, *values):
        self.tokens += values

    def call(self, body, outs, ins, grid=(), in_specs=None, out_specs=None, flops=0, name=None, vmem=16, us=5.0, scratch=()):
        scalars = after(self.scalars, *self.tokens)
        nbytes = sum(math.prod(a.shape) * a.dtype.itemsize for a in list(ins) + list(outs))
        whole = pl.BlockSpec(memory_space=pltpu.VMEM)
        result = pl.pallas_call(
            body,
            out_shape=outs,
            grid=grid,
            in_specs=[pl.BlockSpec(memory_space=pltpu.SMEM)] + (in_specs if in_specs is not None else [whole] * len(ins)),
            out_specs=out_specs if out_specs is not None else [whole] * len(outs),
            scratch_shapes=scratch,
            compiler_params=pltpu.CompilerParams(vmem_limit_bytes=vmem << 20),
            cost_estimate=pl.CostEstimate(flops=flops // COST_SCALE, bytes_accessed=nbytes // COST_SCALE, transcendentals=0),
            name=name,
        )(scalars, *ins)
        self.tokens = [result[0]]
        self.clock += us
        if not self.hold:
            self.service()
        return result

    def service(self, left=None):
        while True:
            waiting = [c for c in self.chunks if not c.finished]
            if not waiting or (left is not None and len(waiting) <= left):
                return
            chunk = min(waiting, key=lambda c: c.due)
            if chunk.due > self.clock and left is None:
                return
            if chunk.due == math.inf:
                return
            self.take(chunk)

    def take(self, chunk):
        self.clock = max(self.clock, chunk.due)
        if chunk.received is not None:
            chunk.received = after(chunk.received, *self.tokens)
        elif chunk.stage == "start" and hasattr(chunk, "own") and self.tokens:
            chunk.own = after(chunk.own, *self.tokens)
        made = chunk.step()
        self.tokens = [made]
        rows = math.prod(made.shape[:-1])
        self.clock += 0.6 + rows / 768 + (2.7 if chunk.stage == 4 else 1.6)
        if not chunk.finished or chunk.stage == "x":
            chunk.due = self.transfer(chunk.stage, rows)


    def transfer(self, stage, rows):
        us = rows * ROW_US
        uses = {"x": {"x": us}, 1: {"y": us}, 2: {"z": us}, 4: {"m": 2.0 * us, "z": 1.0 * us}, "all": {"y": us / 2, "z": us, "m": us}, "share": {"y": us / 2, "z": us, "m": us}}.get(stage, {})
        start = max([self.clock - 1] + [self.links[n] for n in uses])
        for n, t in uses.items():
            self.links[n] = start + t
        return start + max(list(uses.values()) + [us / 13]) + (HOP_US if uses else 1.0)

    def finish(self, chunk):
        while not chunk.finished:
            self.take(chunk)

    def add(self, chunk):
        chunk.due = self.clock
        self.chunks.append(chunk)
        self.service()

COST_SCALE = 16
SWAPPED = (True, True, True)
OUTER_ORDER = (1, 'x', 2, 4)
INNER_ORDER = (2, 'x', 1, 4)
QKV_ORDER = (1, 2, 4)


def sds(shape, dtype):
    return jax.ShapeDtypeStruct(shape, dtype)


ANY = pl.BlockSpec(memory_space=pltpu.HBM)
VM = pl.BlockSpec(memory_space=pltpu.VMEM)


def rotate(v, cosine, sine):
    a, b = v[:HALF_DEPTH], v[HALF_DEPTH:]
    return jnp.concatenate([a * cosine - b * sine, b * cosine + a * sine], axis=0)


def unrotate(v, cosine, sine):
    a, b = v[:HALF_DEPTH], v[HALF_DEPTH:]
    return jnp.concatenate([a * cosine + b * sine, b * cosine - a * sine], axis=0)


def row_select(rows, columns):
    index = lax.broadcasted_iota(jnp.int32, (8, columns), 0)
    out = jnp.zeros((8, columns), F32)
    for i, r in enumerate(rows):
        if r is not None:
            out = jnp.where(index == i, r, out)
    return out


def augment(top, rows, total=2 * HD):
    columns = top.shape[1]
    tail = row_select(rows, columns)
    rest = jnp.zeros((total - HD - 8, columns), F32)
    return jnp.concatenate([top, tail, rest], axis=0)


def split3(v):
    high = v.astype(BF16).astype(F32)
    mid = (v - high).astype(BF16).astype(F32)
    return high, mid, v - high - mid


def mask_row(length):
    index = lax.broadcasted_iota(jnp.int32, (1, LENGTH), 1)
    return jnp.where(index < length, 0.0, NEGATIVE)


def place_of(sc, own, mine):
    me = lax.axis_index("mp")
    half, seq = me % 2, me // 2
    seq = seq if mine else 1 - seq
    return pl.multiple_of(half * own, own), pl.multiple_of((1 - half) * own, own), pl.multiple_of(seq * LENGTH, LENGTH), sc[seq]


def divide(total_ref, bit, slot, send_ref, keep_ref):
    n = total_ref.shape[0] // 2
    upper = (lax.axis_index("dp") & bit) > 0
    kept, sent = jnp.where(upper, n, 0), jnp.where(upper, 0, n)
    keep_ref[slot] = total_ref[pl.ds(pl.multiple_of(kept, n), n), :]
    send_ref[slot * n : (slot + 1) * n] = total_ref[pl.ds(pl.multiple_of(sent, n), n), :].astype(BF16)


def attention_forward(heads, own, mine, sc, tokens_ref, w_ref, b_ref, wo_ref, angles_ref, kv_ref, q_ref, o_ref, ob_ref, l_ref, kn_ref, keep_ref, give_ref, k_ref, s_ref, x_ref, table_ref, sem, table_sem):
    near, far, start, length = place_of(sc, own, mine)
    width = heads * HD
    copy = pltpu.make_async_copy(tokens_ref.at[pl.ds(start, LENGTH), :], x_ref, sem)
    copy.start()
    table_copy = pltpu.make_async_copy(angles_ref, table_ref, table_sem)
    table_copy.start()
    bias = jnp.concatenate([jnp.transpose(jnp.broadcast_to(b_ref[i : i + 1], (128, width)))[:, :1] for i in range(3)])
    copy.wait()
    x = x_ref[...]
    kv = mm(w_ref[width:], x, NT) + bias[width:]
    q = mm(w_ref[:width], x, NT) + bias[:width]
    table_copy.wait()
    cosine, sine = table_ref[:HALF_DEPTH], table_ref[HALF_DEPTH:]
    mask = mask_row(length)
    one = jnp.ones((1, LENGTH), F32)
    kv_ref[width:] = kv[width:].astype(BF16)
    k_ref[...], s_ref[...] = kv[:width], q
    l_ref[...] = jnp.zeros(l_ref.shape, F32)

    def head(h, carry):
        at = pl.ds(pl.multiple_of(h * HD, HD), HD)
        v_at = pl.ds(pl.multiple_of(width + h * HD, HD), HD)
        k_rot = rotate(k_ref[at, :], cosine, sine)
        kv_ref[at, :] = k_rot.astype(BF16)
        kn_ref[h] = jnp.transpose(augment(k_rot, (one, one, one, mask))).astype(BF16)
        q_rot = rotate(s_ref[at, :], cosine, sine)
        q_ref[at, :] = q_rot.astype(BF16)
        keys = kn_ref[h]
        v_aug = jnp.concatenate([kv_ref[v_at, :], jnp.ones((16, LENGTH), BF16)], axis=0)
        for c in range(0, LENGTH, FORWARD_CHUNK):
            q_aug = augment(q_rot[:, c : c + FORWARD_CHUNK], (None, None, None, jnp.ones((1, FORWARD_CHUNK), F32)))
            s = mm(keys, q_aug.astype(BF16), NN)
            top = jnp.max(s, axis=0, keepdims=True)
            p = jnp.exp2((s - top) * EXP_SCALE).astype(BF16)
            o = mm(v_aug, p, NN)
            mass = o[HD : HD + 1]
            o = o[:HD] / mass
            o_ref[at, c : c + FORWARD_CHUNK] = o
            ob_ref[at, c : c + FORWARD_CHUNK] = o.astype(BF16)
            l_ref[pl.ds(h, 1), c : c + FORWARD_CHUNK] = top + jnp.log2(mass) / EXP_SCALE
        return carry

    lax.fori_loop(0, heads, head, 0)
    keep_ref[...] = mm(ob_ref[:, pl.ds(near, own)], wo_ref[...], TN)
    give_ref[...] = mm(ob_ref[:, pl.ds(far, own)], wo_ref[...], TN).astype(give_ref.dtype)


def attention_backward(heads, own, mine, bit, sc, tokens_ref, kv_ref, q_ref, o_ref, ob_ref, l_ref, kn_ref, near_ref, far_ref, wo_ref, table_ref, *refs):
    before, outs, (da_ref, do_ref, x_ref, sum_ref, sem) = refs[: 0 if mine else 8], refs[0 if mine else 8 : -5], refs[-5:]
    dy_ref, gb_ref = outs[:2]
    near, far, start, length = place_of(sc, own, mine)
    copy = pltpu.make_async_copy(tokens_ref.at[pl.ds(start, LENGTH), :], x_ref, sem)
    copy.start()
    width = heads * HD
    da_ref[pl.ds(near, own), :] = near_ref[...]
    da_ref[pl.ds(far, own), :] = far_ref[...]
    do_ref[...] = mm(wo_ref[...], da_ref[...], NT).astype(BF16)
    cosine, sine = table_ref[:HALF_DEPTH], table_ref[HALF_DEPTH:]
    mask = mask_row(length)
    one = jnp.ones((1, LENGTH), F32)
    zeros = jnp.zeros((HD - 8, LENGTH), F32)
    tail_k = jnp.concatenate([row_select((one, one, one, mask), LENGTH), zeros], axis=0).astype(BF16)
    tail_v = jnp.concatenate([row_select((one, one, one), LENGTH), zeros], axis=0).astype(BF16)
    scale = HD ** (-0.5)
    def head(h, carry):
        at = pl.ds(pl.multiple_of(h * HD, HD), HD)
        k_at = pl.ds(pl.multiple_of(width + h * HD, HD), HD)
        v_at = pl.ds(pl.multiple_of(2 * width + h * HD, HD), HD)
        d_out = do_ref[at, :].astype(F32)
        delta = jnp.sum(d_out * o_ref[at, :], axis=0, keepdims=True)
        qn = jnp.transpose(augment(q_ref[at, :].astype(F32), (*split3(-l_ref[pl.ds(h, 1), :]), one))).astype(BF16)
        dn = jnp.transpose(augment(d_out, split3(-delta))).astype(BF16)
        k_aug = jnp.concatenate([kv_ref[at, :], tail_k], axis=0)
        v_aug = jnp.concatenate([kv_ref[k_at, :], tail_v], axis=0)
        keys = kn_ref[h]
        dk = dv = None
        dq = []
        for c in range(0, LENGTH, BACKWARD_CHUNK):
            p = jnp.exp2(mm(qn[c : c + BACKWARD_CHUNK], k_aug, NN) * EXP_SCALE)
            dp = mm(dn[c : c + BACKWARD_CHUNK], v_aug, NN)
            ds = (p * dp).astype(BF16)
            dq.append(mm(ds, keys, NN))
            dk_part = mm(q_ref[at, c : c + BACKWARD_CHUNK], ds, NN)
            dv_part = mm(do_ref[at, c : c + BACKWARD_CHUNK], p.astype(BF16), NN)
            dk = dk_part if dk is None else dk + dk_part
            dv = dv_part if dv is None else dv + dv_part
        dq_t = jnp.transpose(jnp.concatenate(dq, axis=0))[:HD]
        dy_ref[at, :] = (unrotate(dq_t, cosine, sine) * scale).astype(BF16)
        dy_ref[k_at, :] = (unrotate(dk, cosine, sine) * scale).astype(BF16)
        dy_ref[v_at, :] = dv.astype(BF16)
        return carry

    lax.fori_loop(0, heads, head, 0)
    copy.wait()
    gw = mm(dy_ref[...], x_ref[...], NN)
    go = mm(ob_ref[...], da_ref[...], NN)
    gb = mm(jnp.ones((8, LENGTH), BF16), dy_ref[...], NT)
    if before:
        gw, go, gb = gw + before[0][: 3 * width], go + before[0][3 * width :], gb + before[1][...]
    gb_ref[...] = gb
    total_ref = outs[2] if mine else sum_ref
    total_ref[: 3 * width] = gw
    total_ref[3 * width :] = go
    if not mine:
        divide(sum_ref, bit, 0, outs[2], outs[3])
        pack_small(outs[4], outs[2], gb, *before[2:])


def norm_stats(v):
    centered = v - jnp.mean(v, axis=-1, keepdims=True)
    inverse = lax.rsqrt(jnp.mean(centered * centered, axis=-1, keepdims=True) + EPSILON)
    return centered * inverse, inverse


def norm_back(grad, hat, inverse, gain):
    scaled = grad * gain
    return inverse * (
        scaled
        - jnp.mean(scaled, axis=-1, keepdims=True)
        - hat * jnp.mean(scaled * hat, axis=-1, keepdims=True)
    )


def row_blocks(rows, step, block=128):
    def body(i, carry):
        step(pl.ds(pl.multiple_of(i * block, block), block))
        return carry

    lax.fori_loop(0, rows // block, body, 0)


def project_norm(sc, tokens_ref, keep_ref, core_ref, far_ref, bias_ref, gain_ref, shift_ref, n_ref, nt_ref, hat_ref, inv_ref, x_ref, sem):
    rows = hat_ref.shape[0]
    copy = pltpu.make_async_copy(tokens_ref.at[pl.ds(pl.multiple_of(lax.axis_index("mp") * rows, rows), rows), :], x_ref, sem)
    copy.start()
    copy.wait()

    def step(at):
        total = x_ref[at, :].astype(F32) + bias_ref[...]
        total = total + (keep_ref[at, :] + core_ref[at, :].astype(F32) + far_ref[at, :].astype(F32))
        hat, inverse = norm_stats(total)
        n = hat * gain_ref[...] + shift_ref[...]
        hat_ref[at, :] = hat
        inv_ref[at, :] = inverse
        n_ref[at, :] = n.astype(BF16)
        nt_ref[:, at] = jnp.transpose(n).astype(BF16)

    row_blocks(rows, step)


def gelu_parts(z):
    e = jnp.exp2(z * z * (-0.5 * math.log2(math.e)))
    t = 1.0 / (1.0 + jnp.abs(z) * (ERF_P / math.sqrt(2.0)))
    poly = jnp.full_like(z, 0.5 * ERF_C[-1])
    for c in ERF_C[-2::-1]:
        poly = poly * t + 0.5 * c
    tail = poly * e
    phi = jnp.where(z >= 0, 1.0 - tail, tail)
    return z * phi, phi + z * e * (1.0 / math.sqrt(2.0 * math.pi))


def ffn_forward(block, sc, n_ref, wi_ref, bi_ref, wo_ref, *refs):
    g_ref, d_ref, f_ref = refs[-3:]

    def step(at):
        z = mm(n_ref[at, :], wi_ref[...], NN) + bi_ref[...]
        g, d = gelu_parts(z)
        g = g.astype(BF16)
        g_ref[at, :] = g
        d_ref[at, :] = d
        part = mm(g, wo_ref[...], NN)
        f_ref[at, :] = part + refs[0][at, :] if len(refs) > 3 else part

    row_blocks(n_ref.shape[0], step, block)


def add_sums(small_ref, at, values):
    @pl.when(at.start == 0)
    def _():
        small_ref[...] = jnp.zeros(small_ref.shape, F32)

    small_ref[...] += row_select([jnp.sum(v, axis=0, keepdims=True) for v in values], small_ref.shape[1])


def second_norm(sc, f_ref, hat_ref, cot_ref, g1_ref, s1_ref, ob_ref, g2_ref, s2_ref, out_ref, dr_ref, df_ref, small_ref):
    rows = f_ref.shape[0]

    def step(at):
        first = hat_ref[at, :] * g1_ref[...] + s1_ref[...]
        hat, inverse = norm_stats(first + f_ref[at, :] + ob_ref[...])
        out_ref[at, :] = (hat * g2_ref[...] + s2_ref[...]).astype(BF16)
        me = lax.axis_index("mp")
        place = lax.broadcasted_iota(jnp.int32, (at.size, 1), 0) + at.start + (me % 2) * rows
        grad = jnp.where(place < sc[me // 2], cot_ref[at, :].astype(F32), 0.0)
        dr = norm_back(grad, hat, inverse, g2_ref[...])
        dr_ref[at, :] = dr
        df_ref[at, :] = dr.astype(BF16)
        add_sums(small_ref, at, (grad * hat, grad, dr))

    row_blocks(rows, step)


def outer_odd(sc, one_ref, three_ref, df_ref, *out_refs):
    count = out_refs[0].shape[0] // 2
    df = df_ref[...]
    for j, g_ref in enumerate((one_ref, three_ref)):
        total = mm(g_ref[...], df, TN).astype(BF16)
        for k, out_ref in enumerate(out_refs):
            out_ref[j * count : (j + 1) * count] = total[k * count : (k + 1) * count]


def outer_even(bit, sc, zero_ref, two_ref, df_ref, arrived_ref, send_ref, keep_ref, sum_ref):
    count = sum_ref.shape[0]
    df = df_ref[...]
    for j, g_ref in enumerate((zero_ref, two_ref)):
        sum_ref[...] = mm(g_ref[...], df, TN) + arrived_ref[j * count : (j + 1) * count].astype(F32)
        divide(sum_ref, bit, j, send_ref, keep_ref)


def ffn_backward(slot, bit, sc, df_ref, wo_ref, d_ref, wi_ref, nt_ref, dn_in_ref, *refs):
    arrived, outs, (dz_ref, sum_ref) = refs[: {0: 2}.get(slot, 1 - slot % 2)], refs[{0: 2}.get(slot, 1 - slot % 2) : -2], refs[-2:]
    gb_ref, dn_ref = outs[:2]
    dz = (mm(df_ref[...], wo_ref[...], NT) * d_ref[...]).astype(BF16)
    dz_ref[...] = dz
    dn_ref[...] = dn_in_ref[...] + mm(dz, wi_ref[...], NT)
    gb_ref[...] = jnp.sum(dz_ref[...].astype(F32), axis=0, keepdims=True)
    total = mm(nt_ref[...], dz_ref[...], NN)
    if slot % 2 == 0:
        total = total + arrived[0][...].astype(F32)
    if slot:
        outs[2][...] = total.astype(outs[2].dtype)
    else:
        sum_ref[...] = total
        divide(sum_ref, bit, 0, outs[2], outs[3])
        divide(arrived[1], bit, 1, outs[2], outs[3])


def first_norm_back(sc, dn_ref, hat_ref, inv_ref, gain_ref, dr_ref, low_ref, small_ref):
    def step(at):
        grad, hat = dn_ref[at, :], hat_ref[at, :]
        dr = norm_back(grad, hat, inv_ref[at, :], gain_ref[...])
        dr_ref[at, :] = dr
        low_ref[at, :] = dr.astype(BF16)
        add_sums(small_ref, at, (dr, grad * hat, grad))

    row_blocks(dn_ref.shape[0], step)


def token_grad(own, sc, dy_ref, w_ref, *refs):
    before, (keep_ref, give_ref) = refs[:-2], refs[-2:]
    near, far, _, _ = place_of(sc, own, True)
    total = mm(dy_ref[:, pl.ds(near, own)], w_ref[...], TN)
    for ref in before:
        total = total + ref[...]
    keep_ref[...] = total
    give_ref[...] = mm(dy_ref[:, pl.ds(far, own)], w_ref[...], TN).astype(BF16)


def pack_small(out_ref, send_ref, qkv, small2, small1, *inner):
    me = lax.axis_index("mp")
    out_ref[...] = jnp.zeros(out_ref.shape, F32)
    out_ref[0:3] = small2[0:3]
    out_ref[3:6] = small1[0:3]
    for r in range(4):
        out_ref[pl.ds(8 + (me ^ r), 1), :] = inner[r][...]
    out_ref[pl.ds(12 + me, 1), pl.ds(0, qkv.shape[1])] = qkv[0:1]
    count = out_ref.shape[0]
    for i, part in enumerate(split3(out_ref[...])):
        at = send_ref.shape[0] - (3 - i) * count
        send_ref[at : at + count] = part.astype(BF16)


def swap(v, axis, bit):
    size = lax.axis_size(axis)
    return lax.ppermute(v, axis, [(i, i ^ bit) for i in range(size)])


def after(v, *others):
    return lax.optimization_barrier((v, *others))[0]


def dp_upper(bit):
    return (lax.axis_index("dp") & bit) > 0


def parts3(v):
    high = lax.reduce_precision(v, 8, 7)
    mid = lax.reduce_precision(v - high, 8, 7)
    return high, mid, v - high - mid


class Chunk:
    def __init__(self, order, cut=None, swapped=False):
        size = lax.axis_size("dp")
        bits = [1 << i for i in range(size.bit_length() - 1)]
        self.order = [b for b in order if b == "x" or b in bits]
        self.order += [b for b in bits if b not in order]
        self.last = [b for b in self.order if b != "x"][-1]
        self.back = [b for b in self.order[::-1] if b not in ("x", self.last)]
        self.swapped = swapped and len(self.back) == 2
        if self.swapped:
            self.back = self.back[::-1]
        self.bit = self.order[0]
        self.received = self.total = self.result = self.rider = None
        self.cut = cut
        self.stage = "start"
        self.finished = False

    def begin(self, run, send, keep, rider=None):
        self.stage = self.order.pop(0)
        self.received = self.exchange(send)
        self.total, self.rider = keep, rider
        self.rows = math.prod(keep.shape[:-1])
        run.clock += 1.6
        self.due = run.transfer(self.stage, self.received.shape[0])
        run.chunks.append(self)

    def exchange(self, send):
        self.rows = send.shape[0]
        if self.rider is not None:
            send = jnp.concatenate([send] + [v.astype(BF16) for v in parts3(self.rider)])
        return swap(send, "mp" if self.stage == "x" else "dp", 2 if self.stage == "x" else self.stage)

    def merged(self):
        arrived = self.received[: self.rows].astype(F32)
        if self.rider is not None:
            parts = self.received[self.rows :].astype(F32).reshape(3, *self.rider.shape)
            self.rider = self.rider + (parts[0] + parts[1] + parts[2])
        return self.total + arrived.reshape(self.total.shape)

    def step(self):
        if self.order:
            total = self.merged()
            self.stage = self.order.pop(0)
            if self.stage == "x":
                send, self.total = total[1].astype(BF16), total[:1]
            elif self.stage == self.last:
                send = total.reshape(-1, total.shape[-1]).astype(BF16)
                self.total = send.astype(F32).reshape(total.shape)
            else:
                upper = dp_upper(self.stage)
                n = total.shape[1] // 2
                low, high = total[:, :n], total[:, n:]
                send = jnp.where(upper, low, high).astype(BF16).reshape(-1, total.shape[-1])
                self.total = jnp.where(upper, high, low)
            self.received = self.exchange(send)
            return send
        if self.back:
            if self.total is not None:
                self.held = self.merged()[0].astype(BF16)
                self.ridden, self.rider, self.total = self.rider, None, None
            else:
                self.held = self.joined()
            self.stage = self.back.pop(0)
            self.received = swap(self.held, "dp", self.stage)
            return self.held
        self.finished = True
        if self.cut is None or self.swapped:
            self.result = self.joined().astype(F32)
            return self.result
        upper = dp_upper(self.stage)
        first, second = jnp.where(upper, self.received, self.held), jnp.where(upper, self.held, self.received)
        rest = self.cut - first.shape[0]
        self.result = jnp.concatenate([first, second[:rest]]).astype(F32), second[rest:].astype(F32)
        return self.result[0]

    def joined(self):
        pair = (self.held, self.received)
        if self.swapped and not self.back:
            pair = tuple(v.reshape(2, 1, -1, v.shape[-1]) for v in pair)
            rows = jnp.where(dp_upper(self.stage), jnp.concatenate(pair[::-1], axis=1), jnp.concatenate(pair, axis=1))
            return rows.reshape(-1, rows.shape[-1])
        return jnp.where(dp_upper(self.stage), jnp.concatenate(pair[::-1]), jnp.concatenate(pair))


class Everywhere:
    def __init__(self, v):
        self.own, self.received = v, None
        self.stages = [1, 2]
        self.finished = False
        self.stage = "start"

    def step(self):
        if self.received is not None:
            self.own = self.own + self.received
        if self.stages:
            bit = self.stages.pop(0)
            self.stage = {1: "core", 2: "x"}[bit]
            self.received = swap(self.own, "mp", bit)
        else:
            self.finished, self.stage = True, "end"
        return self.own


class Exchange:
    def __init__(self):
        self.finished = False
        self.stage = "core"

    def begin(self, run, keep, give):
        self.keep = keep
        self.received = swap(give, "mp", 1)
        run.chunks.append(self)
        self.due = run.transfer("core", give.shape[0] * give.dtype.itemsize // 2)

    def step(self):
        made = (self.keep + self.received.astype(F32)).astype(BF16)
        self.received = swap(made, "mp", 2)
        self.stage = "x"
        self.finished = True
        return made


class Gather:
    def __init__(self, own, bits):
        self.own, self.bits = own, list(bits)
        self.received = None
        self.stage = "start"
        self.finished = False

    def step(self):
        if self.stage == "start":
            self.held = self.own
            for bit in self.bits[::-1]:
                self.held = half_of(self.held, bit)
            self.stage, self.received = "x", swap(self.held, "mp", 2)
            return self.held
        if self.stage == "x":
            self.held = self.received
        else:
            self.held = join_halves(self.held, self.received, self.stage)
        if self.bits:
            self.stage = self.bits.pop(0)
            self.received = swap(self.held, "dp", self.stage)
            return self.held
        self.two, self.stage = self.held, "core"
        self.three = swap(self.two, "mp", 1)
        self.finished = True
        return self.two


def half_of(v, bit):
    n = v.shape[0] // 2
    return lax.dynamic_slice_in_dim(v, jnp.where(dp_upper(bit), n, 0), n, 0)


def join_halves(mine, other, bit):
    return jnp.where(dp_upper(bit), jnp.concatenate([other, mine]), jnp.concatenate([mine, other]))


def on_device(
    tokens,
    qkv_weight,
    qkv_bias,
    output_weight,
    output_bias,
    first_gain,
    first_shift,
    inner_weight,
    inner_bias,
    outer_weight,
    outer_bias,
    second_gain,
    second_shift,
    cotangent,
    seq_lengths,
):
    depth = tokens.shape[1]
    own = cotangent.shape[0]
    width = qkv_weight.shape[2]
    heads = width // HD
    hidden = inner_weight.shape[1]
    me = lax.axis_index("mp")
    table = jnp.asarray(rotary_tables())
    run = Program(seq_lengths)

    bias_one = swap(inner_bias, "mp", 1)
    inner_w, outer_w = [inner_weight, None, None, None], [outer_weight, None, None, None]
    inner_w[1], outer_w[1] = swap(inner_weight, "mp", 1), swap(outer_weight, "mp", 1)
    inner_gather, outer_gather = Gather(inner_weight, (1, 2)), Gather(outer_weight, (2, 1))
    run.add(inner_gather)
    run.add(outer_gather)
    qkv_w = jnp.transpose(qkv_weight, (1, 2, 0)).reshape(3 * width, depth)
    rows = {n: v.reshape(1, -1) for n, v in dict(ob=output_bias, g1=first_gain, s1=first_shift, b2=outer_bias, g2=second_gain, s2=second_shift).items()}

    kv, q, o, ob, logs, keys = ([None] * 2 for _ in range(6))

    def attend(mine):
        kv[mine], q[mine], o[mine], ob[mine], logs[mine], keys[mine], keep, give = run.call(
            functools.partial(attention_forward, heads, own, mine),
            [
                sds((2 * width, LENGTH), BF16),
                sds((width, LENGTH), BF16),
                sds((width, LENGTH), F32),
                sds((width, LENGTH), BF16),
                sds((8, LENGTH), F32),
                sds((heads, LENGTH, 2 * HD), BF16),
                sds((own, depth), F32),
                sds((own, depth), BF16 if mine else F32),
            ],
            [tokens, qkv_w, qkv_bias, output_weight, table],
            in_specs=[ANY, VM, VM, VM, ANY],
            flops=2 * depth * width * 4 * LENGTH + 4 * LENGTH * LENGTH * 256 * heads,
            name="attention_forward",
            us=8.7,
            scratch=[pltpu.VMEM((width, LENGTH), F32)] * 2 + [pltpu.VMEM((LENGTH, depth), BF16), pltpu.VMEM((HD, LENGTH), F32), pltpu.SemaphoreType.DMA, pltpu.SemaphoreType.DMA],
        )
        return keep, give

    run.wait(inner_w[1], outer_w[1], bias_one)
    run.clock += 3.0
    far_sum = Exchange()
    run.hold = True
    keep, give = attend(0)
    run.hold = False
    for gather in (inner_gather, outer_gather):
        gather.received = after(gather.received, *run.tokens)
    bias_pair = swap(jnp.stack([after(inner_bias, kv[0]), bias_one]), "mp", 2)
    bias_slots = [inner_bias.reshape(1, -1), bias_one.reshape(1, -1), bias_pair[:1], bias_pair[1:]]
    far_sum.begin(run, keep, after(give, inner_gather.received, outer_gather.received))
    run.finish(far_sum)
    far = far_sum.received
    run.clock = max(run.clock, inner_gather.due, outer_gather.due)
    run.service()
    run.hold = True
    keep, give = attend(1)
    run.hold = False
    for gather in (inner_gather, outer_gather):
        gather.received = after(gather.received, *run.tokens)
    core = swap(after(give, inner_gather.received, outer_gather.received), "mp", 1)
    run.clock = max(run.clock, inner_gather.due, outer_gather.due)
    run.service()
    run.clock = max(run.clock, far_sum.due)
    run.wait(far, core)
    run.service()
    n_low, n_t, hat, inverse = run.call(
        project_norm,
        [sds((own, depth), BF16), sds((depth, own), BF16), sds((own, depth), F32), sds((own, 1), F32)],
        [tokens, keep, core, far, rows["ob"], rows["g1"], rows["s1"]],
        in_specs=[ANY] + [VM] * 6,
        scratch=[pltpu.VMEM((own, depth), BF16), pltpu.SemaphoreType.DMA],
        flops=40 * own * depth,
        name="project_norm",
        us=2.0,
    )

    block = 512
    g, d = [None] * 4, [None] * 4

    def feed(r, *f):
        g[r], d[r], f = run.call(
            functools.partial(ffn_forward, block),
            [sds((own, hidden), BF16), sds((own, hidden), F32), sds((own, depth), F32)],
            [n_low, inner_w[r], bias_slots[r], outer_w[r], *f],
            flops=4 * own * depth * hidden,
            name="ffn_forward",
            us=3.0,
        )
        return f

    run.hold = True
    f = feed(0)
    run.wait(bias_pair)
    f = feed(1, f)
    run.hold = False
    for gather in (inner_gather, outer_gather):
        run.finish(gather)
    inner_w[2:], outer_w[2:] = ([v.two, v.three] for v in (inner_gather, outer_gather))
    f = feed(2, f)
    f = feed(3, f)
    layer_out, dr2, df, small2 = run.call(
        second_norm,
        [sds((own, depth), BF16), sds((own, depth), F32), sds((own, depth), BF16), sds((8, depth), F32)],
        [f, hat, cotangent, rows["g1"], rows["s1"], rows["b2"], rows["g2"], rows["s2"]],
        flops=40 * own * depth,
        name="second_norm",
        us=2.7,
    )
    odd = run.call(
        outer_odd,
        [sds((2 * hidden, depth), BF16)],
        [g[1], g[3], df],
        flops=4 * own * depth * hidden,
        name="outer_odd",
        us=1.9,
    )
    arrived = swap(odd[0], "mp", 1)
    inner_g, inner_bg = [None] * 4, [None] * 4
    dn = dr2

    def feed_back(r, dn, *arrived):
        divided = [sds((depth, hidden), BF16), sds((2, depth // 2, hidden), F32)]
        inner_bg[r], dn, *inner_g[r] = run.call(
            functools.partial(ffn_backward, r, inner_sum.bit),
            [sds((1, hidden), F32), sds((own, depth), F32)] + (divided if r == 0 else [sds((depth, hidden), F32 if r == 2 else BF16)]),
            [df, outer_w[r], d[r], inner_w[r], n_t, dn, *arrived],
            flops=6 * own * depth * hidden,
            name="ffn_backward",
            us=2.6 if r else 3.0,
            scratch=[pltpu.VMEM((own, hidden), BF16), pltpu.VMEM((depth, hidden), F32)],
        )
        return dn

    outer_sum, inner_sum, attention_sum = Chunk(OUTER_ORDER, None, SWAPPED[0]), Chunk(INNER_ORDER, None, SWAPPED[1]), Chunk(QKV_ORDER, 3 * width, SWAPPED[2])
    dn = feed_back(3, dn)
    send, kept = run.call(
        functools.partial(outer_even, outer_sum.bit),
        [sds((hidden, depth), BF16), sds((2, hidden // 2, depth), F32)],
        [g[0], g[2], df, arrived],
        flops=4 * own * depth * hidden,
        name="outer_even",
        us=2.4,
        scratch=[pltpu.VMEM((hidden, depth), F32)],
    )
    outer_sum.begin(run, send, kept)
    three = swap(inner_g[3][0], "mp", 1)
    dn = feed_back(1, dn)
    one = swap(inner_g[1][0], "mp", 1)
    dn = feed_back(2, dn, three)
    dn = feed_back(0, dn, one, inner_g[2][0])
    dr1, low, small1 = run.call(
        first_norm_back,
        [sds((own, depth), F32), sds((own, depth), BF16), sds((8, depth), F32)],
        [dn, hat, inverse, rows["g1"]],
        flops=40 * own * depth,
        name="first_norm_back",
        us=1.9,
    )

    low_far = swap(low, "mp", 2)
    low_due = run.transfer("x", own)
    run.clock += 1.5
    inner_sum.begin(run, *inner_g[0])
    low_core = swap(low, "mp", 1)

    def attend_back(mine, near, far, *before):
        divided = [sds((2 * width + 48, depth), BF16), sds((1, 2 * width, depth), F32), sds((16, depth), F32)]
        return run.call(
            functools.partial(attention_backward, heads, own, mine, attention_sum.bit),
            [sds((3 * width, LENGTH), BF16), sds((8, 3 * width), F32)] + ([sds((4 * width, depth), F32)] if mine else divided),
            [tokens, kv[mine], q[mine], o[mine], ob[mine], logs[mine], keys[mine], near, far, output_weight, table, *before],
            in_specs=[ANY] + [VM] * (10 + len(before)),
            flops=2 * depth * width * 5 * LENGTH + 10 * LENGTH * LENGTH * 256 * heads,
            name="attention_backward",
            us=11.0 if mine else 12.0,
            scratch=[pltpu.VMEM((LENGTH, depth), BF16), pltpu.VMEM((width, LENGTH), BF16), pltpu.VMEM((LENGTH, depth), BF16), pltpu.VMEM((4 * width, depth), F32), pltpu.SemaphoreType.DMA],
        )

    def token_part(dy, *before):
        return run.call(
            functools.partial(token_grad, own),
            [sds((own, depth), F32), sds((own, depth), BF16)],
            [dy, qkv_w, *before],
            flops=6 * own * depth * depth,
            name="token_grad",
            us=2.4,
        )

    run.hold = True
    dy, bias_sum, weight_sum = attend_back(1, low, low_core)
    own_keep, own_give = token_part(dy, dr1)
    own_core = swap(own_give, "mp", 1)
    run.hold = False
    run.take(outer_sum)
    run.clock = max(run.clock, low_due)
    low_far = after(low_far, *run.tokens)
    low_far_core = swap(low_far, "mp", 1)
    run.tokens = [low_far]
    run.wait(own_core)
    run.service()
    run.clock += 1.5
    dy, _, send, kept, packed = attend_back(0, low_far, low_far_core, weight_sum, bias_sum, small2, small1, *inner_bg)
    attention_sum.begin(run, send, kept, packed)
    far_keep, far_give = token_part(dy)
    token_far = Exchange()
    token_far.begin(run, far_keep, far_give)
    while not hasattr(attention_sum, "ridden"):
        run.take(min([c for c in run.chunks if not c.finished], key=lambda c: c.due))
    small_sum = Everywhere(attention_sum.ridden)
    run.add(small_sum)
    run.service(0)
    tokens_grad = own_keep + (own_core.astype(F32) + token_far.received.astype(F32))
    small = small_sum.own
    outer_weight_grad, inner_weight_grad = outer_sum.result, inner_sum.result
    if attention_sum.swapped:
        attention_sum.result = attention_sum.result[: 3 * width], attention_sum.result[3 * width :]
    qkv_weight_grad, output_weight_grad = attention_sum.result
    qkv_weight_grad = jnp.transpose(qkv_weight_grad.reshape(3, width, depth), (2, 0, 1))
    second_gain_grad, second_shift_grad, outer_bias_grad, output_bias_grad, first_gain_grad, first_shift_grad = (small[i] for i in range(6))
    inner_bias_grad = lax.dynamic_index_in_dim(small, 8 + me, 0, keepdims=False)
    qkv_bias_grad = lax.dynamic_index_in_dim(small, 12 + me, 0, keepdims=False)[: 3 * width].reshape(3, width)
    return (
        layer_out,
        tokens_grad,
        qkv_weight_grad,
        qkv_bias_grad,
        output_weight_grad,
        output_bias_grad,
        first_gain_grad,
        first_shift_grad,
        inner_weight_grad,
        inner_bias_grad,
        outer_weight_grad,
        outer_bias_grad,
        second_gain_grad,
        second_shift_grad,
    )


def solution(mesh):
    return jax.shard_map(
        on_device,
        mesh=mesh,
        in_specs=(
            P("dp", None),
            P(None, None, "mp"),
            P(None, "mp"),
            P("mp", None),
            P(),
            P(),
            P(),
            P(None, "mp"),
            P("mp"),
            P("mp", None),
            P(),
            P(),
            P(),
            P(("dp", "mp"), None),
            P("dp"),
        ),
        out_specs=(
            P(("dp", "mp"), None),
            P(("dp", "mp"), None),
            P(None, None, "mp"),
            P(None, "mp"),
            P("mp", None),
            P(),
            P(),
            P(),
            P(None, "mp"),
            P("mp"),
            P("mp", None),
            P(),
            P(),
            P(),
        ),
        check_vma=False,
    )
```

```python
import functools
import math

import jax
import jax.numpy as jnp
import numpy as np
from jax import lax
from jax.experimental import pallas as pl
from jax.experimental.pallas import tpu as pltpu
from jax.sharding import PartitionSpec as P

HD = 64
FORWARD_CHUNK = 512
BACKWARD_CHUNK = 256
HALF_DEPTH = HD // 2
LENGTH = 1024
EPSILON = 1e-12
NEGATIVE = -1e30
F32 = jnp.float32
BF16 = jnp.bfloat16
EXP_SCALE = HD ** (-0.5) * math.log2(math.e)

ERF_P = 0.52
ERF_C = (0.00514851, 0.23724269, 0.55266472, -0.39660497, 1.10267122, -0.61325166, 0.1121295)

NN = (((1,), (0,)), ((), ()))
NT = (((1,), (1,)), ((), ()))
TN = (((0,), (0,)), ((), ()))


def mm(a, b, dims):
    return lax.dot_general(a, b, dims, preferred_element_type=F32)


def rotary_tables():
    frequency = 10000.0 ** (-np.arange(HALF_DEPTH, dtype=np.float64) / HALF_DEPTH)
    angle = frequency[:, None] * np.arange(LENGTH, dtype=np.float64)[None, :]
    return np.concatenate([np.cos(angle), np.sin(angle)]).astype(np.float32)


ROW_US = 0.038
HOP_US = 4.0


class Program:
    def __init__(self, scalars):
        self.scalars = scalars
        self.tokens = []
        self.clock = 0.0
        self.links = {"x": 0.0, "y": 0.0, "z": 0.0, "m": 0.0}
        self.chunks = []
        self.hold = False

    def wait(self, *values):
        self.tokens += values

    def call(self, body, outs, ins, grid=(), in_specs=None, out_specs=None, flops=0, name=None, vmem=16, us=5.0, scratch=()):
        scalars = after(self.scalars, *self.tokens)
        nbytes = sum(math.prod(a.shape) * a.dtype.itemsize for a in list(ins) + list(outs))
        whole = pl.BlockSpec(memory_space=pltpu.VMEM)
        result = pl.pallas_call(
            body,
            out_shape=outs,
            grid=grid,
            in_specs=[pl.BlockSpec(memory_space=pltpu.SMEM)] + (in_specs if in_specs is not None else [whole] * len(ins)),
            out_specs=out_specs if out_specs is not None else [whole] * len(outs),
            scratch_shapes=scratch,
            compiler_params=pltpu.CompilerParams(vmem_limit_bytes=vmem << 20),
            cost_estimate=pl.CostEstimate(flops=flops // COST_SCALE, bytes_accessed=nbytes // COST_SCALE, transcendentals=0),
            name=name,
        )(scalars, *ins)
        self.tokens = [result[0]]
        self.clock += us
        if not self.hold:
            self.service()
        return result

    def service(self, left=None):
        while True:
            waiting = [c for c in self.chunks if not c.finished]
            if not waiting or (left is not None and len(waiting) <= left):
                return
            chunk = min(waiting, key=lambda c: c.due)
            if chunk.due > self.clock and left is None:
                return
            if chunk.due == math.inf:
                return
            self.take(chunk)

    def take(self, chunk):
        self.clock = max(self.clock, chunk.due)
        if chunk.received is not None:
            chunk.received = after(chunk.received, *self.tokens)
        elif chunk.stage == "start" and hasattr(chunk, "own") and self.tokens:
            chunk.own = after(chunk.own, *self.tokens)
        made = chunk.step()
        self.tokens = [made]
        rows = math.prod(made.shape[:-1])
        self.clock += 0.6 + rows / 768 + (2.7 if chunk.stage == 4 else 1.6)
        if not chunk.finished or chunk.stage == "x":
            chunk.due = self.transfer(chunk.stage, rows)


    def transfer(self, stage, rows):
        us = rows * ROW_US
        uses = {"x": {"x": us}, 1: {"y": us}, 2: {"z": us}, 4: {"m": 2.0 * us, "z": 1.0 * us}, "all": {"y": us / 2, "z": us, "m": us}, "share": {"y": us / 2, "z": us, "m": us}}.get(stage, {})
        start = max([self.clock - 1] + [self.links[n] for n in uses])
        for n, t in uses.items():
            self.links[n] = start + t
        return start + max(list(uses.values()) + [us / 13]) + (HOP_US if uses else 1.0)

    def finish(self, chunk):
        while not chunk.finished:
            self.take(chunk)

    def add(self, chunk):
        chunk.due = self.clock
        self.chunks.append(chunk)
        self.service()

COST_SCALE = 16
SWAPPED = (True, True, True)
OUTER_ORDER = (1, 'x', 2, 4)
INNER_ORDER = (2, 'x', 1, 4)
QKV_ORDER = (1, 2, 4)


def sds(shape, dtype):
    return jax.ShapeDtypeStruct(shape, dtype)


ANY = pl.BlockSpec(memory_space=pltpu.HBM)
VM = pl.BlockSpec(memory_space=pltpu.VMEM)


def rotate(v, cosine, sine):
    a, b = v[:HALF_DEPTH], v[HALF_DEPTH:]
    return jnp.concatenate([a * cosine - b * sine, b * cosine + a * sine], axis=0)


def unrotate(v, cosine, sine):
    a, b = v[:HALF_DEPTH], v[HALF_DEPTH:]
    return jnp.concatenate([a * cosine + b * sine, b * cosine - a * sine], axis=0)


def row_select(rows, columns):
    index = lax.broadcasted_iota(jnp.int32, (8, columns), 0)
    out = jnp.zeros((8, columns), F32)
    for i, r in enumerate(rows):
        if r is not None:
            out = jnp.where(index == i, r, out)
    return out


def augment(top, rows, total=2 * HD):
    columns = top.shape[1]
    tail = row_select(rows, columns)
    rest = jnp.zeros((total - HD - 8, columns), F32)
    return jnp.concatenate([top, tail, rest], axis=0)


def split3(v):
    high = v.astype(BF16).astype(F32)
    mid = (v - high).astype(BF16).astype(F32)
    return high, mid, v - high - mid


def mask_row(length):
    index = lax.broadcasted_iota(jnp.int32, (1, LENGTH), 1)
    return jnp.where(index < length, 0.0, NEGATIVE)


def place_of(sc, own, mine):
    me = lax.axis_index("mp")
    half, seq = me % 2, me // 2
    seq = seq if mine else 1 - seq
    return pl.multiple_of(half * own, own), pl.multiple_of((1 - half) * own, own), pl.multiple_of(seq * LENGTH, LENGTH), sc[seq]


def divide(total_ref, bit, slot, send_ref, keep_ref):
    n = total_ref.shape[0] // 2
    upper = (lax.axis_index("dp") & bit) > 0
    kept, sent = jnp.where(upper, n, 0), jnp.where(upper, 0, n)
    keep_ref[slot] = total_ref[pl.ds(pl.multiple_of(kept, n), n), :]
    send_ref[slot * n : (slot + 1) * n] = total_ref[pl.ds(pl.multiple_of(sent, n), n), :].astype(BF16)


def attention_forward(heads, own, mine, sc, tokens_ref, w_ref, b_ref, wo_ref, angles_ref, kv_ref, q_ref, o_ref, ob_ref, l_ref, kn_ref, keep_ref, give_ref, k_ref, s_ref, x_ref, table_ref, sem, table_sem):
    near, far, start, length = place_of(sc, own, mine)
    width = heads * HD
    copy = pltpu.make_async_copy(tokens_ref.at[pl.ds(start, LENGTH), :], x_ref, sem)
    copy.start()
    table_copy = pltpu.make_async_copy(angles_ref, table_ref, table_sem)
    table_copy.start()
    bias = jnp.concatenate([jnp.transpose(jnp.broadcast_to(b_ref[i : i + 1], (128, width)))[:, :1] for i in range(3)])
    copy.wait()
    x = x_ref[...]
    kv = mm(w_ref[width:], x, NT) + bias[width:]
    q = mm(w_ref[:width], x, NT) + bias[:width]
    table_copy.wait()
    cosine, sine = table_ref[:HALF_DEPTH], table_ref[HALF_DEPTH:]
    mask = mask_row(length)
    one = jnp.ones((1, LENGTH), F32)
    kv_ref[width:] = kv[width:].astype(BF16)
    k_ref[...], s_ref[...] = kv[:width], q
    l_ref[...] = jnp.zeros(l_ref.shape, F32)

    def head(h, carry):
        at = pl.ds(pl.multiple_of(h * HD, HD), HD)
        v_at = pl.ds(pl.multiple_of(width + h * HD, HD), HD)
        k_rot = rotate(k_ref[at, :], cosine, sine)
        kv_ref[at, :] = k_rot.astype(BF16)
        kn_ref[h] = jnp.transpose(augment(k_rot, (one, one, one, mask))).astype(BF16)
        q_rot = rotate(s_ref[at, :], cosine, sine)
        q_ref[at, :] = q_rot.astype(BF16)
        keys = kn_ref[h]
        v_aug = jnp.concatenate([kv_ref[v_at, :], jnp.ones((16, LENGTH), BF16)], axis=0)
        for c in range(0, LENGTH, FORWARD_CHUNK):
            q_aug = augment(q_rot[:, c : c + FORWARD_CHUNK], (None, None, None, jnp.ones((1, FORWARD_CHUNK), F32)))
            s = mm(keys, q_aug.astype(BF16), NN)
            top = jnp.max(s, axis=0, keepdims=True)
            p = jnp.exp2((s - top) * EXP_SCALE).astype(BF16)
            o = mm(v_aug, p, NN)
            mass = o[HD : HD + 1]
            o = o[:HD] / mass
            o_ref[at, c : c + FORWARD_CHUNK] = o
            ob_ref[at, c : c + FORWARD_CHUNK] = o.astype(BF16)
            l_ref[pl.ds(h, 1), c : c + FORWARD_CHUNK] = top + jnp.log2(mass) / EXP_SCALE
        return carry

    lax.fori_loop(0, heads, head, 0)
    keep_ref[...] = mm(ob_ref[:, pl.ds(near, own)], wo_ref[...], TN)
    give_ref[...] = mm(ob_ref[:, pl.ds(far, own)], wo_ref[...], TN).astype(give_ref.dtype)


def attention_backward(heads, own, mine, bit, sc, tokens_ref, kv_ref, q_ref, o_ref, ob_ref, l_ref, kn_ref, near_ref, far_ref, wo_ref, table_ref, *refs):
    before, outs, (da_ref, do_ref, x_ref, sum_ref, sem) = refs[: 0 if mine else 8], refs[0 if mine else 8 : -5], refs[-5:]
    dy_ref, gb_ref = outs[:2]
    near, far, start, length = place_of(sc, own, mine)
    copy = pltpu.make_async_copy(tokens_ref.at[pl.ds(start, LENGTH), :], x_ref, sem)
    copy.start()
    width = heads * HD
    da_ref[pl.ds(near, own), :] = near_ref[...]
    da_ref[pl.ds(far, own), :] = far_ref[...]
    do_ref[...] = mm(wo_ref[...], da_ref[...], NT).astype(BF16)
    cosine, sine = table_ref[:HALF_DEPTH], table_ref[HALF_DEPTH:]
    mask = mask_row(length)
    one = jnp.ones((1, LENGTH), F32)
    zeros = jnp.zeros((HD - 8, LENGTH), F32)
    tail_k = jnp.concatenate([row_select((one, one, one, mask), LENGTH), zeros], axis=0).astype(BF16)
    tail_v = jnp.concatenate([row_select((one, one, one), LENGTH), zeros], axis=0).astype(BF16)
    scale = HD ** (-0.5)
    def head(h, carry):
        at = pl.ds(pl.multiple_of(h * HD, HD), HD)
        k_at = pl.ds(pl.multiple_of(width + h * HD, HD), HD)
        v_at = pl.ds(pl.multiple_of(2 * width + h * HD, HD), HD)
        d_out = do_ref[at, :].astype(F32)
        delta = jnp.sum(d_out * o_ref[at, :], axis=0, keepdims=True)
        qn = jnp.transpose(augment(q_ref[at, :].astype(F32), (*split3(-l_ref[pl.ds(h, 1), :]), one))).astype(BF16)
        dn = jnp.transpose(augment(d_out, split3(-delta))).astype(BF16)
        k_aug = jnp.concatenate([kv_ref[at, :], tail_k], axis=0)
        v_aug = jnp.concatenate([kv_ref[k_at, :], tail_v], axis=0)
        keys = kn_ref[h]
        dk = dv = None
        dq = []
        for c in range(0, LENGTH, BACKWARD_CHUNK):
            p = jnp.exp2(mm(qn[c : c + BACKWARD_CHUNK], k_aug, NN) * EXP_SCALE)
            dp = mm(dn[c : c + BACKWARD_CHUNK], v_aug, NN)
            ds = (p * dp).astype(BF16)
            dq.append(mm(ds, keys, NN))
            dk_part = mm(q_ref[at, c : c + BACKWARD_CHUNK], ds, NN)
            dv_part = mm(do_ref[at, c : c + BACKWARD_CHUNK], p.astype(BF16), NN)
            dk = dk_part if dk is None else dk + dk_part
            dv = dv_part if dv is None else dv + dv_part
        dq_t = jnp.transpose(jnp.concatenate(dq, axis=0))[:HD]
        dy_ref[at, :] = (unrotate(dq_t, cosine, sine) * scale).astype(BF16)
        dy_ref[k_at, :] = (unrotate(dk, cosine, sine) * scale).astype(BF16)
        dy_ref[v_at, :] = dv.astype(BF16)
        return carry

    lax.fori_loop(0, heads, head, 0)
    copy.wait()
    gw = mm(dy_ref[...], x_ref[...], NN)
    go = mm(ob_ref[...], da_ref[...], NN)
    gb = mm(jnp.ones((8, LENGTH), BF16), dy_ref[...], NT)
    if before:
        gw, go, gb = gw + before[0][: 3 * width], go + before[0][3 * width :], gb + before[1][...]
    gb_ref[...] = gb
    total_ref = outs[2] if mine else sum_ref
    total_ref[: 3 * width] = gw
    total_ref[3 * width :] = go
    if not mine:
        divide(sum_ref, bit, 0, outs[2], outs[3])
        pack_small(outs[4], outs[2], gb, *before[2:])


def norm_stats(v):
    centered = v - jnp.mean(v, axis=-1, keepdims=True)
    inverse = lax.rsqrt(jnp.mean(centered * centered, axis=-1, keepdims=True) + EPSILON)
    return centered * inverse, inverse


def norm_back(grad, hat, inverse, gain):
    scaled = grad * gain
    return inverse * (
        scaled
        - jnp.mean(scaled, axis=-1, keepdims=True)
        - hat * jnp.mean(scaled * hat, axis=-1, keepdims=True)
    )


def row_blocks(rows, step, block=256):
    def body(i, carry):
        step(pl.ds(pl.multiple_of(i * block, block), block))
        return carry

    lax.fori_loop(0, rows // block, body, 0)


def project_norm(sc, tokens_ref, keep_ref, core_ref, far_ref, bias_ref, gain_ref, shift_ref, n_ref, nt_ref, hat_ref, inv_ref, x_ref, sem):
    rows = hat_ref.shape[0]
    copy = pltpu.make_async_copy(tokens_ref.at[pl.ds(pl.multiple_of(lax.axis_index("mp") * rows, rows), rows), :], x_ref, sem)
    copy.start()
    copy.wait()

    def step(at):
        total = x_ref[at, :].astype(F32) + bias_ref[...]
        total = total + (keep_ref[at, :] + core_ref[at, :].astype(F32) + far_ref[at, :].astype(F32))
        hat, inverse = norm_stats(total)
        n = hat * gain_ref[...] + shift_ref[...]
        hat_ref[at, :] = hat
        inv_ref[at, :] = inverse
        n_ref[at, :] = n.astype(BF16)
        nt_ref[:, at] = jnp.transpose(n).astype(BF16)

    row_blocks(rows, step)


def gelu_parts(z):
    e = jnp.exp2(z * z * (-0.5 * math.log2(math.e)))
    t = 1.0 / (1.0 + jnp.abs(z) * (ERF_P / math.sqrt(2.0)))
    poly = jnp.full_like(z, 0.5 * ERF_C[-1])
    for c in ERF_C[-2::-1]:
        poly = poly * t + 0.5 * c
    tail = poly * e
    phi = jnp.where(z >= 0, 1.0 - tail, tail)
    return z * phi, phi + z * e * (1.0 / math.sqrt(2.0 * math.pi))


def ffn_forward(block, sc, n_ref, wi_ref, bi_ref, wo_ref, *refs):
    g_ref, d_ref, f_ref = refs[-3:]

    def step(at):
        z = mm(n_ref[at, :], wi_ref[...], NN) + bi_ref[...]
        g, d = gelu_parts(z)
        g = g.astype(BF16)
        g_ref[at, :] = g
        d_ref[at, :] = d
        part = mm(g, wo_ref[...], NN)
        f_ref[at, :] = part + refs[0][at, :] if len(refs) > 3 else part

    row_blocks(n_ref.shape[0], step, block)


def add_sums(small_ref, at, values):
    @pl.when(at.start == 0)
    def _():
        small_ref[...] = jnp.zeros(small_ref.shape, F32)

    small_ref[...] += row_select([jnp.sum(v, axis=0, keepdims=True) for v in values], small_ref.shape[1])


def second_norm(sc, f_ref, hat_ref, cot_ref, g1_ref, s1_ref, ob_ref, g2_ref, s2_ref, out_ref, dr_ref, df_ref, small_ref):
    rows = f_ref.shape[0]

    def step(at):
        first = hat_ref[at, :] * g1_ref[...] + s1_ref[...]
        hat, inverse = norm_stats(first + f_ref[at, :] + ob_ref[...])
        out_ref[at, :] = (hat * g2_ref[...] + s2_ref[...]).astype(BF16)
        me = lax.axis_index("mp")
        place = lax.broadcasted_iota(jnp.int32, (at.size, 1), 0) + at.start + (me % 2) * rows
        grad = jnp.where(place < sc[me // 2], cot_ref[at, :].astype(F32), 0.0)
        dr = norm_back(grad, hat, inverse, g2_ref[...])
        dr_ref[at, :] = dr
        df_ref[at, :] = dr.astype(BF16)
        add_sums(small_ref, at, (grad * hat, grad, dr))

    row_blocks(rows, step)


def outer_odd(sc, one_ref, three_ref, df_ref, *out_refs):
    count = out_refs[0].shape[0] // 2
    df = df_ref[...]
    for j, g_ref in enumerate((one_ref, three_ref)):
        total = mm(g_ref[...], df, TN).astype(BF16)
        for k, out_ref in enumerate(out_refs):
            out_ref[j * count : (j + 1) * count] = total[k * count : (k + 1) * count]


def outer_even(bit, sc, zero_ref, two_ref, df_ref, arrived_ref, send_ref, keep_ref, sum_ref):
    count = sum_ref.shape[0]
    df = df_ref[...]
    for j, g_ref in enumerate((zero_ref, two_ref)):
        sum_ref[...] = mm(g_ref[...], df, TN) + arrived_ref[j * count : (j + 1) * count].astype(F32)
        divide(sum_ref, bit, j, send_ref, keep_ref)


def ffn_backward(slot, bit, sc, df_ref, wo_ref, d_ref, wi_ref, nt_ref, dn_in_ref, *refs):
    arrived, outs, (dz_ref, sum_ref) = refs[: {0: 2}.get(slot, 1 - slot % 2)], refs[{0: 2}.get(slot, 1 - slot % 2) : -2], refs[-2:]
    gb_ref, dn_ref = outs[:2]
    dz = (mm(df_ref[...], wo_ref[...], NT) * d_ref[...]).astype(BF16)
    dz_ref[...] = dz
    dn_ref[...] = dn_in_ref[...] + mm(dz, wi_ref[...], NT)
    gb_ref[...] = jnp.sum(dz_ref[...].astype(F32), axis=0, keepdims=True)
    total = mm(nt_ref[...], dz_ref[...], NN)
    if slot % 2 == 0:
        total = total + arrived[0][...].astype(F32)
    if slot:
        outs[2][...] = total.astype(outs[2].dtype)
    else:
        sum_ref[...] = total
        divide(sum_ref, bit, 0, outs[2], outs[3])
        divide(arrived[1], bit, 1, outs[2], outs[3])


def first_norm_back(sc, dn_ref, hat_ref, inv_ref, gain_ref, dr_ref, low_ref, small_ref):
    def step(at):
        grad, hat = dn_ref[at, :], hat_ref[at, :]
        dr = norm_back(grad, hat, inv_ref[at, :], gain_ref[...])
        dr_ref[at, :] = dr
        low_ref[at, :] = dr.astype(BF16)
        add_sums(small_ref, at, (dr, grad * hat, grad))

    row_blocks(dn_ref.shape[0], step)


def token_grad(own, sc, dy_ref, w_ref, *refs):
    before, (keep_ref, give_ref) = refs[:-2], refs[-2:]
    near, far, _, _ = place_of(sc, own, True)
    total = mm(dy_ref[:, pl.ds(near, own)], w_ref[...], TN)
    for ref in before:
        total = total + ref[...]
    keep_ref[...] = total
    give_ref[...] = mm(dy_ref[:, pl.ds(far, own)], w_ref[...], TN).astype(BF16)


def pack_small(out_ref, send_ref, qkv, small2, small1, *inner):
    me = lax.axis_index("mp")
    out_ref[...] = jnp.zeros(out_ref.shape, F32)
    out_ref[0:3] = small2[0:3]
    out_ref[3:6] = small1[0:3]
    for r in range(4):
        out_ref[pl.ds(8 + (me ^ r), 1), :] = inner[r][...]
    out_ref[pl.ds(12 + me, 1), pl.ds(0, qkv.shape[1])] = qkv[0:1]
    count = out_ref.shape[0]
    for i, part in enumerate(split3(out_ref[...])):
        at = send_ref.shape[0] - (3 - i) * count
        send_ref[at : at + count] = part.astype(BF16)


def swap(v, axis, bit):
    size = lax.axis_size(axis)
    return lax.ppermute(v, axis, [(i, i ^ bit) for i in range(size)])


def after(v, *others):
    return lax.optimization_barrier((v, *others))[0]


def dp_upper(bit):
    return (lax.axis_index("dp") & bit) > 0


def parts3(v):
    high = lax.reduce_precision(v, 8, 7)
    mid = lax.reduce_precision(v - high, 8, 7)
    return high, mid, v - high - mid


class Chunk:
    def __init__(self, order, cut=None, swapped=False):
        size = lax.axis_size("dp")
        bits = [1 << i for i in range(size.bit_length() - 1)]
        self.order = [b for b in order if b == "x" or b in bits]
        self.order += [b for b in bits if b not in order]
        self.last = [b for b in self.order if b != "x"][-1]
        self.back = [b for b in self.order[::-1] if b not in ("x", self.last)]
        self.swapped = swapped and len(self.back) == 2
        if self.swapped:
            self.back = self.back[::-1]
        self.bit = self.order[0]
        self.received = self.total = self.result = self.rider = None
        self.cut = cut
        self.stage = "start"
        self.finished = False

    def begin(self, run, send, keep, rider=None):
        self.stage = self.order.pop(0)
        self.received = self.exchange(send)
        self.total, self.rider = keep, rider
        self.rows = math.prod(keep.shape[:-1])
        run.clock += 1.6
        self.due = run.transfer(self.stage, self.received.shape[0])
        run.chunks.append(self)

    def exchange(self, send):
        self.rows = send.shape[0]
        if self.rider is not None:
            send = jnp.concatenate([send] + [v.astype(BF16) for v in parts3(self.rider)])
        return swap(send, "mp" if self.stage == "x" else "dp", 2 if self.stage == "x" else self.stage)

    def merged(self):
        arrived = self.received[: self.rows].astype(F32)
        if self.rider is not None:
            parts = self.received[self.rows :].astype(F32).reshape(3, *self.rider.shape)
            self.rider = self.rider + (parts[0] + parts[1] + parts[2])
        return self.total + arrived.reshape(self.total.shape)

    def step(self):
        if self.order:
            total = self.merged()
            self.stage = self.order.pop(0)
            if self.stage == "x":
                send, self.total = total[1].astype(BF16), total[:1]
            elif self.stage == self.last:
                send = total.reshape(-1, total.shape[-1]).astype(BF16)
                self.total = send.astype(F32).reshape(total.shape)
            else:
                upper = dp_upper(self.stage)
                n = total.shape[1] // 2
                low, high = total[:, :n], total[:, n:]
                send = jnp.where(upper, low, high).astype(BF16).reshape(-1, total.shape[-1])
                self.total = jnp.where(upper, high, low)
            self.received = self.exchange(send)
            return send
        if self.back:
            if self.total is not None:
                self.held = self.merged()[0].astype(BF16)
                self.ridden, self.rider, self.total = self.rider, None, None
            else:
                self.held = self.joined()
            self.stage = self.back.pop(0)
            self.received = swap(self.held, "dp", self.stage)
            return self.held
        self.finished = True
        if self.cut is None or self.swapped:
            self.result = self.joined().astype(F32)
            return self.result
        upper = dp_upper(self.stage)
        first, second = jnp.where(upper, self.received, self.held), jnp.where(upper, self.held, self.received)
        rest = self.cut - first.shape[0]
        self.result = jnp.concatenate([first, second[:rest]]).astype(F32), second[rest:].astype(F32)
        return self.result[0]

    def joined(self):
        pair = (self.held, self.received)
        if self.swapped and not self.back:
            pair = tuple(v.reshape(2, 1, -1, v.shape[-1]) for v in pair)
            rows = jnp.where(dp_upper(self.stage), jnp.concatenate(pair[::-1], axis=1), jnp.concatenate(pair, axis=1))
            return rows.reshape(-1, rows.shape[-1])
        return jnp.where(dp_upper(self.stage), jnp.concatenate(pair[::-1]), jnp.concatenate(pair))


class Everywhere:
    def __init__(self, v):
        self.own, self.received = v, None
        self.stages = [1, 2]
        self.finished = False
        self.stage = "start"

    def step(self):
        if self.received is not None:
            self.own = self.own + self.received
        if self.stages:
            bit = self.stages.pop(0)
            self.stage = {1: "core", 2: "x"}[bit]
            self.received = swap(self.own, "mp", bit)
        else:
            self.finished, self.stage = True, "end"
        return self.own


class Exchange:
    def __init__(self):
        self.finished = False
        self.stage = "core"

    def begin(self, run, keep, give):
        self.keep = keep
        self.received = swap(give, "mp", 1)
        run.chunks.append(self)
        self.due = run.transfer("core", give.shape[0] * give.dtype.itemsize // 2)

    def step(self):
        made = (self.keep + self.received.astype(F32)).astype(BF16)
        self.received = swap(made, "mp", 2)
        self.stage = "x"
        self.finished = True
        return made


class Gather:
    def __init__(self, own, bits):
        self.own, self.bits = own, list(bits)
        self.received = None
        self.stage = "start"
        self.finished = False

    def step(self):
        if self.stage == "start":
            self.held = self.own
            for bit in self.bits[::-1]:
                self.held = half_of(self.held, bit)
            self.stage, self.received = "x", swap(self.held, "mp", 2)
            return self.held
        if self.stage == "x":
            self.held = self.received
        else:
            self.held = join_halves(self.held, self.received, self.stage)
        if self.bits:
            self.stage = self.bits.pop(0)
            self.received = swap(self.held, "dp", self.stage)
            return self.held
        self.two, self.stage = self.held, "core"
        self.three = swap(self.two, "mp", 1)
        self.finished = True
        return self.two


def half_of(v, bit):
    n = v.shape[0] // 2
    return lax.dynamic_slice_in_dim(v, jnp.where(dp_upper(bit), n, 0), n, 0)


def join_halves(mine, other, bit):
    return jnp.where(dp_upper(bit), jnp.concatenate([other, mine]), jnp.concatenate([mine, other]))


def on_device(
    tokens,
    qkv_weight,
    qkv_bias,
    output_weight,
    output_bias,
    first_gain,
    first_shift,
    inner_weight,
    inner_bias,
    outer_weight,
    outer_bias,
    second_gain,
    second_shift,
    cotangent,
    seq_lengths,
):
    depth = tokens.shape[1]
    own = cotangent.shape[0]
    width = qkv_weight.shape[2]
    heads = width // HD
    hidden = inner_weight.shape[1]
    me = lax.axis_index("mp")
    table = jnp.asarray(rotary_tables())
    run = Program(seq_lengths)

    bias_one = swap(inner_bias, "mp", 1)
    inner_w, outer_w = [inner_weight, None, None, None], [outer_weight, None, None, None]
    inner_w[1], outer_w[1] = swap(inner_weight, "mp", 1), swap(outer_weight, "mp", 1)
    inner_gather, outer_gather = Gather(inner_weight, (1, 2)), Gather(outer_weight, (2, 1))
    run.add(inner_gather)
    run.add(outer_gather)
    qkv_w = jnp.transpose(qkv_weight, (1, 2, 0)).reshape(3 * width, depth)
    rows = {n: v.reshape(1, -1) for n, v in dict(ob=output_bias, g1=first_gain, s1=first_shift, b2=outer_bias, g2=second_gain, s2=second_shift).items()}

    kv, q, o, ob, logs, keys = ([None] * 2 for _ in range(6))

    def attend(mine):
        kv[mine], q[mine], o[mine], ob[mine], logs[mine], keys[mine], keep, give = run.call(
            functools.partial(attention_forward, heads, own, mine),
            [
                sds((2 * width, LENGTH), BF16),
                sds((width, LENGTH), BF16),
                sds((width, LENGTH), F32),
                sds((width, LENGTH), BF16),
                sds((8, LENGTH), F32),
                sds((heads, LENGTH, 2 * HD), BF16),
                sds((own, depth), F32),
                sds((own, depth), BF16 if mine else F32),
            ],
            [tokens, qkv_w, qkv_bias, output_weight, table],
            in_specs=[ANY, VM, VM, VM, ANY],
            flops=2 * depth * width * 4 * LENGTH + 4 * LENGTH * LENGTH * 256 * heads,
            name="attention_forward",
            us=8.7,
            scratch=[pltpu.VMEM((width, LENGTH), F32)] * 2 + [pltpu.VMEM((LENGTH, depth), BF16), pltpu.VMEM((HD, LENGTH), F32), pltpu.SemaphoreType.DMA, pltpu.SemaphoreType.DMA],
        )
        return keep, give

    run.wait(inner_w[1], outer_w[1], bias_one)
    run.clock += 3.0
    far_sum = Exchange()
    run.hold = True
    keep, give = attend(0)
    run.hold = False
    for gather in (inner_gather, outer_gather):
        gather.received = after(gather.received, *run.tokens)
    bias_pair = swap(jnp.stack([after(inner_bias, kv[0]), bias_one]), "mp", 2)
    bias_slots = [inner_bias.reshape(1, -1), bias_one.reshape(1, -1), bias_pair[:1], bias_pair[1:]]
    far_sum.begin(run, keep, after(give, inner_gather.received, outer_gather.received))
    run.finish(far_sum)
    far = far_sum.received
    run.clock = max(run.clock, inner_gather.due, outer_gather.due)
    run.service()
    run.hold = True
    keep, give = attend(1)
    run.hold = False
    for gather in (inner_gather, outer_gather):
        gather.received = after(gather.received, *run.tokens)
    core = swap(after(give, inner_gather.received, outer_gather.received), "mp", 1)
    run.clock = max(run.clock, inner_gather.due, outer_gather.due)
    run.service()
    run.clock = max(run.clock, far_sum.due)
    run.wait(far, core)
    run.service()
    n_low, n_t, hat, inverse = run.call(
        project_norm,
        [sds((own, depth), BF16), sds((depth, own), BF16), sds((own, depth), F32), sds((own, 1), F32)],
        [tokens, keep, core, far, rows["ob"], rows["g1"], rows["s1"]],
        in_specs=[ANY] + [VM] * 6,
        scratch=[pltpu.VMEM((own, depth), BF16), pltpu.SemaphoreType.DMA],
        flops=40 * own * depth,
        name="project_norm",
        us=2.0,
    )

    block = 512
    g, d = [None] * 4, [None] * 4

    def feed(r, *f):
        g[r], d[r], f = run.call(
            functools.partial(ffn_forward, block),
            [sds((own, hidden), BF16), sds((own, hidden), F32), sds((own, depth), F32)],
            [n_low, inner_w[r], bias_slots[r], outer_w[r], *f],
            flops=4 * own * depth * hidden,
            name="ffn_forward",
            us=3.0,
        )
        return f

    run.hold = True
    f = feed(0)
    run.wait(bias_pair)
    f = feed(1, f)
    run.hold = False
    for gather in (inner_gather, outer_gather):
        run.finish(gather)
    inner_w[2:], outer_w[2:] = ([v.two, v.three] for v in (inner_gather, outer_gather))
    f = feed(2, f)
    f = feed(3, f)
    layer_out, dr2, df, small2 = run.call(
        second_norm,
        [sds((own, depth), BF16), sds((own, depth), F32), sds((own, depth), BF16), sds((8, depth), F32)],
        [f, hat, cotangent, rows["g1"], rows["s1"], rows["b2"], rows["g2"], rows["s2"]],
        flops=40 * own * depth,
        name="second_norm",
        us=2.7,
    )
    odd = run.call(
        outer_odd,
        [sds((2 * hidden, depth), BF16)],
        [g[1], g[3], df],
        flops=4 * own * depth * hidden,
        name="outer_odd",
        us=1.9,
    )
    arrived = swap(odd[0], "mp", 1)
    inner_g, inner_bg = [None] * 4, [None] * 4
    dn = dr2

    def feed_back(r, dn, *arrived):
        divided = [sds((depth, hidden), BF16), sds((2, depth // 2, hidden), F32)]
        inner_bg[r], dn, *inner_g[r] = run.call(
            functools.partial(ffn_backward, r, inner_sum.bit),
            [sds((1, hidden), F32), sds((own, depth), F32)] + (divided if r == 0 else [sds((depth, hidden), F32 if r == 2 else BF16)]),
            [df, outer_w[r], d[r], inner_w[r], n_t, dn, *arrived],
            flops=6 * own * depth * hidden,
            name="ffn_backward",
            us=2.6 if r else 3.0,
            scratch=[pltpu.VMEM((own, hidden), BF16), pltpu.VMEM((depth, hidden), F32)],
        )
        return dn

    outer_sum, inner_sum, attention_sum = Chunk(OUTER_ORDER, None, SWAPPED[0]), Chunk(INNER_ORDER, None, SWAPPED[1]), Chunk(QKV_ORDER, 3 * width, SWAPPED[2])
    dn = feed_back(3, dn)
    send, kept = run.call(
        functools.partial(outer_even, outer_sum.bit),
        [sds((hidden, depth), BF16), sds((2, hidden // 2, depth), F32)],
        [g[0], g[2], df, arrived],
        flops=4 * own * depth * hidden,
        name="outer_even",
        us=2.4,
        scratch=[pltpu.VMEM((hidden, depth), F32)],
    )
    outer_sum.begin(run, send, kept)
    three = swap(inner_g[3][0], "mp", 1)
    dn = feed_back(1, dn)
    one = swap(inner_g[1][0], "mp", 1)
    dn = feed_back(2, dn, three)
    dn = feed_back(0, dn, one, inner_g[2][0])
    dr1, low, small1 = run.call(
        first_norm_back,
        [sds((own, depth), F32), sds((own, depth), BF16), sds((8, depth), F32)],
        [dn, hat, inverse, rows["g1"]],
        flops=40 * own * depth,
        name="first_norm_back",
        us=1.9,
    )

    low_far = swap(low, "mp", 2)
    low_due = run.transfer("x", own)
    run.clock += 1.5
    inner_sum.begin(run, *inner_g[0])
    low_core = swap(low, "mp", 1)

    def attend_back(mine, near, far, *before):
        divided = [sds((2 * width + 48, depth), BF16), sds((1, 2 * width, depth), F32), sds((16, depth), F32)]
        return run.call(
            functools.partial(attention_backward, heads, own, mine, attention_sum.bit),
            [sds((3 * width, LENGTH), BF16), sds((8, 3 * width), F32)] + ([sds((4 * width, depth), F32)] if mine else divided),
            [tokens, kv[mine], q[mine], o[mine], ob[mine], logs[mine], keys[mine], near, far, output_weight, table, *before],
            in_specs=[ANY] + [VM] * (10 + len(before)),
            flops=2 * depth * width * 5 * LENGTH + 10 * LENGTH * LENGTH * 256 * heads,
            name="attention_backward",
            us=11.0 if mine else 12.0,
            scratch=[pltpu.VMEM((LENGTH, depth), BF16), pltpu.VMEM((width, LENGTH), BF16), pltpu.VMEM((LENGTH, depth), BF16), pltpu.VMEM((4 * width, depth), F32), pltpu.SemaphoreType.DMA],
        )

    def token_part(dy, *before):
        return run.call(
            functools.partial(token_grad, own),
            [sds((own, depth), F32), sds((own, depth), BF16)],
            [dy, qkv_w, *before],
            flops=6 * own * depth * depth,
            name="token_grad",
            us=2.4,
        )

    run.hold = True
    dy, bias_sum, weight_sum = attend_back(1, low, low_core)
    own_keep, own_give = token_part(dy, dr1)
    own_core = swap(own_give, "mp", 1)
    run.hold = False
    run.take(outer_sum)
    run.clock = max(run.clock, low_due)
    low_far = after(low_far, *run.tokens)
    low_far_core = swap(low_far, "mp", 1)
    run.tokens = [low_far]
    run.wait(own_core)
    run.service()
    run.clock += 1.5
    dy, _, send, kept, packed = attend_back(0, low_far, low_far_core, weight_sum, bias_sum, small2, small1, *inner_bg)
    attention_sum.begin(run, send, kept, packed)
    far_keep, far_give = token_part(dy)
    token_far = Exchange()
    token_far.begin(run, far_keep, far_give)
    while not hasattr(attention_sum, "ridden"):
        run.take(min([c for c in run.chunks if not c.finished], key=lambda c: c.due))
    small_sum = Everywhere(attention_sum.ridden)
    run.add(small_sum)
    run.service(0)
    tokens_grad = own_keep + (own_core.astype(F32) + token_far.received.astype(F32))
    small = small_sum.own
    outer_weight_grad, inner_weight_grad = outer_sum.result, inner_sum.result
    if attention_sum.swapped:
        attention_sum.result = attention_sum.result[: 3 * width], attention_sum.result[3 * width :]
    qkv_weight_grad, output_weight_grad = attention_sum.result
    qkv_weight_grad = jnp.transpose(qkv_weight_grad.reshape(3, width, depth), (2, 0, 1))
    second_gain_grad, second_shift_grad, outer_bias_grad, output_bias_grad, first_gain_grad, first_shift_grad = (small[i] for i in range(6))
    inner_bias_grad = lax.dynamic_index_in_dim(small, 8 + me, 0, keepdims=False)
    qkv_bias_grad = lax.dynamic_index_in_dim(small, 12 + me, 0, keepdims=False)[: 3 * width].reshape(3, width)
    return (
        layer_out,
        tokens_grad,
        qkv_weight_grad,
        qkv_bias_grad,
        output_weight_grad,
        output_bias_grad,
        first_gain_grad,
        first_shift_grad,
        inner_weight_grad,
        inner_bias_grad,
        outer_weight_grad,
        outer_bias_grad,
        second_gain_grad,
        second_shift_grad,
    )


def solution(mesh):
    return jax.shard_map(
        on_device,
        mesh=mesh,
        in_specs=(
            P("dp", None),
            P(None, None, "mp"),
            P(None, "mp"),
            P("mp", None),
            P(),
            P(),
            P(),
            P(None, "mp"),
            P("mp"),
            P("mp", None),
            P(),
            P(),
            P(),
            P(("dp", "mp"), None),
            P("dp"),
        ),
        out_specs=(
            P(("dp", "mp"), None),
            P(("dp", "mp"), None),
            P(None, None, "mp"),
            P(None, "mp"),
            P("mp", None),
            P(),
            P(),
            P(),
            P(None, "mp"),
            P("mp"),
            P("mp", None),
            P(),
            P(),
            P(),
        ),
        check_vma=False,
    )
```
